128 devices in a mesh: det: 8 (over x, core), pix: 16 (over z, y).
Axes of the slice: x: 4, y: 4, z: 4, core: 2. Of those that a mesh axis runs over, the one named last changes fastest.
Arguments:
- timestream: float32 [128, 256, 128], P(('det', 'pix')), may hold values from -48 to 48
- weights: bfloat16 [128, 256, 128, 256], P(('det', 'pix')), may hold values from 0.0004 to 1
- block_owner: int32 [128, 256, 1], P(('det', 'pix')), may hold values from 0 to 15; in each aligned block of 256 rows (0 to 255, 256 to 511, ..., all dimensions but the last counted through in order) at most 64 rows name the same one
- block_local: int32 [128, 256], P(('det', 'pix')), may hold values from 0 to 63
- baseline_of: int32 [128, 256], P(('det', 'pix')), may hold values from 0 to 127, never falling along the last dimension, each value on 1 to 3 neighbouring positions
Outputs:
- offset_levels: float32 [128, 128], P(('det', 'pix'))
- leftover_error: float32 [128, 128], P(('det', 'pix'))
The draws below stay inside these ranges and needn't reach their ends.
Inputs may be any that keep to these rules, and one draw needn't show every extreme that they name: `block_owner`: among the 256 blocks of one timestream row at most 64 name the same owner, and in every row some owner is named by exactly 64. `baseline_of`: along each row the baseline index never falls; each of the 128 baselines covers 1 to 3 blocks, and some covers exactly 3.
All inputs are finite; a program needn't handle non-finite values.
Results may differ from the reference program's by a relative error of at most 0.013.
Values may be sent and summed in bfloat16 or wider, within the bound.
A program may use at most 64 MiB of HBM per device.

```python
import math
import jax
import jax.numpy as jnp
import numpy as np
from jax import lax

SAMP = 128
PIX = 256
NBLK_DEV = 256
PB_DEV = 64
ITERS = 2
CAP = 64
NBASE_DEV = 128
N_TOD = 128
NPB = 1024
N_PIX = 16


def pointing_common(key):
    keys = jax.random.split(jax.random.fold_in(key, 7), 3)
    shape = (N_TOD, NBLK_DEV, SAMP)
    candidates = jax.random.randint(keys[0], (3,) + shape, 0, PIX - 1)
    pointed = jnp.min(candidates, axis=0).astype(jnp.int32)
    fraction = jax.random.uniform(keys[1], shape, jnp.float32, 0.05, 1.0)
    pattern = jax.random.uniform(keys[2], (PIX,), jnp.float32, -1.0, 1.0)
    return (pointed, fraction, pattern)


def draw_weights(key, part):
    pointed, fraction, pattern = pointing_common(key)
    floor_key = jax.random.fold_in(key, 11)
    shape = (N_TOD, NBLK_DEV, SAMP, PIX)
    floor_vals = jnp.exp(jax.random.uniform(floor_key, shape, jnp.float32, jnp.log(0.0005), jnp.log(0.005)))
    column = jnp.arange(PIX, dtype=jnp.int32)
    first_col = pointed[..., None]
    values = jnp.where(column == first_col, 1.0, jnp.where(column == first_col + 1, fraction[..., None], floor_vals))
    return values.astype(jnp.float32).astype(jnp.bfloat16)


def draw_timestream(key, part):
    pointed, fraction, pattern = pointing_common(key)
    keys = jax.random.split(jax.random.fold_in(key, 13), 2)
    shape = (N_TOD, NBLK_DEV, SAMP)
    sky_values = pattern
    noise = 4.0 * jax.random.normal(keys[0], shape, jnp.float32)
    offsets = 3.0 * jax.random.normal(keys[1], (N_TOD, NBLK_DEV, 1), jnp.float32)
    signal = 30.0 * (jnp.take(sky_values, pointed) + fraction * jnp.take(sky_values, pointed + 1)) / (1.0 + fraction)
    return jnp.clip(signal + offsets + noise, -48.0, 48.0).astype(jnp.float32)


def touch_ends(entries, stream_key, low, high):
    longest = entries.shape.index(max(entries.shape))
    spots = []
    for shift in (0, 1):
        where = [jax.random.randint(jax.random.fold_in(stream_key, axis), (), 0, length) for axis, length in enumerate(entries.shape)]
        where[longest] = (where[longest] + shift) % entries.shape[longest]
        spots.append(tuple(where))
    return entries.at[spots[0]].set(low).at[spots[1]].set(high)


def length_profile(count, total, most, lean):
    weights = [(1 << 20) // math.isqrt(grade ** lean) + 1 for grade in range(2, count + 1)]
    spare, holding = total - most - (count - 1), [1] * (count - 1)
    while spare > 0:
        movable = [i for i in range(count - 1) if holding[i] < most]
        mass, left = sum([weights[i] for i in movable]), spare
        for i in movable:
            more = min(most - holding[i], max(1, left * weights[i] // mass), spare)
            holding[i] = holding[i] + more
            spare = spare - more
    return np.array([most] + holding)


def ragged(stream_key, number_of, total, bound, lean):
    if number_of == 2:
        one = jax.random.randint(stream_key, (), max(1, total - bound), min(bound, total - 1) + 1)
        return jnp.stack([one, total - one])
    tallies = jnp.asarray(length_profile(number_of, total, bound, lean), jnp.int32)
    pairs = (number_of - 1) // 2
    donor, sink = tallies[1:1 + 2 * pairs:2], tallies[2:2 + 2 * pairs:2]
    room = jnp.minimum(donor - 1, bound - sink)
    shifted = jax.random.randint(jax.random.fold_in(stream_key, 1), (pairs,), 0, 1 << 20) % (room + 1)
    tallies = tallies.at[1:1 + 2 * pairs:2].set(donor - shifted).at[2:2 + 2 * pairs:2].set(sink + shifted)
    return tallies[jax.random.permutation(jax.random.fold_in(stream_key, 2), number_of)]


def assign_block(stream_key, own, number, rows, count, top, bound, skew):
    sequence = jax.random.permutation(stream_key, count)
    crowded, ordinary = shares(count, rows * top, bound, skew, True), shares(count, rows * top, bound, skew, False)
    places = jnp.arange(count)

    def named(lengths, offset_by):
        used = int((lengths > 0).sum())
        fixed = max(1, used // 4)
        shifted = fixed + (places - fixed + offset_by * (used - fixed)) % max(1, count - fixed)
        return jnp.zeros((count,), jnp.int32).at[sequence[jnp.where(places < fixed, places, shifted)]].set(jnp.asarray(lengths, jnp.int32))

    lengths = jnp.where(number % 4 == 0, named(crowded, number // 4), named(ordinary, number - number // 4 - 1))
    mixed = jax.random.permutation(jax.random.fold_in(own, 3), count)
    donor, receiver = mixed[0:count // 2 * 2:2], mixed[1:count // 2 * 2:2]
    room = jnp.minimum(lengths[donor] - 1, bound - lengths[receiver]) // 2
    room = jnp.where((donor == sequence[0]) | (receiver == sequence[0]) | (lengths[receiver] == 0), 0, jnp.maximum(room, 0))
    shifted = jax.random.randint(jax.random.fold_in(own, 4), (count // 2,), 0, 1 << 20) % (room + 1)
    lengths = lengths.at[donor].add(-shifted).at[receiver].add(shifted)
    items = jnp.searchsorted(jnp.cumsum(lengths), jnp.arange(rows * top), side="right").astype(jnp.int32)
    grid = items.reshape(top, rows).T
    grid = grid[jax.random.permutation(jax.random.fold_in(own, 1), rows)]
    offset_by = jax.random.randint(jax.random.fold_in(own, 2), (rows, 1), 0, top)
    return jnp.take_along_axis(grid, (jnp.arange(top)[None, :] + offset_by) % top, axis=1)


def shares(count, total, reach, lean, full):
    loads = [(1 << 20) // math.isqrt(rank ** lean) + 1 for rank in range(1, count + 1)]
    largest = reach if full else min(reach, max(-(-total // count), total * loads[0] // sum(loads)))
    least = 1 if total - largest >= count - 1 else 0
    counts, rest = [largest] + [least] * (count - 1), total - largest - least * (count - 1)
    while rest > 0:
        free = [i for i in range(1, count) if counts[i] < largest] or [i for i in range(1, count) if counts[i] < reach]
        pool, left = sum([loads[i] for i in free]), rest
        for i in free:
            extra = min(reach - counts[i], max(1, left * loads[i] // pool), rest)
            counts[i] = counts[i] + extra
            rest = rest - extra
    return np.array(counts)


def setup_inputs(seed: int = 0) -> dict:
    splits = jax.random.split(jax.random.key(seed), 6)
    timestream = draw_timestream(jax.random.fold_in(splits[5], 71), 0)
    weights = draw_weights(jax.random.fold_in(splits[5], 71), 0)
    block_owner_keys = jax.random.split(jax.random.fold_in(splits[2], 1), N_TOD * NBLK_DEV // NBLK_DEV)
    block_owner_turns = jax.random.permutation(jax.random.fold_in(splits[2], 3), N_TOD * NBLK_DEV // NBLK_DEV)
    block_owner = jax.vmap(lambda own, number: assign_block(jax.random.fold_in(splits[2], 2), own, number, NBLK_DEV, N_PIX, 1, CAP, 2))(block_owner_keys, block_owner_turns).reshape((N_TOD, NBLK_DEV, 1))
    block_local = touch_ends(jax.random.randint(splits[3], (N_TOD, NBLK_DEV), 0, PB_DEV), jax.random.fold_in(splits[3], 1), 0, PB_DEV - 1).astype(jnp.int32)
    baseline_of = jax.vmap(lambda own: jnp.searchsorted(jnp.cumsum(ragged(own, NBASE_DEV, NBLK_DEV, 3, 0)), jnp.arange(NBLK_DEV), side="right"))(jax.random.split(splits[4], N_TOD)).reshape((N_TOD, NBLK_DEV)).astype(jnp.int32)
    return {"timestream": timestream, "weights": weights, "block_owner": block_owner, "block_local": block_local, "baseline_of": baseline_of}


def reference(timestream, weights, block_owner, block_local, baseline_of):
    block_pix = (block_owner[:, :, 0] * PB_DEV + block_local).astype(jnp.int32)
    flat_pix = block_pix.reshape(-1)

    def bin_terms(series_b):
        def one_row(pair):
            weight_row, series_row = pair
            return jnp.einsum('kbs,bsp->kbp', series_row.astype(jnp.float32), weight_row.astype(jnp.float32))
        terms = lax.map(one_row, (weights, jnp.swapaxes(series_b, 0, 1)))
        count_k = series_b.shape[0]
        terms = jnp.swapaxes(terms, 0, 1).reshape(count_k, -1, PIX)
        return jax.vmap(lambda values: jax.ops.segment_sum(values, flat_pix, num_segments=NPB))(terms)

    def project_map(map_b):
        def one_row(pair):
            weight_row, pix_row = pair
            return jnp.einsum('bsp,bp->bs', weight_row.astype(jnp.float32), map_b[pix_row].astype(jnp.float32))
        return lax.map(one_row, (weights, block_pix))

    def collapse(series):
        per_block = jnp.sum(series, axis=-1)
        return jax.vmap(lambda values, segs: jax.ops.segment_sum(values, segs, num_segments=NBASE_DEV))(per_block, baseline_of)

    def expand(amps):
        per_block = jnp.take_along_axis(amps, baseline_of, axis=1)
        return jnp.broadcast_to(per_block[:, :, None], (per_block.shape[0], per_block.shape[1], SAMP))

    row_sums = lax.map(lambda weight_row: jnp.sum(weight_row.astype(jnp.float32), axis=-1), weights).astype(jnp.bfloat16)
    first = bin_terms(jnp.stack([row_sums, timestream.astype(jnp.bfloat16)]))
    hit_sums = first[0]
    sky_map = first[1] / (hit_sums + 1.0)
    projected = project_map(sky_map.astype(jnp.bfloat16))
    equation_target = collapse(timestream - projected) / SAMP

    def normal_equations_action(amps):
        series = expand(amps)
        binned = bin_terms(series.astype(jnp.bfloat16)[None])[0]
        sky = binned / (hit_sums + 1.0)
        proj = project_map(sky.astype(jnp.bfloat16))
        return collapse(series - proj) / SAMP + amps

    offset_levels = jnp.zeros_like(equation_target)
    leftover_error = equation_target
    descent_heading = equation_target
    current_norm = jnp.sum(leftover_error * leftover_error)
    for iteration in range(ITERS):
        image = normal_equations_action(descent_heading)
        descent_factor = current_norm / jnp.sum(descent_heading * image)
        offset_levels = offset_levels + descent_factor * descent_heading
        leftover_error = leftover_error - descent_factor * image
        norm_next = jnp.sum(leftover_error * leftover_error)
        descent_heading = leftover_error + (norm_next / current_norm) * descent_heading
        current_norm = norm_next
    return offset_levels, leftover_error
```

```python
import jax
import jax.numpy as jnp
from jax import lax
from jax.sharding import PartitionSpec as P

PB_DEV = 64
NBASE_DEV = 128
HIGHEST = lax.Precision.HIGHEST
EXTRA = 8


def body(timestream, weights, block_owner, block_local, baseline_of):
    series_data = timestream[0]
    weight_rows = weights[0]
    owners = block_owner[0, :, 0]
    local_idx = block_local[0]
    segments_row = baseline_of[0]
    blocks, samples, pixels = weight_rows.shape
    pix_count = lax.axis_size("pix")
    capacity = blocks // 4
    slot_count = pix_count * capacity

    base_hot = (segments_row[:, None] == jnp.arange(NBASE_DEV)[None, :]).astype(jnp.float32)
    per_base = jnp.sum(base_hot, axis=0)
    owner_hot = (owners[:, None] == jnp.arange(pix_count)[None, :]).astype(jnp.int32)
    before = jnp.cumsum(owner_hot, axis=0) - owner_hot
    slot_position = jnp.sum(before * owner_hot, axis=1)
    slot_ids = owners * capacity + slot_position
    slot_match = slot_ids[None, :] == jnp.arange(slot_count)[:, None]
    slot_hot = slot_match.astype(jnp.float32)
    send_idx = jnp.sum(jnp.where(slot_match, local_idx[None, :] + 1, 0), axis=1) - 1
    incoming_idx = lax.all_to_all(send_idx, "pix", split_axis=0, concat_axis=0, tiled=True)
    received_onehot = (incoming_idx[None, :] == jnp.arange(PB_DEV)[:, None]).astype(jnp.float32)
    incoming_t = (incoming_idx[:, None] == jnp.arange(PB_DEV)[None, :]).astype(jnp.float32)
    slot_hot_t = (slot_ids[:, None] == jnp.arange(slot_count)[None, :]).astype(jnp.float32)

    unit_row_vector = jnp.ones((pixels,), jnp.bfloat16)
    row_sums = jnp.einsum(
        "bsp,p->bs", weight_rows, unit_row_vector, preferred_element_type=jnp.float32
    ).astype(jnp.bfloat16)
    stacked = jnp.stack(
        [row_sums, series_data.astype(jnp.bfloat16), jnp.ones_like(row_sums)]
    )
    first_terms = jnp.einsum(
        "kbs,bsp->kbp", stacked, weight_rows, preferred_element_type=jnp.float32
    )
    col_sums = first_terms[2]
    series_block_sums = jnp.sum(series_data, axis=1)

    def to_slots(terms):
        outgoing = jnp.einsum("cb,kbp->kcp", slot_hot, terms, precision=HIGHEST)
        k = terms.shape[0]
        return outgoing.reshape(k, pix_count, capacity, pixels).transpose(1, 0, 2, 3)

    def owner_sum(arrived):
        k = arrived.shape[1]
        flat = arrived.transpose(1, 0, 2, 3).reshape(k, slot_count, pixels)
        return jnp.einsum("qc,kcp->kqp", received_onehot, flat, precision=HIGHEST)

    def from_owner(map_own):
        return jnp.dot(incoming_t, map_own, precision=HIGHEST).reshape(pix_count, capacity, pixels)

    def to_blocks(arrived):
        return jnp.dot(slot_hot_t, arrived.reshape(slot_count, pixels), precision=HIGHEST)

    out1 = to_slots(first_terms[:2])
    arr1 = lax.all_to_all(out1, "pix", split_axis=0, concat_axis=0, tiled=True)
    own1 = lax.psum(owner_sum(arr1), "det")
    hit_plus = own1[0] + 1.0
    sky0 = (own1[1] / hit_plus).astype(jnp.bfloat16)
    back1 = lax.all_to_all(from_owner(sky0.astype(jnp.float32)).astype(jnp.bfloat16),
                           "pix", split_axis=0, concat_axis=0, tiled=True)
    sky_blocks0 = to_blocks(back1.astype(jnp.float32))
    projected0 = jnp.sum(col_sums * sky_blocks0, axis=1)
    equation_target = jnp.dot(series_block_sums - projected0, base_hot, precision=HIGHEST) / samples

    def extra_rows(values):
        row = jnp.zeros((EXTRA, pixels), jnp.float32)
        return row.at[0, : values.shape[0]].set(values)

    def apply_round(amps, scalars):
        per_block = jnp.dot(base_hot, amps, precision=HIGHEST)
        terms = per_block[:, None] * col_sums
        slots = to_slots(terms[None])[:, 0]
        payload = jnp.concatenate(
            [slots, jnp.broadcast_to(extra_rows(scalars)[None], (pix_count, EXTRA, pixels))], axis=1
        )
        arrived = lax.all_to_all(payload, "pix", split_axis=0, concat_axis=0, tiled=True)
        partial = owner_sum(arrived[:, None, :capacity])[0]
        scal = jnp.sum(arrived[:, capacity:], axis=0)
        summed = lax.psum(jnp.concatenate([partial, scal], axis=0), "det")
        binned = summed[:PB_DEV]
        sky = binned / hit_plus
        return binned, sky, summed[PB_DEV, : scalars.shape[0]]

    def project_back(sky, sky_scalars):
        payload = jnp.concatenate(
            [from_owner(sky),
             jnp.broadcast_to(extra_rows(sky_scalars)[None], (pix_count, EXTRA, pixels))], axis=1
        )
        arrived = lax.all_to_all(payload, "pix", split_axis=0, concat_axis=0, tiled=True)
        sky_blocks = to_blocks(arrived[:, :capacity])
        scal = jnp.sum(arrived[:, capacity:], axis=0)[0, : sky_scalars.shape[0]]
        return jnp.sum(col_sums * sky_blocks, axis=1), scal

    def normal_action(amps, projected_blocks):
        collapsed = jnp.dot(projected_blocks, base_hot, precision=HIGHEST)
        return amps * (1.0 + per_base) - collapsed / samples

    r0 = equation_target
    binned_r0, sky_r0, _ = apply_round(r0, jnp.zeros((1,), jnp.float32))
    proj_r0, _ = project_back(sky_r0, jnp.zeros((1,), jnp.float32))
    v1 = normal_action(r0, proj_r0)
    weight_n = 1.0 + per_base
    local = jnp.stack([
        jnp.sum(r0 * r0),
        jnp.sum(r0 * v1),
        jnp.sum(v1 * v1),
        jnp.sum(r0 * v1 * weight_n),
        jnp.sum(v1 * v1 * weight_n),
    ])
    binned_v1, sky_v1, totals = apply_round(v1, local)
    sky_products = jnp.stack([jnp.sum(binned_r0 * sky_v1), jnp.sum(binned_v1 * sky_v1)])
    proj_v1, sky_totals = project_back(sky_v1, sky_products)
    v2 = normal_action(v1, proj_v1)

    rr0, r0v1, v1v1 = totals[0], totals[1], totals[2]
    r0v2 = totals[3] - sky_totals[0] / samples
    v1v2 = totals[4] - sky_totals[1] / samples
    alpha0 = rr0 / r0v1
    rr1 = rr0 - 2.0 * alpha0 * r0v1 + alpha0 * alpha0 * v1v1
    beta0 = rr1 / rr0
    grow = 1.0 + beta0
    d1_ad1 = grow * grow * r0v1 - grow * alpha0 * r0v2 - alpha0 * grow * v1v1 + alpha0 * alpha0 * v1v2
    alpha1 = rr1 / d1_ad1
    d1 = grow * r0 - alpha0 * v1
    ad1 = grow * v1 - alpha0 * v2
    offset_levels = alpha0 * r0 + alpha1 * d1
    leftover_error = r0 - alpha0 * v1 - alpha1 * ad1
    return (offset_levels[None], leftover_error[None])


def solution(mesh):
    placed = (
        P(("det", "pix"), None, None),
        P(("det", "pix"), None, None, None),
        P(("det", "pix"), None, None),
        P(("det", "pix"), None),
        P(("det", "pix"), None),
    )
    return jax.shard_map(
        body,
        mesh=mesh,
        in_specs=placed,
        out_specs=(P(("det", "pix"), None), P(("det", "pix"), None)),
        check_vma=False,
    )
```

```python
import functools

import jax
import jax.numpy as jnp
from jax import lax
from jax.experimental import pallas as pl
from jax.experimental.pallas import tpu as pltpu
from jax.sharding import PartitionSpec as P

MESH = pl.DeviceIdType.MESH

PB_DEV = 64
NBASE_DEV = 128
HIGHEST = lax.Precision.HIGHEST
EXTRA = 8


def _greet(peers, device_of):
    barrier = pltpu.get_barrier_semaphore()
    for peer in peers:
        pl.semaphore_signal(barrier, inc=1, device_id=device_of(peer), device_id_type=MESH)
    pl.semaphore_wait(barrier, len(peers))


def _det_sum_kernel(n, x_ref, o_ref, recv, send_sem, recv_sem, local_sem):
    me = lax.axis_index("det")
    pix = lax.axis_index("pix")
    device_of = lambda d: (d, pix)
    _greet([lax.rem(me + k, n) for k in range(1, n)], device_of)
    sends = []
    for k in range(1, n):
        peer = lax.rem(me + k, n)
        copy = pltpu.make_async_remote_copy(
            src_ref=x_ref, dst_ref=recv.at[me], send_sem=send_sem.at[k],
            recv_sem=recv_sem.at[me], device_id=device_of(peer), device_id_type=MESH)
        copy.start()
        sends.append(copy)
    local = pltpu.make_async_copy(x_ref, recv.at[me], local_sem)
    local.start()
    for copy in sends:
        copy.wait_send()
    for k in range(1, n):
        src = lax.rem(me + k, n)
        pltpu.make_async_remote_copy(
            src_ref=x_ref, dst_ref=recv.at[src], send_sem=send_sem.at[k],
            recv_sem=recv_sem.at[src], device_id=device_of(src), device_id_type=MESH).wait_recv()
    local.wait()
    acc = recv[0]
    for s in range(1, n):
        acc = acc + recv[s]
    o_ref[...] = acc


def det_sum(x, cid):
    n = lax.axis_size("det")
    return pl.pallas_call(
        functools.partial(_det_sum_kernel, n),
        out_shape=jax.ShapeDtypeStruct(x.shape, x.dtype),
        in_specs=[pl.BlockSpec(memory_space=pltpu.VMEM)],
        out_specs=pl.BlockSpec(memory_space=pltpu.VMEM),
        scratch_shapes=[
            pltpu.VMEM((n,) + x.shape, x.dtype),
            pltpu.SemaphoreType.DMA((n,)),
            pltpu.SemaphoreType.DMA((n,)),
            pltpu.SemaphoreType.DMA(()),
        ],
        compiler_params=pltpu.CompilerParams(collective_id=cid, has_side_effects=True),
    )(x)


def _pix_exchange_kernel(n, x_ref, o_ref, send_sem, recv_sem, local_sem):
    me = lax.axis_index("pix")
    det = lax.axis_index("det")
    device_of = lambda j: (det, j)
    _greet([lax.rem(me + k, n) for k in range(1, n)], device_of)
    sends = []
    for k in range(1, n):
        peer = lax.rem(me + k, n)
        copy = pltpu.make_async_remote_copy(
            src_ref=x_ref.at[peer], dst_ref=o_ref.at[me], send_sem=send_sem.at[k],
            recv_sem=recv_sem.at[me], device_id=device_of(peer), device_id_type=MESH)
        copy.start()
        sends.append(copy)
    local = pltpu.make_async_copy(x_ref.at[me], o_ref.at[me], local_sem)
    local.start()
    for copy in sends:
        copy.wait_send()
    for k in range(1, n):
        src = lax.rem(me + k, n)
        pltpu.make_async_remote_copy(
            src_ref=x_ref.at[src], dst_ref=o_ref.at[src], send_sem=send_sem.at[k],
            recv_sem=recv_sem.at[src], device_id=device_of(src), device_id_type=MESH).wait_recv()
    local.wait()


def pix_exchange(x, cid):
    n = lax.axis_size("pix")
    return pl.pallas_call(
        functools.partial(_pix_exchange_kernel, n),
        out_shape=jax.ShapeDtypeStruct(x.shape, x.dtype),
        in_specs=[pl.BlockSpec(memory_space=pltpu.VMEM)],
        out_specs=pl.BlockSpec(memory_space=pltpu.VMEM),
        scratch_shapes=[
            pltpu.SemaphoreType.DMA((n,)),
            pltpu.SemaphoreType.DMA((n,)),
            pltpu.SemaphoreType.DMA(()),
        ],
        compiler_params=pltpu.CompilerParams(collective_id=cid, has_side_effects=True),
    )(x)


def body(timestream, weights, block_owner, block_local, baseline_of):
    series_data = timestream[0]
    weight_rows = weights[0]
    owners = block_owner[0, :, 0]
    local_idx = block_local[0]
    segments_row = baseline_of[0]
    blocks, samples, pixels = weight_rows.shape
    pix_count = lax.axis_size("pix")
    capacity = blocks // 4
    slot_count = pix_count * capacity

    base_hot = (segments_row[:, None] == jnp.arange(NBASE_DEV)[None, :]).astype(jnp.float32)
    per_base = jnp.sum(base_hot, axis=0)
    owner_hot = (owners[:, None] == jnp.arange(pix_count)[None, :]).astype(jnp.int32)
    before = jnp.cumsum(owner_hot, axis=0) - owner_hot
    slot_position = jnp.sum(before * owner_hot, axis=1)
    slot_ids = owners * capacity + slot_position
    slot_match = slot_ids[None, :] == jnp.arange(slot_count)[:, None]
    slot_hot = slot_match.astype(jnp.float32)
    send_idx = jnp.sum(jnp.where(slot_match, local_idx[None, :] + 1, 0), axis=1) - 1
    incoming_idx = lax.all_to_all(send_idx, "pix", split_axis=0, concat_axis=0, tiled=True)
    received_onehot = (incoming_idx[None, :] == jnp.arange(PB_DEV)[:, None]).astype(jnp.float32)
    incoming_t = (incoming_idx[:, None] == jnp.arange(PB_DEV)[None, :]).astype(jnp.float32)
    slot_hot_t = (slot_ids[:, None] == jnp.arange(slot_count)[None, :]).astype(jnp.float32)

    unit_row_vector = jnp.ones((pixels,), jnp.bfloat16)
    row_sums = jnp.einsum(
        "bsp,p->bs", weight_rows, unit_row_vector, preferred_element_type=jnp.float32
    ).astype(jnp.bfloat16)
    stacked = jnp.stack(
        [row_sums, series_data.astype(jnp.bfloat16), jnp.ones_like(row_sums)]
    )
    first_terms = jnp.einsum(
        "kbs,bsp->kbp", stacked, weight_rows, preferred_element_type=jnp.float32
    )
    col_sums = first_terms[2]
    series_block_sums = jnp.sum(series_data, axis=1)

    def to_slots(terms):
        outgoing = jnp.einsum("cb,kbp->kcp", slot_hot, terms, precision=HIGHEST)
        k = terms.shape[0]
        return outgoing.reshape(k, pix_count, capacity, pixels).transpose(1, 0, 2, 3)

    def owner_sum(arrived):
        k = arrived.shape[1]
        flat = arrived.transpose(1, 0, 2, 3).reshape(k, slot_count, pixels)
        return jnp.einsum("qc,kcp->kqp", received_onehot, flat, precision=HIGHEST)

    def from_owner(map_own):
        return jnp.dot(incoming_t, map_own, precision=HIGHEST).reshape(pix_count, capacity, pixels)

    def to_blocks(arrived):
        return jnp.dot(slot_hot_t, arrived.reshape(slot_count, pixels), precision=HIGHEST)

    out1 = to_slots(first_terms[:2])
    arr1 = pix_exchange(out1.reshape(pix_count, 2 * capacity, pixels), 0).reshape(out1.shape)
    own1 = det_sum(owner_sum(arr1).reshape(2 * PB_DEV, pixels), 1).reshape(2, PB_DEV, pixels)
    hit_plus = own1[0] + 1.0
    sky0 = (own1[1] / hit_plus).astype(jnp.bfloat16)
    back1 = pix_exchange(from_owner(sky0.astype(jnp.float32)).astype(jnp.bfloat16), 2)
    sky_blocks0 = to_blocks(back1.astype(jnp.float32))
    projected0 = jnp.sum(col_sums * sky_blocks0, axis=1)
    equation_target = jnp.dot(series_block_sums - projected0, base_hot, precision=HIGHEST) / samples

    def extra_rows(values):
        row = jnp.zeros((EXTRA, pixels), jnp.float32)
        return row.at[0, : values.shape[0]].set(values)

    def apply_round(amps, scalars, cid):
        per_block = jnp.dot(base_hot, amps, precision=HIGHEST)
        terms = per_block[:, None] * col_sums
        slots = to_slots(terms[None])[:, 0]
        payload = jnp.concatenate(
            [slots, jnp.broadcast_to(extra_rows(scalars)[None], (pix_count, EXTRA, pixels))], axis=1
        )
        arrived = pix_exchange(payload, cid)
        partial = owner_sum(arrived[:, None, :capacity])[0]
        scal = jnp.sum(arrived[:, capacity:], axis=0)
        summed = det_sum(jnp.concatenate([partial, scal], axis=0), cid + 1)
        binned = summed[:PB_DEV]
        sky = binned / hit_plus
        return binned, sky, summed[PB_DEV, : scalars.shape[0]]

    def project_back(sky, sky_scalars, cid):
        payload = jnp.concatenate(
            [from_owner(sky),
             jnp.broadcast_to(extra_rows(sky_scalars)[None], (pix_count, EXTRA, pixels))], axis=1
        )
        arrived = pix_exchange(payload, cid)
        sky_blocks = to_blocks(arrived[:, :capacity])
        scal = jnp.sum(arrived[:, capacity:], axis=0)[0, : sky_scalars.shape[0]]
        return jnp.sum(col_sums * sky_blocks, axis=1), scal

    def normal_action(amps, projected_blocks):
        collapsed = jnp.dot(projected_blocks, base_hot, precision=HIGHEST)
        return amps * (1.0 + per_base) - collapsed / samples

    r0 = equation_target
    binned_r0, sky_r0, _ = apply_round(r0, jnp.zeros((1,), jnp.float32), 3)
    proj_r0, _ = project_back(sky_r0, jnp.zeros((1,), jnp.float32), 5)
    v1 = normal_action(r0, proj_r0)
    weight_n = 1.0 + per_base
    local = jnp.stack([
        jnp.sum(r0 * r0),
        jnp.sum(r0 * v1),
        jnp.sum(v1 * v1),
        jnp.sum(r0 * v1 * weight_n),
        jnp.sum(v1 * v1 * weight_n),
    ])
    binned_v1, sky_v1, totals = apply_round(v1, local, 6)
    sky_products = jnp.stack([jnp.sum(binned_r0 * sky_v1), jnp.sum(binned_v1 * sky_v1)])
    proj_v1, sky_totals = project_back(sky_v1, sky_products, 8)
    v2 = normal_action(v1, proj_v1)

    rr0, r0v1, v1v1 = totals[0], totals[1], totals[2]
    r0v2 = totals[3] - sky_totals[0] / samples
    v1v2 = totals[4] - sky_totals[1] / samples
    alpha0 = rr0 / r0v1
    rr1 = rr0 - 2.0 * alpha0 * r0v1 + alpha0 * alpha0 * v1v1
    beta0 = rr1 / rr0
    grow = 1.0 + beta0
    d1_ad1 = grow * grow * r0v1 - grow * alpha0 * r0v2 - alpha0 * grow * v1v1 + alpha0 * alpha0 * v1v2
    alpha1 = rr1 / d1_ad1
    d1 = grow * r0 - alpha0 * v1
    ad1 = grow * v1 - alpha0 * v2
    offset_levels = alpha0 * r0 + alpha1 * d1
    leftover_error = r0 - alpha0 * v1 - alpha1 * ad1
    return (offset_levels[None], leftover_error[None])


def solution(mesh):
    placed = (
        P(("det", "pix"), None, None),
        P(("det", "pix"), None, None, None),
        P(("det", "pix"), None, None),
        P(("det", "pix"), None),
        P(("det", "pix"), None),
    )
    return jax.shard_map(
        body,
        mesh=mesh,
        in_specs=placed,
        out_specs=(P(("det", "pix"), None), P(("det", "pix"), None)),
        check_vma=False,
    )
```

```python
import functools

import jax
import jax.numpy as jnp
from jax import lax
from jax.experimental import pallas as pl
from jax.experimental.pallas import tpu as pltpu
from jax.sharding import PartitionSpec as P

MESH = pl.DeviceIdType.MESH
PB_DEV = 64
NBASE_DEV = 128
HIGHEST = lax.Precision.HIGHEST


def _greet(peers, device_of):
    barrier = pltpu.get_barrier_semaphore()
    for peer in peers:
        pl.semaphore_signal(barrier, inc=1, device_id=device_of(peer), device_id_type=MESH)
    pl.semaphore_wait(barrier, len(peers))


def _det_sum_kernel(n, x_ref, o_ref, recv, send_sem, recv_sem, local_sem):
    me = lax.axis_index("det")
    pix = lax.axis_index("pix")
    device_of = lambda d: (d, pix)
    _greet([lax.rem(me + k, n) for k in range(1, n)], device_of)
    sends = []
    for k in range(1, n):
        peer = lax.rem(me + k, n)
        copy = pltpu.make_async_remote_copy(
            src_ref=x_ref, dst_ref=recv.at[me], send_sem=send_sem.at[k],
            recv_sem=recv_sem.at[me], device_id=device_of(peer), device_id_type=MESH)
        copy.start()
        sends.append(copy)
    local = pltpu.make_async_copy(x_ref, recv.at[me], local_sem)
    local.start()
    for copy in sends:
        copy.wait_send()
    for k in range(1, n):
        src = lax.rem(me + k, n)
        pltpu.make_async_remote_copy(
            src_ref=x_ref, dst_ref=recv.at[src], send_sem=send_sem.at[k],
            recv_sem=recv_sem.at[src], device_id=device_of(src), device_id_type=MESH).wait_recv()
    local.wait()
    acc = recv[0]
    for s in range(1, n):
        acc = acc + recv[s]
    o_ref[...] = acc


def det_sum(x, cid):
    n = lax.axis_size("det")
    return pl.pallas_call(
        functools.partial(_det_sum_kernel, n),
        out_shape=jax.ShapeDtypeStruct(x.shape, x.dtype),
        in_specs=[pl.BlockSpec(memory_space=pltpu.VMEM)],
        out_specs=pl.BlockSpec(memory_space=pltpu.VMEM),
        scratch_shapes=[
            pltpu.VMEM((n,) + x.shape, x.dtype),
            pltpu.SemaphoreType.DMA((n,)),
            pltpu.SemaphoreType.DMA((n,)),
            pltpu.SemaphoreType.DMA(()),
        ],
        compiler_params=pltpu.CompilerParams(collective_id=cid, has_side_effects=True),
    )(x)


def _pix_exchange_kernel(n, spread, *refs):
    count = len(spread)
    ins, outs = refs[:count], refs[count:2 * count]
    send_sem, recv_sem, local_sem = refs[2 * count:]
    me = lax.axis_index("pix")
    det = lax.axis_index("det")
    device_of = lambda j: (det, j)
    _greet([lax.rem(me + k, n) for k in range(1, n)], device_of)
    source = lambda a, j: ins[a].at[j] if spread[a] else ins[a]
    sends, locals_ = [], []
    for a in range(count):
        for k in range(1, n):
            peer = lax.rem(me + k, n)
            copy = pltpu.make_async_remote_copy(
                src_ref=source(a, peer), dst_ref=outs[a].at[me], send_sem=send_sem.at[a, k],
                recv_sem=recv_sem.at[a, me], device_id=device_of(peer), device_id_type=MESH)
            copy.start()
            sends.append(copy)
        local = pltpu.make_async_copy(source(a, me), outs[a].at[me], local_sem.at[a])
        local.start()
        locals_.append(local)
    for copy in sends:
        copy.wait_send()
    for a in range(count):
        for k in range(1, n):
            src = lax.rem(me + k, n)
            pltpu.make_async_remote_copy(
                src_ref=source(a, src), dst_ref=outs[a].at[src], send_sem=send_sem.at[a, k],
                recv_sem=recv_sem.at[a, src], device_id=device_of(src), device_id_type=MESH).wait_recv()
        locals_[a].wait()


def pix_exchange(arrays, spread, cid):
    n = lax.axis_size("pix")
    count = len(arrays)
    out_shape = [
        jax.ShapeDtypeStruct(x.shape if s else (n,) + x.shape, x.dtype) for x, s in zip(arrays, spread)
    ]
    return pl.pallas_call(
        functools.partial(_pix_exchange_kernel, n, tuple(spread)),
        out_shape=out_shape,
        in_specs=[pl.BlockSpec(memory_space=pltpu.VMEM)] * count,
        out_specs=[pl.BlockSpec(memory_space=pltpu.VMEM)] * count,
        scratch_shapes=[
            pltpu.SemaphoreType.DMA((count, n)),
            pltpu.SemaphoreType.DMA((count, n)),
            pltpu.SemaphoreType.DMA((count,)),
        ],
        compiler_params=pltpu.CompilerParams(collective_id=cid, has_side_effects=True),
    )(*arrays)


def body(timestream, weights, block_owner, block_local, baseline_of):
    series_data = timestream[0]
    weight_rows = weights[0]
    owners = block_owner[0, :, 0]
    local_idx = block_local[0]
    segments_row = baseline_of[0]
    blocks, samples, pixels = weight_rows.shape
    pix_count = lax.axis_size("pix")
    sky_blocks_count = pix_count * PB_DEV

    base_hot = (segments_row[:, None] == jnp.arange(NBASE_DEV)[None, :]).astype(jnp.float32)
    per_base = jnp.sum(base_hot, axis=0)
    weight_n = 1.0 + per_base
    block_pix = owners * PB_DEV + local_idx
    sky_hot = (block_pix[None, :] == jnp.arange(sky_blocks_count)[:, None]).astype(jnp.float32)
    sky_hot_t = (block_pix[:, None] == jnp.arange(sky_blocks_count)[None, :]).astype(jnp.bfloat16)

    unit_row_vector = jnp.ones((pixels,), jnp.bfloat16)
    row_sums = jnp.einsum(
        "bsp,p->bs", weight_rows, unit_row_vector, preferred_element_type=jnp.float32
    ).astype(jnp.bfloat16)
    stacked = jnp.stack(
        [row_sums, series_data.astype(jnp.bfloat16), jnp.ones_like(row_sums)]
    )
    first_terms = jnp.einsum(
        "kbs,bsp->kbp", stacked, weight_rows, preferred_element_type=jnp.float32
    )
    col_sums = first_terms[2]
    series_block_sums = jnp.sum(series_data, axis=1)

    def to_owners(terms):
        dense = jnp.einsum("qb,kbp->kqp", sky_hot, terms, precision=HIGHEST)
        k = terms.shape[0]
        dense = dense.reshape(k, pix_count, PB_DEV, pixels).transpose(1, 0, 2, 3)
        return dense.reshape(pix_count, k * PB_DEV, pixels).astype(jnp.bfloat16)

    def to_blocks(sky_all):
        return jnp.dot(sky_hot_t, sky_all.reshape(sky_blocks_count, pixels),
                       preferred_element_type=jnp.float32)

    def scalar_rows(values):
        row = jnp.zeros((8, 128), jnp.float32)
        return row.at[0, : values.shape[0]].set(values)

    (arr1,) = pix_exchange([to_owners(first_terms[:2])], [True], 0)
    part1 = jnp.sum(arr1.astype(jnp.float32), axis=0)
    own1 = det_sum(part1, 1).reshape(2, PB_DEV, pixels)
    hit_plus = own1[0] + 1.0
    sky0 = (own1[1] / hit_plus).astype(jnp.bfloat16)
    (back1,) = pix_exchange([sky0], [False], 2)
    projected0 = jnp.sum(col_sums * to_blocks(back1), axis=1)
    r0 = jnp.dot(series_block_sums - projected0, base_hot, precision=HIGHEST) / samples

    def apply_round(amps, scalars, cid):
        per_block = jnp.dot(base_hot, amps, precision=HIGHEST)
        terms = per_block[:, None] * col_sums
        scal = jnp.broadcast_to(scalar_rows(scalars)[None], (pix_count, 8, 128))
        arrived, scal_in = pix_exchange([to_owners(terms[None]), scal], [True, True], cid)
        partial = jnp.sum(arrived.astype(jnp.float32), axis=0)
        scal_sum = jnp.sum(scal_in, axis=0)
        scal_wide = jnp.zeros((8, pixels), jnp.float32).at[:, :128].set(scal_sum)
        summed = det_sum(jnp.concatenate([partial, scal_wide], axis=0), cid + 1)
        binned = summed[:PB_DEV]
        sky = (binned / hit_plus).astype(jnp.bfloat16)
        return binned, sky, summed[PB_DEV, : scalars.shape[0]]

    def project_back(sky, sky_scalars, cid):
        back, scal_in = pix_exchange([sky, scalar_rows(sky_scalars)], [False, False], cid)
        scal = jnp.sum(scal_in, axis=0)[0, : sky_scalars.shape[0]]
        return jnp.sum(col_sums * to_blocks(back), axis=1), scal

    def normal_action(amps, projected_blocks):
        collapsed = jnp.dot(projected_blocks, base_hot, precision=HIGHEST)
        return amps * weight_n - collapsed / samples

    binned_r0, sky_r0, _ = apply_round(r0, jnp.zeros((1,), jnp.float32), 3)
    proj_r0, _ = project_back(sky_r0, jnp.zeros((1,), jnp.float32), 5)
    v1 = normal_action(r0, proj_r0)
    local = jnp.stack([
        jnp.sum(r0 * r0),
        jnp.sum(r0 * v1),
        jnp.sum(v1 * v1),
        jnp.sum(r0 * v1 * weight_n),
        jnp.sum(v1 * v1 * weight_n),
    ])
    binned_v1, sky_v1, totals = apply_round(v1, local, 6)
    sky_v1_wide = sky_v1.astype(jnp.float32)
    sky_products = jnp.stack([jnp.sum(binned_r0 * sky_v1_wide), jnp.sum(binned_v1 * sky_v1_wide)])
    proj_v1, sky_totals = project_back(sky_v1, sky_products, 8)
    v2 = normal_action(v1, proj_v1)

    rr0, r0v1, v1v1 = totals[0], totals[1], totals[2]
    r0v2 = totals[3] - sky_totals[0] / samples
    v1v2 = totals[4] - sky_totals[1] / samples
    alpha0 = rr0 / r0v1
    rr1 = rr0 - 2.0 * alpha0 * r0v1 + alpha0 * alpha0 * v1v1
    beta0 = rr1 / rr0
    grow = 1.0 + beta0
    d1_ad1 = grow * grow * r0v1 - grow * alpha0 * r0v2 - alpha0 * grow * v1v1 + alpha0 * alpha0 * v1v2
    alpha1 = rr1 / d1_ad1
    d1 = grow * r0 - alpha0 * v1
    ad1 = grow * v1 - alpha0 * v2
    offset_levels = alpha0 * r0 + alpha1 * d1
    leftover_error = r0 - alpha0 * v1 - alpha1 * ad1
    return (offset_levels[None], leftover_error[None])


def solution(mesh):
    placed = (
        P(("det", "pix"), None, None),
        P(("det", "pix"), None, None, None),
        P(("det", "pix"), None, None),
        P(("det", "pix"), None),
        P(("det", "pix"), None),
    )
    return jax.shard_map(
        body,
        mesh=mesh,
        in_specs=placed,
        out_specs=(P(("det", "pix"), None), P(("det", "pix"), None)),
        check_vma=False,
    )
```

```python
import functools

import jax
import jax.numpy as jnp
from jax import lax
from jax.experimental import pallas as pl
from jax.experimental.pallas import tpu as pltpu
from jax.sharding import PartitionSpec as P

MESH = pl.DeviceIdType.MESH
PB_DEV = 64
NBASE_DEV = 128
HIGHEST = lax.Precision.HIGHEST


def _greet(peers, device_of):
    barrier = pltpu.get_barrier_semaphore()
    for peer in peers:
        pl.semaphore_signal(barrier, inc=1, device_id=device_of(peer), device_id_type=MESH)
    pl.semaphore_wait(barrier, len(peers))


def _det_sum_kernel(n, x_ref, o_ref, recv, send_sem, recv_sem, local_sem):
    me = lax.axis_index("det")
    pix = lax.axis_index("pix")
    device_of = lambda d: (d, pix)
    _greet([lax.rem(me + k, n) for k in range(1, n)], device_of)
    sends = []
    for k in range(1, n):
        peer = lax.rem(me + k, n)
        copy = pltpu.make_async_remote_copy(
            src_ref=x_ref, dst_ref=recv.at[me], send_sem=send_sem.at[k],
            recv_sem=recv_sem.at[me], device_id=device_of(peer), device_id_type=MESH)
        copy.start()
        sends.append(copy)
    local = pltpu.make_async_copy(x_ref, recv.at[me], local_sem)
    local.start()
    for copy in sends:
        copy.wait_send()
    for k in range(1, n):
        src = lax.rem(me + k, n)
        pltpu.make_async_remote_copy(
            src_ref=x_ref, dst_ref=recv.at[src], send_sem=send_sem.at[k],
            recv_sem=recv_sem.at[src], device_id=device_of(src), device_id_type=MESH).wait_recv()
    local.wait()
    acc = recv[0]
    for s in range(1, n):
        acc = acc + recv[s]
    o_ref[...] = acc


def det_sum(x, cid):
    n = lax.axis_size("det")
    return pl.pallas_call(
        functools.partial(_det_sum_kernel, n),
        out_shape=jax.ShapeDtypeStruct(x.shape, x.dtype),
        in_specs=[pl.BlockSpec(memory_space=pltpu.VMEM)],
        out_specs=pl.BlockSpec(memory_space=pltpu.VMEM),
        scratch_shapes=[
            pltpu.VMEM((n,) + x.shape, x.dtype),
            pltpu.SemaphoreType.DMA((n,)),
            pltpu.SemaphoreType.DMA((n,)),
            pltpu.SemaphoreType.DMA(()),
        ],
        compiler_params=pltpu.CompilerParams(collective_id=cid, has_side_effects=True),
    )(x)


def _pix_exchange_kernel(n, spread, *refs):
    count = len(spread)
    ins, outs = refs[:count], refs[count:2 * count]
    send_sem, recv_sem, local_sem = refs[2 * count:]
    me = lax.axis_index("pix")
    det = lax.axis_index("det")
    device_of = lambda j: (det, j)
    _greet([lax.rem(me + k, n) for k in range(1, n)], device_of)
    source = lambda a, j: ins[a].at[j] if spread[a] else ins[a]
    sends, locals_ = [], []
    for a in range(count):
        for k in range(1, n):
            peer = lax.rem(me + k, n)
            copy = pltpu.make_async_remote_copy(
                src_ref=source(a, peer), dst_ref=outs[a].at[me], send_sem=send_sem.at[a, k],
                recv_sem=recv_sem.at[a, me], device_id=device_of(peer), device_id_type=MESH)
            copy.start()
            sends.append(copy)
        local = pltpu.make_async_copy(source(a, me), outs[a].at[me], local_sem.at[a])
        local.start()
        locals_.append(local)
    for copy in sends:
        copy.wait_send()
    for a in range(count):
        for k in range(1, n):
            src = lax.rem(me + k, n)
            pltpu.make_async_remote_copy(
                src_ref=source(a, src), dst_ref=outs[a].at[src], send_sem=send_sem.at[a, k],
                recv_sem=recv_sem.at[a, src], device_id=device_of(src), device_id_type=MESH).wait_recv()
        locals_[a].wait()


def pix_exchange(arrays, spread, cid):
    n = lax.axis_size("pix")
    count = len(arrays)
    out_shape = [
        jax.ShapeDtypeStruct(x.shape if s else (n,) + x.shape, x.dtype) for x, s in zip(arrays, spread)
    ]
    return pl.pallas_call(
        functools.partial(_pix_exchange_kernel, n, tuple(spread)),
        out_shape=out_shape,
        in_specs=[pl.BlockSpec(memory_space=pltpu.VMEM)] * count,
        out_specs=[pl.BlockSpec(memory_space=pltpu.VMEM)] * count,
        scratch_shapes=[
            pltpu.SemaphoreType.DMA((count, n)),
            pltpu.SemaphoreType.DMA((count, n)),
            pltpu.SemaphoreType.DMA((count,)),
        ],
        compiler_params=pltpu.CompilerParams(collective_id=cid, has_side_effects=True),
    )(*arrays)


def _all_exchange_kernel(npix, n, spread, *refs):
    count = len(spread)
    ins, outs = refs[:count], refs[count:2 * count]
    send_sem, recv_sem, local_sem = refs[2 * count:]
    me = lax.axis_index("det") * npix + lax.axis_index("pix")
    device_of = lambda c: (lax.div(c, npix), lax.rem(c, npix))
    source = lambda a, c: ins[a].at[c] if spread[a] else ins[a]
    barrier = pltpu.get_barrier_semaphore()

    def greet(k, carry):
        peer = lax.rem(me + k, n)
        pl.semaphore_signal(barrier, inc=1, device_id=device_of(peer), device_id_type=MESH)
        return carry

    lax.fori_loop(1, n, greet, 0)
    pl.semaphore_wait(barrier, n - 1)

    def copy(a, k, c, slot):
        return pltpu.make_async_remote_copy(
            src_ref=source(a, c), dst_ref=outs[a].at[slot], send_sem=send_sem.at[a, k],
            recv_sem=recv_sem.at[a, slot], device_id=device_of(c), device_id_type=MESH)

    def send(k, carry):
        peer = lax.rem(me + k, n)
        for a in range(count):
            copy(a, k, peer, me).start()
        return carry

    lax.fori_loop(1, n, send, 0)
    locals_ = []
    for a in range(count):
        local = pltpu.make_async_copy(source(a, me), outs[a].at[me], local_sem.at[a])
        local.start()
        locals_.append(local)

    def finish(k, carry):
        peer = lax.rem(me + k, n)
        for a in range(count):
            copy(a, k, peer, me).wait_send()
            copy(a, k, peer, peer).wait_recv()
        return carry

    lax.fori_loop(1, n, finish, 0)
    for local in locals_:
        local.wait()


def all_exchange(arrays, spread, cid):
    npix = lax.axis_size("pix")
    n = lax.axis_size("det") * npix
    count = len(arrays)
    out_shape = [
        jax.ShapeDtypeStruct(x.shape if s else (n,) + x.shape, x.dtype) for x, s in zip(arrays, spread)
    ]
    return pl.pallas_call(
        functools.partial(_all_exchange_kernel, npix, n, tuple(spread)),
        out_shape=out_shape,
        in_specs=[pl.BlockSpec(memory_space=pltpu.VMEM)] * count,
        out_specs=[pl.BlockSpec(memory_space=pltpu.VMEM)] * count,
        scratch_shapes=[
            pltpu.SemaphoreType.DMA((count, n)),
            pltpu.SemaphoreType.DMA((count, n)),
            pltpu.SemaphoreType.DMA((count,)),
        ],
        compiler_params=pltpu.CompilerParams(collective_id=cid, has_side_effects=True),
    )(*arrays)


def body(timestream, weights, block_owner, block_local, baseline_of):
    series_data = timestream[0]
    weight_rows = weights[0]
    owners = block_owner[0, :, 0]
    local_idx = block_local[0]
    segments_row = baseline_of[0]
    blocks, samples, pixels = weight_rows.shape
    pix_count = lax.axis_size("pix")
    devices = lax.axis_size("det") * pix_count
    sky_blocks_count = pix_count * PB_DEV
    cell = sky_blocks_count // devices
    cell_rows = cell * pixels // 128

    base_hot = (segments_row[:, None] == jnp.arange(NBASE_DEV)[None, :]).astype(jnp.float32)
    per_base = jnp.sum(base_hot, axis=0)
    weight_n = 1.0 + per_base
    block_pix = owners * PB_DEV + local_idx
    sky_hot = (block_pix[None, :] == jnp.arange(sky_blocks_count)[:, None]).astype(jnp.float32)
    sky_hot_t = (block_pix[:, None] == jnp.arange(sky_blocks_count)[None, :]).astype(jnp.bfloat16)

    unit_row_vector = jnp.ones((pixels,), jnp.bfloat16)
    row_sums = jnp.einsum(
        "bsp,p->bs", weight_rows, unit_row_vector, preferred_element_type=jnp.float32
    ).astype(jnp.bfloat16)
    stacked = jnp.stack(
        [row_sums, series_data.astype(jnp.bfloat16), jnp.ones_like(row_sums)]
    )
    first_terms = jnp.einsum(
        "kbs,bsp->kbp", stacked, weight_rows, preferred_element_type=jnp.float32
    )
    col_sums = first_terms[2]
    series_block_sums = jnp.sum(series_data, axis=1)

    def to_cells(terms):
        dense = jnp.einsum("qb,kbp->kqp", sky_hot, terms, precision=HIGHEST)
        k = terms.shape[0]
        dense = dense.reshape(k, devices, cell_rows, 128).transpose(1, 0, 2, 3)
        return dense.reshape(devices, k * cell_rows, 128).astype(jnp.bfloat16)

    def to_blocks(sky_cells):
        return jnp.dot(sky_hot_t, sky_cells.reshape(sky_blocks_count, pixels),
                       preferred_element_type=jnp.float32)

    def scalar_rows(values):
        row = jnp.zeros((8, 128), jnp.float32)
        return row.at[0, : values.shape[0]].set(values)

    def cell_sum(arrived, k):
        total = jnp.sum(arrived.astype(jnp.float32), axis=0)
        return total.reshape(k, cell, pixels)

    (arr1,) = all_exchange([to_cells(first_terms[:2])], [True], 0)
    own1 = cell_sum(arr1, 2)
    hit_plus = own1[0] + 1.0
    sky0 = (own1[1] / hit_plus).astype(jnp.bfloat16)
    (back1,) = all_exchange([sky0.reshape(cell_rows, 128)], [False], 1)
    projected0 = jnp.sum(col_sums * to_blocks(back1), axis=1)
    r0 = jnp.dot(series_block_sums - projected0, base_hot, precision=HIGHEST) / samples

    def apply_round(amps, scalars, cid):
        per_block = jnp.dot(base_hot, amps, precision=HIGHEST)
        terms = per_block[:, None] * col_sums
        arrays, spread = [to_cells(terms[None])], [True]
        if scalars is not None:
            arrays.append(scalar_rows(scalars))
            spread.append(False)
        got = all_exchange(arrays, spread, cid)
        binned = cell_sum(got[0], 1)[0]
        sky = (binned / hit_plus).astype(jnp.bfloat16)
        totals = None if scalars is None else jnp.sum(got[1], axis=0)[0, : scalars.shape[0]]
        return binned, sky, totals

    def project_back(sky, sky_scalars, cid):
        arrays, spread = [sky.reshape(cell_rows, 128)], [False]
        if sky_scalars is not None:
            arrays.append(scalar_rows(sky_scalars))
            spread.append(False)
        got = all_exchange(arrays, spread, cid)
        scal = None if sky_scalars is None else jnp.sum(got[1], axis=0)[0, : sky_scalars.shape[0]]
        return jnp.sum(col_sums * to_blocks(got[0]), axis=1), scal

    def normal_action(amps, projected_blocks):
        collapsed = jnp.dot(projected_blocks, base_hot, precision=HIGHEST)
        return amps * weight_n - collapsed / samples

    binned_r0, sky_r0, _ = apply_round(r0, None, 2)
    proj_r0, _ = project_back(sky_r0, None, 3)
    v1 = normal_action(r0, proj_r0)
    local = jnp.stack([
        jnp.sum(r0 * r0),
        jnp.sum(r0 * v1),
        jnp.sum(v1 * v1),
        jnp.sum(r0 * v1 * weight_n),
        jnp.sum(v1 * v1 * weight_n),
    ])
    binned_v1, sky_v1, totals = apply_round(v1, local, 4)
    sky_v1_wide = sky_v1.astype(jnp.float32)
    sky_products = jnp.stack([jnp.sum(binned_r0 * sky_v1_wide), jnp.sum(binned_v1 * sky_v1_wide)])
    proj_v1, sky_totals = project_back(sky_v1, sky_products, 5)
    v2 = normal_action(v1, proj_v1)

    rr0, r0v1, v1v1 = totals[0], totals[1], totals[2]
    r0v2 = totals[3] - sky_totals[0] / samples
    v1v2 = totals[4] - sky_totals[1] / samples
    alpha0 = rr0 / r0v1
    rr1 = rr0 - 2.0 * alpha0 * r0v1 + alpha0 * alpha0 * v1v1
    beta0 = rr1 / rr0
    grow = 1.0 + beta0
    d1_ad1 = grow * grow * r0v1 - grow * alpha0 * r0v2 - alpha0 * grow * v1v1 + alpha0 * alpha0 * v1v2
    alpha1 = rr1 / d1_ad1
    d1 = grow * r0 - alpha0 * v1
    ad1 = grow * v1 - alpha0 * v2
    offset_levels = alpha0 * r0 + alpha1 * d1
    leftover_error = r0 - alpha0 * v1 - alpha1 * ad1
    return (offset_levels[None], leftover_error[None])


def solution(mesh):
    placed = (
        P(("det", "pix"), None, None),
        P(("det", "pix"), None, None, None),
        P(("det", "pix"), None, None),
        P(("det", "pix"), None),
        P(("det", "pix"), None),
    )
    return jax.shard_map(
        body,
        mesh=mesh,
        in_specs=placed,
        out_specs=(P(("det", "pix"), None), P(("det", "pix"), None)),
        check_vma=False,
    )
```

```python
import functools

import jax
import jax.numpy as jnp
from jax import lax
from jax.experimental import pallas as pl
from jax.experimental.pallas import tpu as pltpu
from jax.sharding import PartitionSpec as P

MESH = pl.DeviceIdType.MESH
PB_DEV = 64
NBASE_DEV = 128
HIGHEST = lax.Precision.HIGHEST


def _greet(peers, device_of):
    barrier = pltpu.get_barrier_semaphore()
    for peer in peers:
        pl.semaphore_signal(barrier, inc=1, device_id=device_of(peer), device_id_type=MESH)
    pl.semaphore_wait(barrier, len(peers))


def _det_sum_kernel(n, x_ref, o_ref, recv, send_sem, recv_sem, local_sem):
    me = lax.axis_index("det")
    pix = lax.axis_index("pix")
    device_of = lambda d: (d, pix)
    _greet([lax.rem(me + k, n) for k in range(1, n)], device_of)
    sends = []
    for k in range(1, n):
        peer = lax.rem(me + k, n)
        copy = pltpu.make_async_remote_copy(
            src_ref=x_ref, dst_ref=recv.at[me], send_sem=send_sem.at[k],
            recv_sem=recv_sem.at[me], device_id=device_of(peer), device_id_type=MESH)
        copy.start()
        sends.append(copy)
    local = pltpu.make_async_copy(x_ref, recv.at[me], local_sem)
    local.start()
    for copy in sends:
        copy.wait_send()
    for k in range(1, n):
        src = lax.rem(me + k, n)
        pltpu.make_async_remote_copy(
            src_ref=x_ref, dst_ref=recv.at[src], send_sem=send_sem.at[k],
            recv_sem=recv_sem.at[src], device_id=device_of(src), device_id_type=MESH).wait_recv()
    local.wait()
    acc = recv[0]
    for s in range(1, n):
        acc = acc + recv[s]
    o_ref[...] = acc


def det_sum(x, cid):
    n = lax.axis_size("det")
    return pl.pallas_call(
        functools.partial(_det_sum_kernel, n),
        out_shape=jax.ShapeDtypeStruct(x.shape, x.dtype),
        in_specs=[pl.BlockSpec(memory_space=pltpu.VMEM)],
        out_specs=pl.BlockSpec(memory_space=pltpu.VMEM),
        scratch_shapes=[
            pltpu.VMEM((n,) + x.shape, x.dtype),
            pltpu.SemaphoreType.DMA((n,)),
            pltpu.SemaphoreType.DMA((n,)),
            pltpu.SemaphoreType.DMA(()),
        ],
        compiler_params=pltpu.CompilerParams(collective_id=cid, has_side_effects=True),
    )(x)


def _pix_exchange_kernel(n, spread, *refs):
    count = len(spread)
    ins, outs = refs[:count], refs[count:2 * count]
    send_sem, recv_sem, local_sem = refs[2 * count:]
    me = lax.axis_index("pix")
    det = lax.axis_index("det")
    device_of = lambda j: (det, j)
    _greet([lax.rem(me + k, n) for k in range(1, n)], device_of)
    source = lambda a, j: ins[a].at[j] if spread[a] else ins[a]
    sends, locals_ = [], []
    for a in range(count):
        for k in range(1, n):
            peer = lax.rem(me + k, n)
            copy = pltpu.make_async_remote_copy(
                src_ref=source(a, peer), dst_ref=outs[a].at[me], send_sem=send_sem.at[a, k],
                recv_sem=recv_sem.at[a, me], device_id=device_of(peer), device_id_type=MESH)
            copy.start()
            sends.append(copy)
        local = pltpu.make_async_copy(source(a, me), outs[a].at[me], local_sem.at[a])
        local.start()
        locals_.append(local)
    for copy in sends:
        copy.wait_send()
    for a in range(count):
        for k in range(1, n):
            src = lax.rem(me + k, n)
            pltpu.make_async_remote_copy(
                src_ref=source(a, src), dst_ref=outs[a].at[src], send_sem=send_sem.at[a, k],
                recv_sem=recv_sem.at[a, src], device_id=device_of(src), device_id_type=MESH).wait_recv()
        locals_[a].wait()


def pix_exchange(arrays, spread, cid):
    n = lax.axis_size("pix")
    count = len(arrays)
    out_shape = [
        jax.ShapeDtypeStruct(x.shape if s else (n,) + x.shape, x.dtype) for x, s in zip(arrays, spread)
    ]
    return pl.pallas_call(
        functools.partial(_pix_exchange_kernel, n, tuple(spread)),
        out_shape=out_shape,
        in_specs=[pl.BlockSpec(memory_space=pltpu.VMEM)] * count,
        out_specs=[pl.BlockSpec(memory_space=pltpu.VMEM)] * count,
        scratch_shapes=[
            pltpu.SemaphoreType.DMA((count, n)),
            pltpu.SemaphoreType.DMA((count, n)),
            pltpu.SemaphoreType.DMA((count,)),
        ],
        compiler_params=pltpu.CompilerParams(collective_id=cid, has_side_effects=True),
    )(*arrays)


def _all_exchange_kernel(npix, n, spread, *refs):
    count = len(spread)
    ins, outs = refs[:count], refs[count:2 * count]
    send_sem, recv_sem, local_sem = refs[2 * count:]
    me = lax.axis_index("det") * npix + lax.axis_index("pix")
    device_of = lambda c: (lax.div(c, npix), lax.rem(c, npix))
    source = lambda a, c: ins[a].at[c] if spread[a] else ins[a]
    barrier = pltpu.get_barrier_semaphore()

    def greet(k, carry):
        peer = lax.rem(me + k, n)
        pl.semaphore_signal(barrier, inc=1, device_id=device_of(peer), device_id_type=MESH)
        return carry

    lax.fori_loop(1, n, greet, 0)
    pl.semaphore_wait(barrier, n - 1)

    def copy(a, k, c, slot):
        return pltpu.make_async_remote_copy(
            src_ref=source(a, c), dst_ref=outs[a].at[slot], send_sem=send_sem.at[a, k],
            recv_sem=recv_sem.at[a, slot], device_id=device_of(c), device_id_type=MESH)

    def send(k, carry):
        peer = lax.rem(me + k, n)
        for a in range(count):
            copy(a, k, peer, me).start()
        return carry

    lax.fori_loop(1, n, send, 0)
    locals_ = []
    for a in range(count):
        local = pltpu.make_async_copy(source(a, me), outs[a].at[me], local_sem.at[a])
        local.start()
        locals_.append(local)

    def finish(k, carry):
        peer = lax.rem(me + k, n)
        for a in range(count):
            copy(a, k, peer, me).wait_send()
            copy(a, k, peer, peer).wait_recv()
        return carry

    lax.fori_loop(1, n, finish, 0)
    for local in locals_:
        local.wait()


def all_exchange(arrays, spread, cid):
    npix = lax.axis_size("pix")
    n = lax.axis_size("det") * npix
    count = len(arrays)
    out_shape = [
        jax.ShapeDtypeStruct(x.shape if s else (n,) + x.shape, x.dtype) for x, s in zip(arrays, spread)
    ]
    return pl.pallas_call(
        functools.partial(_all_exchange_kernel, npix, n, tuple(spread)),
        out_shape=out_shape,
        in_specs=[pl.BlockSpec(memory_space=pltpu.VMEM)] * count,
        out_specs=[pl.BlockSpec(memory_space=pltpu.VMEM)] * count,
        scratch_shapes=[
            pltpu.SemaphoreType.DMA((count, n)),
            pltpu.SemaphoreType.DMA((count, n)),
            pltpu.SemaphoreType.DMA((count,)),
        ],
        compiler_params=pltpu.CompilerParams(collective_id=cid, has_side_effects=True),
    )(*arrays)


def body(timestream, weights, block_owner, block_local, baseline_of):
    series_data = timestream[0]
    weight_rows = weights[0]
    owners = block_owner[0, :, 0]
    local_idx = block_local[0]
    segments_row = baseline_of[0]
    blocks, samples, pixels = weight_rows.shape
    pix_count = lax.axis_size("pix")
    devices = lax.axis_size("det") * pix_count
    sky_blocks_count = pix_count * PB_DEV
    cell = sky_blocks_count // devices
    cell_rows = cell * pixels // 128

    base_hot = (segments_row[:, None] == jnp.arange(NBASE_DEV)[None, :]).astype(jnp.float32)
    per_base = jnp.sum(base_hot, axis=0)
    weight_n = 1.0 + per_base
    block_pix = owners * PB_DEV + local_idx
    sky_hot = (block_pix[None, :] == jnp.arange(sky_blocks_count)[:, None]).astype(jnp.float32)
    sky_hot_t = (block_pix[:, None] == jnp.arange(sky_blocks_count)[None, :]).astype(jnp.bfloat16)

    unit_row_vector = jnp.ones((pixels,), jnp.bfloat16)
    row_sums = jnp.einsum(
        "bsp,p->bs", weight_rows, unit_row_vector, preferred_element_type=jnp.float32
    ).astype(jnp.bfloat16)
    stacked = jnp.stack(
        [row_sums, series_data.astype(jnp.bfloat16), jnp.ones_like(row_sums)]
    )
    first_terms = jnp.einsum(
        "kbs,bsp->kbp", stacked, weight_rows, preferred_element_type=jnp.float32
    )
    col_sums = first_terms[2]
    series_block_sums = jnp.sum(series_data, axis=1)

    def to_cells(terms):
        dense = jnp.einsum("qb,kbp->kqp", sky_hot, terms, precision=HIGHEST)
        k = terms.shape[0]
        dense = dense.reshape(k, devices, cell_rows, 128).transpose(1, 0, 2, 3)
        return dense.reshape(devices, k * cell_rows, 128).astype(jnp.bfloat16)

    def to_blocks(sky_cells):
        return jnp.dot(sky_hot_t, sky_cells.reshape(sky_blocks_count, pixels),
                       preferred_element_type=jnp.float32)

    def scalar_rows(values):
        row = jnp.zeros((1, 128), jnp.float32)
        return row.at[0, : values.shape[0]].set(values)

    def cell_sum(arrived, k):
        total = jnp.sum(arrived.astype(jnp.float32), axis=0)
        return total.reshape(k, cell, pixels)

    (arr1,) = all_exchange([to_cells(first_terms[:2])], [True], 0)
    own1 = cell_sum(arr1, 2)
    hit_plus = own1[0] + 1.0
    sky0 = (own1[1] / hit_plus).astype(jnp.bfloat16)
    (back1,) = all_exchange([sky0.reshape(cell_rows, 128)], [False], 1)
    projected0 = jnp.sum(col_sums * to_blocks(back1), axis=1)
    r0 = jnp.dot(series_block_sums - projected0, base_hot, precision=HIGHEST) / samples

    def apply_round(amps, scalars, cid):
        per_block = jnp.dot(base_hot, amps, precision=HIGHEST)
        terms = per_block[:, None] * col_sums
        arrays, spread = [to_cells(terms[None])], [True]
        if scalars is not None:
            arrays.append(scalar_rows(scalars))
            spread.append(False)
        got = all_exchange(arrays, spread, cid)
        binned = cell_sum(got[0], 1)[0]
        sky = (binned / hit_plus).astype(jnp.bfloat16)
        totals = None if scalars is None else jnp.sum(got[1], axis=0)[0, : scalars.shape[0]]
        return binned, sky, totals

    def project_back(sky, sky_scalars, cid):
        arrays, spread = [sky.reshape(cell_rows, 128)], [False]
        if sky_scalars is not None:
            arrays.append(scalar_rows(sky_scalars))
            spread.append(False)
        got = all_exchange(arrays, spread, cid)
        scal = None if sky_scalars is None else jnp.sum(got[1], axis=0)[0, : sky_scalars.shape[0]]
        return jnp.sum(col_sums * to_blocks(got[0]), axis=1), scal

    def normal_action(amps, projected_blocks):
        collapsed = jnp.dot(projected_blocks, base_hot, precision=HIGHEST)
        return amps * weight_n - collapsed / samples

    binned_r0, sky_r0, _ = apply_round(r0, None, 2)
    proj_r0, _ = project_back(sky_r0, None, 3)
    v1 = normal_action(r0, proj_r0)
    local = jnp.stack([
        jnp.sum(r0 * r0),
        jnp.sum(r0 * v1),
        jnp.sum(v1 * v1),
        jnp.sum(r0 * v1 * weight_n),
        jnp.sum(v1 * v1 * weight_n),
    ])
    binned_v1, sky_v1, _ = apply_round(v1, None, 4)
    sky_v1_wide = sky_v1.astype(jnp.float32)
    carried = jnp.concatenate(
        [local, jnp.stack([jnp.sum(binned_r0 * sky_v1_wide), jnp.sum(binned_v1 * sky_v1_wide)])])
    proj_v1, totals = project_back(sky_v1, carried, 5)
    v2 = normal_action(v1, proj_v1)

    rr0, r0v1, v1v1 = totals[0], totals[1], totals[2]
    r0v2 = totals[3] - totals[5] / samples
    v1v2 = totals[4] - totals[6] / samples
    alpha0 = rr0 / r0v1
    rr1 = rr0 - 2.0 * alpha0 * r0v1 + alpha0 * alpha0 * v1v1
    beta0 = rr1 / rr0
    grow = 1.0 + beta0
    d1_ad1 = grow * grow * r0v1 - grow * alpha0 * r0v2 - alpha0 * grow * v1v1 + alpha0 * alpha0 * v1v2
    alpha1 = rr1 / d1_ad1
    d1 = grow * r0 - alpha0 * v1
    ad1 = grow * v1 - alpha0 * v2
    offset_levels = alpha0 * r0 + alpha1 * d1
    leftover_error = r0 - alpha0 * v1 - alpha1 * ad1
    return (offset_levels[None], leftover_error[None])


def solution(mesh):
    placed = (
        P(("det", "pix"), None, None),
        P(("det", "pix"), None, None, None),
        P(("det", "pix"), None, None),
        P(("det", "pix"), None),
        P(("det", "pix"), None),
    )
    return jax.shard_map(
        body,
        mesh=mesh,
        in_specs=placed,
        out_specs=(P(("det", "pix"), None), P(("det", "pix"), None)),
        check_vma=False,
    )
```

```python
import functools

import jax
import jax.numpy as jnp
from jax import lax
from jax.experimental import pallas as pl
from jax.experimental.pallas import tpu as pltpu
from jax.sharding import PartitionSpec as P

MESH = pl.DeviceIdType.MESH
PB_DEV = 64
NBASE_DEV = 128
HIGHEST = lax.Precision.HIGHEST


def _greet(peers, device_of):
    barrier = pltpu.get_barrier_semaphore()
    for peer in peers:
        pl.semaphore_signal(barrier, inc=1, device_id=device_of(peer), device_id_type=MESH)
    pl.semaphore_wait(barrier, len(peers))


def _det_sum_kernel(n, x_ref, o_ref, recv, send_sem, recv_sem, local_sem):
    me = lax.axis_index("det")
    pix = lax.axis_index("pix")
    device_of = lambda d: (d, pix)
    _greet([lax.rem(me + k, n) for k in range(1, n)], device_of)
    sends = []
    for k in range(1, n):
        peer = lax.rem(me + k, n)
        copy = pltpu.make_async_remote_copy(
            src_ref=x_ref, dst_ref=recv.at[me], send_sem=send_sem.at[k],
            recv_sem=recv_sem.at[me], device_id=device_of(peer), device_id_type=MESH)
        copy.start()
        sends.append(copy)
    local = pltpu.make_async_copy(x_ref, recv.at[me], local_sem)
    local.start()
    for copy in sends:
        copy.wait_send()
    for k in range(1, n):
        src = lax.rem(me + k, n)
        pltpu.make_async_remote_copy(
            src_ref=x_ref, dst_ref=recv.at[src], send_sem=send_sem.at[k],
            recv_sem=recv_sem.at[src], device_id=device_of(src), device_id_type=MESH).wait_recv()
    local.wait()
    acc = recv[0]
    for s in range(1, n):
        acc = acc + recv[s]
    o_ref[...] = acc


def det_sum(x, cid):
    n = lax.axis_size("det")
    return pl.pallas_call(
        functools.partial(_det_sum_kernel, n),
        out_shape=jax.ShapeDtypeStruct(x.shape, x.dtype),
        in_specs=[pl.BlockSpec(memory_space=pltpu.VMEM)],
        out_specs=pl.BlockSpec(memory_space=pltpu.VMEM),
        scratch_shapes=[
            pltpu.VMEM((n,) + x.shape, x.dtype),
            pltpu.SemaphoreType.DMA((n,)),
            pltpu.SemaphoreType.DMA((n,)),
            pltpu.SemaphoreType.DMA(()),
        ],
        compiler_params=pltpu.CompilerParams(collective_id=cid, has_side_effects=True),
    )(x)


def _pix_exchange_kernel(n, spread, *refs):
    count = len(spread)
    ins, outs = refs[:count], refs[count:2 * count]
    send_sem, recv_sem, local_sem = refs[2 * count:]
    me = lax.axis_index("pix")
    det = lax.axis_index("det")
    device_of = lambda j: (det, j)
    _greet([lax.rem(me + k, n) for k in range(1, n)], device_of)
    source = lambda a, j: ins[a].at[j] if spread[a] else ins[a]
    sends, locals_ = [], []
    for a in range(count):
        for k in range(1, n):
            peer = lax.rem(me + k, n)
            copy = pltpu.make_async_remote_copy(
                src_ref=source(a, peer), dst_ref=outs[a].at[me], send_sem=send_sem.at[a, k],
                recv_sem=recv_sem.at[a, me], device_id=device_of(peer), device_id_type=MESH)
            copy.start()
            sends.append(copy)
        local = pltpu.make_async_copy(source(a, me), outs[a].at[me], local_sem.at[a])
        local.start()
        locals_.append(local)
    for copy in sends:
        copy.wait_send()
    for a in range(count):
        for k in range(1, n):
            src = lax.rem(me + k, n)
            pltpu.make_async_remote_copy(
                src_ref=source(a, src), dst_ref=outs[a].at[src], send_sem=send_sem.at[a, k],
                recv_sem=recv_sem.at[a, src], device_id=device_of(src), device_id_type=MESH).wait_recv()
        locals_[a].wait()


def pix_exchange(arrays, spread, cid):
    n = lax.axis_size("pix")
    count = len(arrays)
    out_shape = [
        jax.ShapeDtypeStruct(x.shape if s else (n,) + x.shape, x.dtype) for x, s in zip(arrays, spread)
    ]
    return pl.pallas_call(
        functools.partial(_pix_exchange_kernel, n, tuple(spread)),
        out_shape=out_shape,
        in_specs=[pl.BlockSpec(memory_space=pltpu.VMEM)] * count,
        out_specs=[pl.BlockSpec(memory_space=pltpu.VMEM)] * count,
        scratch_shapes=[
            pltpu.SemaphoreType.DMA((count, n)),
            pltpu.SemaphoreType.DMA((count, n)),
            pltpu.SemaphoreType.DMA((count,)),
        ],
        compiler_params=pltpu.CompilerParams(collective_id=cid, has_side_effects=True),
    )(*arrays)


def _all_exchange_kernel(npix, n, spread, *refs):
    count = len(spread)
    ins, outs = refs[:count], refs[count:2 * count]
    send_sem, recv_sem, local_sem = refs[2 * count:]
    me = lax.axis_index("det") * npix + lax.axis_index("pix")
    device_of = lambda c: (lax.div(c, npix), lax.rem(c, npix))
    source = lambda a, c: ins[a].at[c] if spread[a] else ins[a]
    barrier = pltpu.get_barrier_semaphore()

    def greet(k, carry):
        peer = lax.rem(me + k, n)
        pl.semaphore_signal(barrier, inc=1, device_id=device_of(peer), device_id_type=MESH)
        return carry

    lax.fori_loop(1, n, greet, 0)
    pl.semaphore_wait(barrier, n - 1)

    def copy(a, k, c, slot):
        return pltpu.make_async_remote_copy(
            src_ref=source(a, c), dst_ref=outs[a].at[slot], send_sem=send_sem.at[a, k],
            recv_sem=recv_sem.at[a, slot], device_id=device_of(c), device_id_type=MESH)

    def send(k, carry):
        peer = lax.rem(me + k, n)
        for a in range(count):
            copy(a, k, peer, me).start()
        return carry

    lax.fori_loop(1, n, send, 0)
    locals_ = []
    for a in range(count):
        local = pltpu.make_async_copy(source(a, me), outs[a].at[me], local_sem.at[a])
        local.start()
        locals_.append(local)

    def finish(k, carry):
        peer = lax.rem(me + k, n)
        for a in range(count):
            copy(a, k, peer, me).wait_send()
            copy(a, k, peer, peer).wait_recv()
        return carry

    lax.fori_loop(1, n, finish, 0)
    for local in locals_:
        local.wait()


def all_exchange(arrays, spread, cid):
    npix = lax.axis_size("pix")
    n = lax.axis_size("det") * npix
    count = len(arrays)
    out_shape = [
        jax.ShapeDtypeStruct(x.shape if s else (n,) + x.shape, x.dtype) for x, s in zip(arrays, spread)
    ]
    return pl.pallas_call(
        functools.partial(_all_exchange_kernel, npix, n, tuple(spread)),
        out_shape=out_shape,
        in_specs=[pl.BlockSpec(memory_space=pltpu.VMEM)] * count,
        out_specs=[pl.BlockSpec(memory_space=pltpu.VMEM)] * count,
        scratch_shapes=[
            pltpu.SemaphoreType.DMA((count, n)),
            pltpu.SemaphoreType.DMA((count, n)),
            pltpu.SemaphoreType.DMA((count,)),
        ],
        compiler_params=pltpu.CompilerParams(collective_id=cid, has_side_effects=True),
    )(*arrays)


def _round_kernel(npix, n, k, scal, *refs):
    refs = list(refs)
    cells_in = refs.pop(0)
    hit_in = refs.pop(0) if k == 1 else None
    prev_in, local_in = (refs.pop(0), refs.pop(0)) if scal else (None, None)
    first_out, sky_all = refs.pop(0), refs.pop(0)
    scal_all = refs.pop(0) if scal else None
    recv, sky_cell = refs.pop(0), refs.pop(0)
    scal_cell = refs.pop(0) if scal else None
    send_sem, recv_sem, local_sem = refs
    me = lax.axis_index("det") * npix + lax.axis_index("pix")
    device_of = lambda c: (lax.div(c, npix), lax.rem(c, npix))
    barrier = pltpu.get_barrier_semaphore()

    def greet(j, carry):
        peer = lax.rem(me + j, n)
        pl.semaphore_signal(barrier, inc=1, device_id=device_of(peer), device_id_type=MESH)
        return carry

    lax.fori_loop(1, n, greet, 0)
    pl.semaphore_wait(barrier, n - 1)

    def exchange(a, src, dst, spread):
        def copy(j, c, slot):
            return pltpu.make_async_remote_copy(
                src_ref=src.at[c] if spread else src, dst_ref=dst.at[slot],
                send_sem=send_sem.at[a, j], recv_sem=recv_sem.at[a, slot],
                device_id=device_of(c), device_id_type=MESH)

        def send(j, carry):
            copy(j, lax.rem(me + j, n), me).start()
            return carry

        lax.fori_loop(1, n, send, 0)
        local = pltpu.make_async_copy(src.at[me] if spread else src, dst.at[me], local_sem.at[a])
        local.start()
        return copy, local

    def finish(copy, local):
        def wait(j, carry):
            peer = lax.rem(me + j, n)
            copy(j, peer, me).wait_send()
            copy(j, peer, peer).wait_recv()
            return carry

        lax.fori_loop(1, n, wait, 0)
        local.wait()

    finish(*exchange(0, cells_in, recv, True))
    rows = sky_cell.shape[0]
    acc = lax.fori_loop(
        0, n, lambda c, t: t + recv[c].astype(jnp.float32), jnp.zeros((k * rows, 128), jnp.float32))
    if k == 2:
        hit_plus = acc[:rows] + 1.0
        binned = acc[rows:]
        first_out[...] = hit_plus
    else:
        hit_plus = hit_in[...]
        binned = acc
        first_out[...] = binned
    sky = (binned / hit_plus).astype(sky_cell.dtype)
    sky_cell[...] = sky
    if scal:
        sky_wide = sky.astype(jnp.float32)
        lane = lax.broadcasted_iota(jnp.int32, (1, 128), 1)
        products = (jnp.where(lane == 5, jnp.sum(prev_in[...] * sky_wide), 0.0)
                    + jnp.where(lane == 6, jnp.sum(binned * sky_wide), 0.0))
        scal_cell[...] = local_in[...] + products
    pending = [exchange(1, sky_cell, sky_all, False)]
    if scal:
        pending.append(exchange(2, scal_cell, scal_all, False))
    for item in pending:
        finish(*item)


def fused_round(cells, k, hit_plus, prev, local, cid):
    npix = lax.axis_size("pix")
    n = lax.axis_size("det") * npix
    rows = cells.shape[1] // k
    scal = prev is not None
    args = [cells] + ([hit_plus] if k == 1 else []) + ([prev, local] if scal else [])
    out_shape = [jax.ShapeDtypeStruct((rows, 128), jnp.float32),
                 jax.ShapeDtypeStruct((n, rows, 128), jnp.bfloat16)]
    scratch = [pltpu.VMEM(cells.shape, cells.dtype), pltpu.VMEM((rows, 128), jnp.bfloat16)]
    if scal:
        out_shape.append(jax.ShapeDtypeStruct((n, 1, 128), jnp.float32))
        scratch.append(pltpu.VMEM((1, 128), jnp.float32))
    return pl.pallas_call(
        functools.partial(_round_kernel, npix, n, k, scal),
        out_shape=out_shape,
        in_specs=[pl.BlockSpec(memory_space=pltpu.VMEM)] * len(args),
        out_specs=[pl.BlockSpec(memory_space=pltpu.VMEM)] * len(out_shape),
        scratch_shapes=scratch + [
            pltpu.SemaphoreType.DMA((3, n)),
            pltpu.SemaphoreType.DMA((3, n)),
            pltpu.SemaphoreType.DMA((3,)),
        ],
        compiler_params=pltpu.CompilerParams(collective_id=cid, has_side_effects=True),
    )(*args)


def body(timestream, weights, block_owner, block_local, baseline_of):
    series_data = timestream[0]
    weight_rows = weights[0]
    owners = block_owner[0, :, 0]
    local_idx = block_local[0]
    segments_row = baseline_of[0]
    blocks, samples, pixels = weight_rows.shape
    pix_count = lax.axis_size("pix")
    devices = lax.axis_size("det") * pix_count
    sky_blocks_count = pix_count * PB_DEV
    cell = sky_blocks_count // devices
    cell_rows = cell * pixels // 128

    base_hot = (segments_row[:, None] == jnp.arange(NBASE_DEV)[None, :]).astype(jnp.float32)
    per_base = jnp.sum(base_hot, axis=0)
    weight_n = 1.0 + per_base
    block_pix = owners * PB_DEV + local_idx
    sky_hot = (block_pix[None, :] == jnp.arange(sky_blocks_count)[:, None]).astype(jnp.float32)
    sky_hot_t = (block_pix[:, None] == jnp.arange(sky_blocks_count)[None, :]).astype(jnp.bfloat16)

    unit_row_vector = jnp.ones((pixels,), jnp.bfloat16)
    row_sums = jnp.einsum(
        "bsp,p->bs", weight_rows, unit_row_vector, preferred_element_type=jnp.float32
    ).astype(jnp.bfloat16)
    stacked = jnp.stack(
        [row_sums, series_data.astype(jnp.bfloat16), jnp.ones_like(row_sums)]
    )
    first_terms = jnp.einsum(
        "kbs,bsp->kbp", stacked, weight_rows, preferred_element_type=jnp.float32
    )
    col_sums = first_terms[2]
    series_block_sums = jnp.sum(series_data, axis=1)

    def to_cells(terms):
        dense = jnp.einsum("qb,kbp->kqp", sky_hot, terms, precision=HIGHEST)
        k = terms.shape[0]
        dense = dense.reshape(k, devices, cell_rows, 128).transpose(1, 0, 2, 3)
        return dense.reshape(devices, k * cell_rows, 128).astype(jnp.bfloat16)

    def to_blocks(sky_cells):
        return jnp.dot(sky_hot_t, sky_cells.reshape(sky_blocks_count, pixels),
                       preferred_element_type=jnp.float32)

    def scalar_rows(values):
        row = jnp.zeros((1, 128), jnp.float32)
        return row.at[0, : values.shape[0]].set(values)

    def cell_sum(arrived, k):
        total = jnp.sum(arrived.astype(jnp.float32), axis=0)
        return total.reshape(k, cell, pixels)

    hit_plus, back1 = fused_round(to_cells(first_terms[:2]), 2, None, None, None, 0)
    projected0 = jnp.sum(col_sums * to_blocks(back1), axis=1)
    r0 = jnp.dot(series_block_sums - projected0, base_hot, precision=HIGHEST) / samples

    def normal_action(amps, projected_blocks):
        collapsed = jnp.dot(projected_blocks, base_hot, precision=HIGHEST)
        return amps * weight_n - collapsed / samples

    def cells_of(amps):
        per_block = jnp.dot(base_hot, amps, precision=HIGHEST)
        return to_cells((per_block[:, None] * col_sums)[None])

    binned_r0, sky_r0 = fused_round(cells_of(r0), 1, hit_plus, None, None, 1)
    v1 = normal_action(r0, jnp.sum(col_sums * to_blocks(sky_r0), axis=1))
    local = jnp.stack([
        jnp.sum(r0 * r0),
        jnp.sum(r0 * v1),
        jnp.sum(v1 * v1),
        jnp.sum(r0 * v1 * weight_n),
        jnp.sum(v1 * v1 * weight_n),
    ])
    _, sky_v1, carried = fused_round(cells_of(v1), 1, hit_plus, binned_r0, scalar_rows(local), 2)
    totals = jnp.sum(carried, axis=0)[0, :7]
    v2 = normal_action(v1, jnp.sum(col_sums * to_blocks(sky_v1), axis=1))

    rr0, r0v1, v1v1 = totals[0], totals[1], totals[2]
    r0v2 = totals[3] - totals[5] / samples
    v1v2 = totals[4] - totals[6] / samples
    alpha0 = rr0 / r0v1
    rr1 = rr0 - 2.0 * alpha0 * r0v1 + alpha0 * alpha0 * v1v1
    beta0 = rr1 / rr0
    grow = 1.0 + beta0
    d1_ad1 = grow * grow * r0v1 - grow * alpha0 * r0v2 - alpha0 * grow * v1v1 + alpha0 * alpha0 * v1v2
    alpha1 = rr1 / d1_ad1
    d1 = grow * r0 - alpha0 * v1
    ad1 = grow * v1 - alpha0 * v2
    offset_levels = alpha0 * r0 + alpha1 * d1
    leftover_error = r0 - alpha0 * v1 - alpha1 * ad1
    return (offset_levels[None], leftover_error[None])


def solution(mesh):
    placed = (
        P(("det", "pix"), None, None),
        P(("det", "pix"), None, None, None),
        P(("det", "pix"), None, None),
        P(("det", "pix"), None),
        P(("det", "pix"), None),
    )
    return jax.shard_map(
        body,
        mesh=mesh,
        in_specs=placed,
        out_specs=(P(("det", "pix"), None), P(("det", "pix"), None)),
        check_vma=False,
    )
```

```python
import functools

import jax
import jax.numpy as jnp
from jax import lax
from jax.experimental import pallas as pl
from jax.experimental.pallas import tpu as pltpu
from jax.sharding import PartitionSpec as P

MESH = pl.DeviceIdType.MESH
PB_DEV = 64
NBASE_DEV = 128
HIGHEST = lax.Precision.HIGHEST


def _greet(peers, device_of):
    barrier = pltpu.get_barrier_semaphore()
    for peer in peers:
        pl.semaphore_signal(barrier, inc=1, device_id=device_of(peer), device_id_type=MESH)
    pl.semaphore_wait(barrier, len(peers))


def _det_sum_kernel(n, x_ref, o_ref, recv, send_sem, recv_sem, local_sem):
    me = lax.axis_index("det")
    pix = lax.axis_index("pix")
    device_of = lambda d: (d, pix)
    _greet([lax.rem(me + k, n) for k in range(1, n)], device_of)
    sends = []
    for k in range(1, n):
        peer = lax.rem(me + k, n)
        copy = pltpu.make_async_remote_copy(
            src_ref=x_ref, dst_ref=recv.at[me], send_sem=send_sem.at[k],
            recv_sem=recv_sem.at[me], device_id=device_of(peer), device_id_type=MESH)
        copy.start()
        sends.append(copy)
    local = pltpu.make_async_copy(x_ref, recv.at[me], local_sem)
    local.start()
    for copy in sends:
        copy.wait_send()
    for k in range(1, n):
        src = lax.rem(me + k, n)
        pltpu.make_async_remote_copy(
            src_ref=x_ref, dst_ref=recv.at[src], send_sem=send_sem.at[k],
            recv_sem=recv_sem.at[src], device_id=device_of(src), device_id_type=MESH).wait_recv()
    local.wait()
    acc = recv[0]
    for s in range(1, n):
        acc = acc + recv[s]
    o_ref[...] = acc


def det_sum(x, cid):
    n = lax.axis_size("det")
    return pl.pallas_call(
        functools.partial(_det_sum_kernel, n),
        out_shape=jax.ShapeDtypeStruct(x.shape, x.dtype),
        in_specs=[pl.BlockSpec(memory_space=pltpu.VMEM)],
        out_specs=pl.BlockSpec(memory_space=pltpu.VMEM),
        scratch_shapes=[
            pltpu.VMEM((n,) + x.shape, x.dtype),
            pltpu.SemaphoreType.DMA((n,)),
            pltpu.SemaphoreType.DMA((n,)),
            pltpu.SemaphoreType.DMA(()),
        ],
        compiler_params=pltpu.CompilerParams(collective_id=cid, has_side_effects=True),
    )(x)


def _pix_exchange_kernel(n, spread, *refs):
    count = len(spread)
    ins, outs = refs[:count], refs[count:2 * count]
    send_sem, recv_sem, local_sem = refs[2 * count:]
    me = lax.axis_index("pix")
    det = lax.axis_index("det")
    device_of = lambda j: (det, j)
    _greet([lax.rem(me + k, n) for k in range(1, n)], device_of)
    source = lambda a, j: ins[a].at[j] if spread[a] else ins[a]
    sends, locals_ = [], []
    for a in range(count):
        for k in range(1, n):
            peer = lax.rem(me + k, n)
            copy = pltpu.make_async_remote_copy(
                src_ref=source(a, peer), dst_ref=outs[a].at[me], send_sem=send_sem.at[a, k],
                recv_sem=recv_sem.at[a, me], device_id=device_of(peer), device_id_type=MESH)
            copy.start()
            sends.append(copy)
        local = pltpu.make_async_copy(source(a, me), outs[a].at[me], local_sem.at[a])
        local.start()
        locals_.append(local)
    for copy in sends:
        copy.wait_send()
    for a in range(count):
        for k in range(1, n):
            src = lax.rem(me + k, n)
            pltpu.make_async_remote_copy(
                src_ref=source(a, src), dst_ref=outs[a].at[src], send_sem=send_sem.at[a, k],
                recv_sem=recv_sem.at[a, src], device_id=device_of(src), device_id_type=MESH).wait_recv()
        locals_[a].wait()


def pix_exchange(arrays, spread, cid):
    n = lax.axis_size("pix")
    count = len(arrays)
    out_shape = [
        jax.ShapeDtypeStruct(x.shape if s else (n,) + x.shape, x.dtype) for x, s in zip(arrays, spread)
    ]
    return pl.pallas_call(
        functools.partial(_pix_exchange_kernel, n, tuple(spread)),
        out_shape=out_shape,
        in_specs=[pl.BlockSpec(memory_space=pltpu.VMEM)] * count,
        out_specs=[pl.BlockSpec(memory_space=pltpu.VMEM)] * count,
        scratch_shapes=[
            pltpu.SemaphoreType.DMA((count, n)),
            pltpu.SemaphoreType.DMA((count, n)),
            pltpu.SemaphoreType.DMA((count,)),
        ],
        compiler_params=pltpu.CompilerParams(collective_id=cid, has_side_effects=True),
    )(*arrays)


def _all_exchange_kernel(npix, n, spread, *refs):
    count = len(spread)
    ins, outs = refs[:count], refs[count:2 * count]
    send_sem, recv_sem, local_sem = refs[2 * count:]
    me = lax.axis_index("det") * npix + lax.axis_index("pix")
    device_of = lambda c: (lax.div(c, npix), lax.rem(c, npix))
    source = lambda a, c: ins[a].at[c] if spread[a] else ins[a]
    barrier = pltpu.get_barrier_semaphore()

    def greet(k, carry):
        peer = lax.rem(me + k, n)
        pl.semaphore_signal(barrier, inc=1, device_id=device_of(peer), device_id_type=MESH)
        return carry

    lax.fori_loop(1, n, greet, 0)
    pl.semaphore_wait(barrier, n - 1)

    def copy(a, k, c, slot):
        return pltpu.make_async_remote_copy(
            src_ref=source(a, c), dst_ref=outs[a].at[slot], send_sem=send_sem.at[a, k],
            recv_sem=recv_sem.at[a, slot], device_id=device_of(c), device_id_type=MESH)

    def send(k, carry):
        peer = lax.rem(me + k, n)
        for a in range(count):
            copy(a, k, peer, me).start()
        return carry

    lax.fori_loop(1, n, send, 0)
    locals_ = []
    for a in range(count):
        local = pltpu.make_async_copy(source(a, me), outs[a].at[me], local_sem.at[a])
        local.start()
        locals_.append(local)

    def finish(k, carry):
        peer = lax.rem(me + k, n)
        for a in range(count):
            copy(a, k, peer, me).wait_send()
            copy(a, k, peer, peer).wait_recv()
        return carry

    lax.fori_loop(1, n, finish, 0)
    for local in locals_:
        local.wait()


def all_exchange(arrays, spread, cid):
    npix = lax.axis_size("pix")
    n = lax.axis_size("det") * npix
    count = len(arrays)
    out_shape = [
        jax.ShapeDtypeStruct(x.shape if s else (n,) + x.shape, x.dtype) for x, s in zip(arrays, spread)
    ]
    return pl.pallas_call(
        functools.partial(_all_exchange_kernel, npix, n, tuple(spread)),
        out_shape=out_shape,
        in_specs=[pl.BlockSpec(memory_space=pltpu.VMEM)] * count,
        out_specs=[pl.BlockSpec(memory_space=pltpu.VMEM)] * count,
        scratch_shapes=[
            pltpu.SemaphoreType.DMA((count, n)),
            pltpu.SemaphoreType.DMA((count, n)),
            pltpu.SemaphoreType.DMA((count,)),
        ],
        compiler_params=pltpu.CompilerParams(collective_id=cid, has_side_effects=True),
    )(*arrays)


def _round_kernel(npix, n, k, scal, *refs):
    refs = list(refs)
    cells_in = refs.pop(0)
    hit_in = refs.pop(0) if k == 1 else None
    prev_in, local_in = (refs.pop(0), refs.pop(0)) if scal else (None, None)
    first_out, sky_all = refs.pop(0), refs.pop(0)
    scal_all = refs.pop(0) if scal else None
    recv, sky_cell = refs.pop(0), refs.pop(0)
    scal_cell = refs.pop(0) if scal else None
    send_sem, recv_sem, local_sem = refs
    me = lax.axis_index("det") * npix + lax.axis_index("pix")
    device_of = lambda c: (lax.div(c, npix), lax.rem(c, npix))
    barrier = pltpu.get_barrier_semaphore()

    def greet(j, carry):
        peer = lax.rem(me + j, n)
        pl.semaphore_signal(barrier, inc=1, device_id=device_of(peer), device_id_type=MESH)
        return carry

    lax.fori_loop(1, n, greet, 0)
    pl.semaphore_wait(barrier, n - 1)

    def exchange(a, src, dst, spread):
        def copy(j, c, slot):
            return pltpu.make_async_remote_copy(
                src_ref=src.at[c] if spread else src, dst_ref=dst.at[slot],
                send_sem=send_sem.at[a, j], recv_sem=recv_sem.at[a, slot],
                device_id=device_of(c), device_id_type=MESH)

        def send(j, carry):
            copy(j, lax.rem(me + j, n), me).start()
            return carry

        lax.fori_loop(1, n, send, 0)
        local = pltpu.make_async_copy(src.at[me] if spread else src, dst.at[me], local_sem.at[a])
        local.start()
        return copy, local

    def finish(copy, local):
        def wait(j, carry):
            peer = lax.rem(me + j, n)
            copy(j, peer, me).wait_send()
            copy(j, peer, peer).wait_recv()
            return carry

        lax.fori_loop(1, n, wait, 0)
        local.wait()

    finish(*exchange(0, cells_in, recv, True))
    rows = sky_cell.shape[0]
    acc = lax.fori_loop(
        0, n, lambda c, t: t + recv[c].astype(jnp.float32), jnp.zeros((k * rows, 128), jnp.float32))
    if k == 2:
        hit_plus = acc[:rows] + 1.0
        binned = acc[rows:]
        first_out[...] = hit_plus
    else:
        hit_plus = hit_in[...]
        binned = acc
        first_out[...] = binned
    sky = (binned / hit_plus).astype(sky_cell.dtype)
    sky_cell[...] = sky
    if scal:
        sky_wide = sky.astype(jnp.float32)
        lane = lax.broadcasted_iota(jnp.int32, (1, 128), 1)
        products = (jnp.where(lane == 5, jnp.sum(prev_in[...] * sky_wide), 0.0)
                    + jnp.where(lane == 6, jnp.sum(binned * sky_wide), 0.0))
        scal_cell[...] = local_in[...] + products
    pending = [exchange(1, sky_cell, sky_all, False)]
    if scal:
        pending.append(exchange(2, scal_cell, scal_all, False))
    for item in pending:
        finish(*item)


def fused_round(cells, k, hit_plus, prev, local, cid):
    npix = lax.axis_size("pix")
    n = lax.axis_size("det") * npix
    rows = cells.shape[1] // k
    scal = prev is not None
    args = [cells] + ([hit_plus] if k == 1 else []) + ([prev, local] if scal else [])
    out_shape = [jax.ShapeDtypeStruct((rows, 128), jnp.float32),
                 jax.ShapeDtypeStruct((n, rows, 128), jnp.bfloat16)]
    scratch = [pltpu.VMEM(cells.shape, cells.dtype), pltpu.VMEM((rows, 128), jnp.bfloat16)]
    if scal:
        out_shape.append(jax.ShapeDtypeStruct((n, 1, 128), jnp.float32))
        scratch.append(pltpu.VMEM((1, 128), jnp.float32))
    return pl.pallas_call(
        functools.partial(_round_kernel, npix, n, k, scal),
        out_shape=out_shape,
        in_specs=[pl.BlockSpec(memory_space=pltpu.VMEM)] * len(args),
        out_specs=[pl.BlockSpec(memory_space=pltpu.VMEM)] * len(out_shape),
        scratch_shapes=scratch + [
            pltpu.SemaphoreType.DMA((3, n)),
            pltpu.SemaphoreType.DMA((3, n)),
            pltpu.SemaphoreType.DMA((3,)),
        ],
        compiler_params=pltpu.CompilerParams(collective_id=cid, has_side_effects=True),
    )(*args)


def body(timestream, weights, block_owner, block_local, baseline_of):
    series_data = timestream[0]
    weight_rows = weights[0]
    owners = block_owner[0, :, 0]
    local_idx = block_local[0]
    segments_row = baseline_of[0]
    blocks, samples, pixels = weight_rows.shape
    pix_count = lax.axis_size("pix")
    devices = lax.axis_size("det") * pix_count
    sky_blocks_count = pix_count * PB_DEV
    cell = sky_blocks_count // devices
    cell_rows = cell * pixels // 128

    base_hot = (segments_row[:, None] == jnp.arange(NBASE_DEV)[None, :]).astype(jnp.float32)
    per_base = jnp.sum(base_hot, axis=0)
    weight_n = 1.0 + per_base
    block_pix = owners * PB_DEV + local_idx
    half = pixels // 128
    sky_rows = sky_blocks_count * half
    block_half = (block_pix[:, None] * half + jnp.arange(half)[None, :]).reshape(-1)
    sky_hot = (block_half[None, :] == jnp.arange(sky_rows)[:, None]).astype(jnp.float32)
    sky_hot_t = (block_half[:, None] == jnp.arange(sky_rows)[None, :]).astype(jnp.bfloat16)
    base_hot_h = jnp.repeat(base_hot, half, axis=0)

    unit_row_vector = jnp.ones((pixels,), jnp.bfloat16)
    row_sums = jnp.einsum(
        "bsp,p->bs", weight_rows, unit_row_vector, preferred_element_type=jnp.float32
    ).astype(jnp.bfloat16)
    stacked = jnp.stack(
        [row_sums, series_data.astype(jnp.bfloat16), jnp.ones_like(row_sums)]
    )
    first_terms = jnp.einsum(
        "kbs,bsp->kbp", stacked, weight_rows, preferred_element_type=jnp.float32
    ).reshape(3, blocks * half, 128)
    col_h = first_terms[2]
    series_base_sums = jnp.dot(jnp.sum(series_data, axis=1), base_hot, precision=HIGHEST)

    def to_cells(terms):
        dense = jnp.einsum("qb,kbp->kqp", sky_hot, terms, precision=HIGHEST)
        k = terms.shape[0]
        dense = dense.reshape(k, devices, cell_rows, 128).transpose(1, 0, 2, 3)
        return dense.reshape(devices, k * cell_rows, 128).astype(jnp.bfloat16)

    def projected(sky_cells):
        per_row = jnp.dot(sky_hot_t, sky_cells.reshape(sky_rows, 128),
                          preferred_element_type=jnp.float32)
        return jnp.sum(col_h * per_row, axis=1)

    def collapse(values):
        return jnp.dot(values, base_hot_h, precision=HIGHEST)

    hit_plus, back1 = fused_round(to_cells(first_terms[:2]), 2, None, None, None, 0)
    r0 = (series_base_sums - collapse(projected(back1))) / samples

    def normal_action(amps, sky_cells):
        return amps * weight_n - collapse(projected(sky_cells)) / samples

    def cells_of(amps):
        per_row = jnp.dot(base_hot_h, amps, precision=HIGHEST)
        return to_cells((per_row[:, None] * col_h)[None])

    binned_r0, sky_r0 = fused_round(cells_of(r0), 1, hit_plus, None, None, 1)
    v1 = normal_action(r0, sky_r0)
    left = jnp.stack([r0, r0, v1, r0 * weight_n, v1 * weight_n])
    right = jnp.stack([r0, v1, v1, v1, v1])
    partials = jnp.sum(left * right, axis=1)
    local = jnp.pad(partials, (0, 128 - partials.shape[0])).reshape(1, 128)
    _, sky_v1, carried = fused_round(cells_of(v1), 1, hit_plus, binned_r0, local, 2)
    totals = jnp.sum(carried, axis=0)[0, :7]
    v2 = normal_action(v1, sky_v1)

    rr0, r0v1, v1v1 = totals[0], totals[1], totals[2]
    r0v2 = totals[3] - totals[5] / samples
    v1v2 = totals[4] - totals[6] / samples
    alpha0 = rr0 / r0v1
    rr1 = rr0 - 2.0 * alpha0 * r0v1 + alpha0 * alpha0 * v1v1
    beta0 = rr1 / rr0
    grow = 1.0 + beta0
    d1_ad1 = grow * grow * r0v1 - grow * alpha0 * r0v2 - alpha0 * grow * v1v1 + alpha0 * alpha0 * v1v2
    alpha1 = rr1 / d1_ad1
    d1 = grow * r0 - alpha0 * v1
    ad1 = grow * v1 - alpha0 * v2
    offset_levels = alpha0 * r0 + alpha1 * d1
    leftover_error = r0 - alpha0 * v1 - alpha1 * ad1
    return (offset_levels[None], leftover_error[None])


def solution(mesh):
    placed = (
        P(("det", "pix"), None, None),
        P(("det", "pix"), None, None, None),
        P(("det", "pix"), None, None),
        P(("det", "pix"), None),
        P(("det", "pix"), None),
    )
    return jax.shard_map(
        body,
        mesh=mesh,
        in_specs=placed,
        out_specs=(P(("det", "pix"), None), P(("det", "pix"), None)),
        check_vma=False,
    )
```

```python
import functools

import jax
import jax.numpy as jnp
from jax import lax
from jax.experimental import pallas as pl
from jax.experimental.pallas import tpu as pltpu
from jax.sharding import PartitionSpec as P

MESH = pl.DeviceIdType.MESH
PB_DEV = 64
NBASE_DEV = 128
HIGHEST = lax.Precision.HIGHEST


def _greet(peers, device_of):
    barrier = pltpu.get_barrier_semaphore()
    for peer in peers:
        pl.semaphore_signal(barrier, inc=1, device_id=device_of(peer), device_id_type=MESH)
    pl.semaphore_wait(barrier, len(peers))


def _det_sum_kernel(n, x_ref, o_ref, recv, send_sem, recv_sem, local_sem):
    me = lax.axis_index("det")
    pix = lax.axis_index("pix")
    device_of = lambda d: (d, pix)
    _greet([lax.rem(me + k, n) for k in range(1, n)], device_of)
    sends = []
    for k in range(1, n):
        peer = lax.rem(me + k, n)
        copy = pltpu.make_async_remote_copy(
            src_ref=x_ref, dst_ref=recv.at[me], send_sem=send_sem.at[k],
            recv_sem=recv_sem.at[me], device_id=device_of(peer), device_id_type=MESH)
        copy.start()
        sends.append(copy)
    local = pltpu.make_async_copy(x_ref, recv.at[me], local_sem)
    local.start()
    for copy in sends:
        copy.wait_send()
    for k in range(1, n):
        src = lax.rem(me + k, n)
        pltpu.make_async_remote_copy(
            src_ref=x_ref, dst_ref=recv.at[src], send_sem=send_sem.at[k],
            recv_sem=recv_sem.at[src], device_id=device_of(src), device_id_type=MESH).wait_recv()
    local.wait()
    acc = recv[0]
    for s in range(1, n):
        acc = acc + recv[s]
    o_ref[...] = acc


def det_sum(x, cid):
    n = lax.axis_size("det")
    return pl.pallas_call(
        functools.partial(_det_sum_kernel, n),
        out_shape=jax.ShapeDtypeStruct(x.shape, x.dtype),
        in_specs=[pl.BlockSpec(memory_space=pltpu.VMEM)],
        out_specs=pl.BlockSpec(memory_space=pltpu.VMEM),
        scratch_shapes=[
            pltpu.VMEM((n,) + x.shape, x.dtype),
            pltpu.SemaphoreType.DMA((n,)),
            pltpu.SemaphoreType.DMA((n,)),
            pltpu.SemaphoreType.DMA(()),
        ],
        compiler_params=pltpu.CompilerParams(collective_id=cid, has_side_effects=True),
    )(x)


def _pix_exchange_kernel(n, spread, *refs):
    count = len(spread)
    ins, outs = refs[:count], refs[count:2 * count]
    send_sem, recv_sem, local_sem = refs[2 * count:]
    me = lax.axis_index("pix")
    det = lax.axis_index("det")
    device_of = lambda j: (det, j)
    _greet([lax.rem(me + k, n) for k in range(1, n)], device_of)
    source = lambda a, j: ins[a].at[j] if spread[a] else ins[a]
    sends, locals_ = [], []
    for a in range(count):
        for k in range(1, n):
            peer = lax.rem(me + k, n)
            copy = pltpu.make_async_remote_copy(
                src_ref=source(a, peer), dst_ref=outs[a].at[me], send_sem=send_sem.at[a, k],
                recv_sem=recv_sem.at[a, me], device_id=device_of(peer), device_id_type=MESH)
            copy.start()
            sends.append(copy)
        local = pltpu.make_async_copy(source(a, me), outs[a].at[me], local_sem.at[a])
        local.start()
        locals_.append(local)
    for copy in sends:
        copy.wait_send()
    for a in range(count):
        for k in range(1, n):
            src = lax.rem(me + k, n)
            pltpu.make_async_remote_copy(
                src_ref=source(a, src), dst_ref=outs[a].at[src], send_sem=send_sem.at[a, k],
                recv_sem=recv_sem.at[a, src], device_id=device_of(src), device_id_type=MESH).wait_recv()
        locals_[a].wait()


def pix_exchange(arrays, spread, cid):
    n = lax.axis_size("pix")
    count = len(arrays)
    out_shape = [
        jax.ShapeDtypeStruct(x.shape if s else (n,) + x.shape, x.dtype) for x, s in zip(arrays, spread)
    ]
    return pl.pallas_call(
        functools.partial(_pix_exchange_kernel, n, tuple(spread)),
        out_shape=out_shape,
        in_specs=[pl.BlockSpec(memory_space=pltpu.VMEM)] * count,
        out_specs=[pl.BlockSpec(memory_space=pltpu.VMEM)] * count,
        scratch_shapes=[
            pltpu.SemaphoreType.DMA((count, n)),
            pltpu.SemaphoreType.DMA((count, n)),
            pltpu.SemaphoreType.DMA((count,)),
        ],
        compiler_params=pltpu.CompilerParams(collective_id=cid, has_side_effects=True),
    )(*arrays)


def _all_exchange_kernel(npix, n, spread, *refs):
    count = len(spread)
    ins, outs = refs[:count], refs[count:2 * count]
    send_sem, recv_sem, local_sem = refs[2 * count:]
    me = lax.axis_index("det") * npix + lax.axis_index("pix")
    device_of = lambda c: (lax.div(c, npix), lax.rem(c, npix))
    source = lambda a, c: ins[a].at[c] if spread[a] else ins[a]
    barrier = pltpu.get_barrier_semaphore()

    def greet(k, carry):
        peer = lax.rem(me + k, n)
        pl.semaphore_signal(barrier, inc=1, device_id=device_of(peer), device_id_type=MESH)
        return carry

    lax.fori_loop(1, n, greet, 0)
    pl.semaphore_wait(barrier, n - 1)

    def copy(a, k, c, slot):
        return pltpu.make_async_remote_copy(
            src_ref=source(a, c), dst_ref=outs[a].at[slot], send_sem=send_sem.at[a, k],
            recv_sem=recv_sem.at[a, slot], device_id=device_of(c), device_id_type=MESH)

    def send(k, carry):
        peer = lax.rem(me + k, n)
        for a in range(count):
            copy(a, k, peer, me).start()
        return carry

    lax.fori_loop(1, n, send, 0)
    locals_ = []
    for a in range(count):
        local = pltpu.make_async_copy(source(a, me), outs[a].at[me], local_sem.at[a])
        local.start()
        locals_.append(local)

    def finish(k, carry):
        peer = lax.rem(me + k, n)
        for a in range(count):
            copy(a, k, peer, me).wait_send()
            copy(a, k, peer, peer).wait_recv()
        return carry

    lax.fori_loop(1, n, finish, 0)
    for local in locals_:
        local.wait()


def all_exchange(arrays, spread, cid):
    npix = lax.axis_size("pix")
    n = lax.axis_size("det") * npix
    count = len(arrays)
    out_shape = [
        jax.ShapeDtypeStruct(x.shape if s else (n,) + x.shape, x.dtype) for x, s in zip(arrays, spread)
    ]
    return pl.pallas_call(
        functools.partial(_all_exchange_kernel, npix, n, tuple(spread)),
        out_shape=out_shape,
        in_specs=[pl.BlockSpec(memory_space=pltpu.VMEM)] * count,
        out_specs=[pl.BlockSpec(memory_space=pltpu.VMEM)] * count,
        scratch_shapes=[
            pltpu.SemaphoreType.DMA((count, n)),
            pltpu.SemaphoreType.DMA((count, n)),
            pltpu.SemaphoreType.DMA((count,)),
        ],
        compiler_params=pltpu.CompilerParams(collective_id=cid, has_side_effects=True),
    )(*arrays)


def _round_kernel(npix, n, k, scal, *refs):
    refs = list(refs)
    cells_in = refs.pop(0)
    hit_in = refs.pop(0) if k == 1 else None
    prev_in, local_in = (refs.pop(0), refs.pop(0)) if scal else (None, None)
    first_out, sky_all = refs.pop(0), refs.pop(0)
    scal_all = refs.pop(0) if scal else None
    recv, sky_cell = refs.pop(0), refs.pop(0)
    scal_cell = refs.pop(0) if scal else None
    send_sem, recv_sem, local_sem = refs
    me = lax.axis_index("det") * npix + lax.axis_index("pix")
    device_of = lambda c: (lax.div(c, npix), lax.rem(c, npix))
    barrier = pltpu.get_barrier_semaphore()

    def greet(j, carry):
        peer = lax.rem(me + j, n)
        pl.semaphore_signal(barrier, inc=1, device_id=device_of(peer), device_id_type=MESH)
        return carry

    lax.fori_loop(1, n, greet, 0)
    pl.semaphore_wait(barrier, n - 1)

    def exchange(a, src, dst, spread):
        def copy(j, c, slot):
            return pltpu.make_async_remote_copy(
                src_ref=src.at[c] if spread else src, dst_ref=dst.at[slot],
                send_sem=send_sem.at[a, j], recv_sem=recv_sem.at[a, slot],
                device_id=device_of(c), device_id_type=MESH)

        def send(j, carry):
            copy(j, lax.rem(me + j, n), me).start()
            return carry

        lax.fori_loop(1, n, send, 0)
        local = pltpu.make_async_copy(src.at[me] if spread else src, dst.at[me], local_sem.at[a])
        local.start()
        return copy, local

    def finish(copy, local):
        def wait(j, carry):
            peer = lax.rem(me + j, n)
            copy(j, peer, me).wait_send()
            copy(j, peer, peer).wait_recv()
            return carry

        lax.fori_loop(1, n, wait, 0)
        local.wait()

    finish(*exchange(0, cells_in, recv, True))
    rows = sky_cell.shape[0]
    acc = lax.fori_loop(
        0, n, lambda c, t: t + recv[c].astype(jnp.float32), jnp.zeros((k * rows, 128), jnp.float32))
    if k == 2:
        hit_plus = acc[:rows] + 1.0
        binned = acc[rows:]
        first_out[...] = hit_plus
    else:
        hit_plus = hit_in[...]
        binned = acc
        first_out[...] = binned
    sky = (binned / hit_plus).astype(sky_cell.dtype)
    sky_cell[...] = sky
    if scal:
        sky_wide = sky.astype(jnp.float32)
        lane = lax.broadcasted_iota(jnp.int32, (1, 128), 1)
        products = (jnp.where(lane == 5, jnp.sum(prev_in[...] * sky_wide), 0.0)
                    + jnp.where(lane == 6, jnp.sum(binned * sky_wide), 0.0))
        scal_cell[...] = local_in[...] + products
    pending = [exchange(1, sky_cell, sky_all, False)]
    if scal:
        pending.append(exchange(2, scal_cell, scal_all, False))
    for item in pending:
        finish(*item)


def fused_round(cells, k, hit_plus, prev, local, cid):
    npix = lax.axis_size("pix")
    n = lax.axis_size("det") * npix
    rows = cells.shape[1] // k
    scal = prev is not None
    args = [cells] + ([hit_plus] if k == 1 else []) + ([prev, local] if scal else [])
    out_shape = [jax.ShapeDtypeStruct((rows, 128), jnp.float32),
                 jax.ShapeDtypeStruct((n, rows, 128), jnp.bfloat16)]
    scratch = [pltpu.VMEM(cells.shape, cells.dtype), pltpu.VMEM((rows, 128), jnp.bfloat16)]
    if scal:
        out_shape.append(jax.ShapeDtypeStruct((n, 1, 128), jnp.float32))
        scratch.append(pltpu.VMEM((1, 128), jnp.float32))
    return pl.pallas_call(
        functools.partial(_round_kernel, npix, n, k, scal),
        out_shape=out_shape,
        in_specs=[pl.BlockSpec(memory_space=pltpu.VMEM)] * len(args),
        out_specs=[pl.BlockSpec(memory_space=pltpu.VMEM)] * len(out_shape),
        scratch_shapes=scratch + [
            pltpu.SemaphoreType.DMA((3, n)),
            pltpu.SemaphoreType.DMA((3, n)),
            pltpu.SemaphoreType.DMA((3,)),
        ],
        compiler_params=pltpu.CompilerParams(collective_id=cid, has_side_effects=True),
    )(*args)


def body(timestream, weights, block_owner, block_local, baseline_of):
    series_data = timestream[0]
    weight_rows = weights[0]
    owners = block_owner[0, :, 0]
    local_idx = block_local[0]
    segments_row = baseline_of[0]
    blocks, samples, pixels = weight_rows.shape
    pix_count = lax.axis_size("pix")
    devices = lax.axis_size("det") * pix_count
    sky_blocks_count = pix_count * PB_DEV
    cell = sky_blocks_count // devices
    cell_rows = cell * pixels // 128

    base_hot = (segments_row[:, None] == jnp.arange(NBASE_DEV)[None, :]).astype(jnp.float32)
    per_base = jnp.sum(base_hot, axis=0)
    weight_n = 1.0 + per_base
    block_pix = owners * PB_DEV + local_idx
    sky_hot = (block_pix[None, :] == jnp.arange(sky_blocks_count)[:, None]).astype(jnp.float32)
    sky_hot_t = (block_pix[:, None] == jnp.arange(sky_blocks_count)[None, :]).astype(jnp.bfloat16)

    unit_row_vector = jnp.ones((pixels,), jnp.bfloat16)
    row_sums = jnp.einsum(
        "bsp,p->bs", weight_rows, unit_row_vector, preferred_element_type=jnp.float32
    ).astype(jnp.bfloat16)
    stacked = jnp.stack(
        [row_sums, series_data.astype(jnp.bfloat16), jnp.ones_like(row_sums)]
    )
    first_terms = jnp.einsum(
        "kbs,bsp->kbp", stacked, weight_rows, preferred_element_type=jnp.float32
    )
    col_sums = first_terms[2]
    series_block_sums = jnp.sum(series_data, axis=1)

    def to_cells(terms):
        dense = jnp.einsum("qb,kbp->kqp", sky_hot.astype(jnp.bfloat16), terms.astype(jnp.bfloat16),
                           preferred_element_type=jnp.float32)
        k = terms.shape[0]
        dense = dense.reshape(k, devices, cell_rows, 128).transpose(1, 0, 2, 3)
        return dense.reshape(devices, k * cell_rows, 128).astype(jnp.bfloat16)

    def to_blocks(sky_cells):
        return jnp.dot(sky_hot_t, sky_cells.reshape(sky_blocks_count, pixels),
                       preferred_element_type=jnp.float32)

    def scalar_rows(values):
        row = jnp.zeros((1, 128), jnp.float32)
        return row.at[0, : values.shape[0]].set(values)

    def cell_sum(arrived, k):
        total = jnp.sum(arrived.astype(jnp.float32), axis=0)
        return total.reshape(k, cell, pixels)

    hit_plus, back1 = fused_round(to_cells(first_terms[:2]), 2, None, None, None, 0)
    projected0 = jnp.sum(col_sums * to_blocks(back1), axis=1)
    r0 = jnp.dot(series_block_sums - projected0, base_hot, precision=HIGHEST) / samples

    def normal_action(amps, projected_blocks):
        collapsed = jnp.dot(projected_blocks, base_hot, precision=HIGHEST)
        return amps * weight_n - collapsed / samples

    def cells_of(amps):
        per_block = jnp.dot(base_hot, amps, precision=HIGHEST)
        return to_cells((per_block[:, None] * col_sums)[None])

    binned_r0, sky_r0 = fused_round(cells_of(r0), 1, hit_plus, None, None, 1)
    v1 = normal_action(r0, jnp.sum(col_sums * to_blocks(sky_r0), axis=1))
    left = jnp.stack([r0, r0, v1, r0 * weight_n, v1 * weight_n])
    right = jnp.stack([r0, v1, v1, v1, v1])
    partials = jnp.sum(left * right, axis=1)
    local = jnp.pad(partials, (0, 128 - partials.shape[0])).reshape(1, 128)
    _, sky_v1, carried = fused_round(cells_of(v1), 1, hit_plus, binned_r0, local, 2)
    totals = jnp.sum(carried, axis=0)[0, :7]
    v2 = normal_action(v1, jnp.sum(col_sums * to_blocks(sky_v1), axis=1))

    rr0, r0v1, v1v1 = totals[0], totals[1], totals[2]
    r0v2 = totals[3] - totals[5] / samples
    v1v2 = totals[4] - totals[6] / samples
    alpha0 = rr0 / r0v1
    rr1 = rr0 - 2.0 * alpha0 * r0v1 + alpha0 * alpha0 * v1v1
    beta0 = rr1 / rr0
    grow = 1.0 + beta0
    d1_ad1 = grow * grow * r0v1 - grow * alpha0 * r0v2 - alpha0 * grow * v1v1 + alpha0 * alpha0 * v1v2
    alpha1 = rr1 / d1_ad1
    d1 = grow * r0 - alpha0 * v1
    ad1 = grow * v1 - alpha0 * v2
    offset_levels = alpha0 * r0 + alpha1 * d1
    leftover_error = r0 - alpha0 * v1 - alpha1 * ad1
    return (offset_levels[None], leftover_error[None])


def solution(mesh):
    placed = (
        P(("det", "pix"), None, None),
        P(("det", "pix"), None, None, None),
        P(("det", "pix"), None, None),
        P(("det", "pix"), None),
        P(("det", "pix"), None),
    )
    return jax.shard_map(
        body,
        mesh=mesh,
        in_specs=placed,
        out_specs=(P(("det", "pix"), None), P(("det", "pix"), None)),
        check_vma=False,
    )
```

```python
import functools

import jax
import jax.numpy as jnp
from jax import lax
from jax.experimental import pallas as pl
from jax.experimental.pallas import tpu as pltpu
from jax.sharding import PartitionSpec as P

MESH = pl.DeviceIdType.MESH
PB_DEV = 64
NBASE_DEV = 128
HIGHEST = lax.Precision.HIGHEST


def _greet(peers, device_of):
    barrier = pltpu.get_barrier_semaphore()
    for peer in peers:
        pl.semaphore_signal(barrier, inc=1, device_id=device_of(peer), device_id_type=MESH)
    pl.semaphore_wait(barrier, len(peers))


def _det_sum_kernel(n, x_ref, o_ref, recv, send_sem, recv_sem, local_sem):
    me = lax.axis_index("det")
    pix = lax.axis_index("pix")
    device_of = lambda d: (d, pix)
    _greet([lax.rem(me + k, n) for k in range(1, n)], device_of)
    sends = []
    for k in range(1, n):
        peer = lax.rem(me + k, n)
        copy = pltpu.make_async_remote_copy(
            src_ref=x_ref, dst_ref=recv.at[me], send_sem=send_sem.at[k],
            recv_sem=recv_sem.at[me], device_id=device_of(peer), device_id_type=MESH)
        copy.start()
        sends.append(copy)
    local = pltpu.make_async_copy(x_ref, recv.at[me], local_sem)
    local.start()
    for copy in sends:
        copy.wait_send()
    for k in range(1, n):
        src = lax.rem(me + k, n)
        pltpu.make_async_remote_copy(
            src_ref=x_ref, dst_ref=recv.at[src], send_sem=send_sem.at[k],
            recv_sem=recv_sem.at[src], device_id=device_of(src), device_id_type=MESH).wait_recv()
    local.wait()
    acc = recv[0]
    for s in range(1, n):
        acc = acc + recv[s]
    o_ref[...] = acc


def det_sum(x, cid):
    n = lax.axis_size("det")
    return pl.pallas_call(
        functools.partial(_det_sum_kernel, n),
        out_shape=jax.ShapeDtypeStruct(x.shape, x.dtype),
        in_specs=[pl.BlockSpec(memory_space=pltpu.VMEM)],
        out_specs=pl.BlockSpec(memory_space=pltpu.VMEM),
        scratch_shapes=[
            pltpu.VMEM((n,) + x.shape, x.dtype),
            pltpu.SemaphoreType.DMA((n,)),
            pltpu.SemaphoreType.DMA((n,)),
            pltpu.SemaphoreType.DMA(()),
        ],
        compiler_params=pltpu.CompilerParams(collective_id=cid, has_side_effects=True),
    )(x)


def _pix_exchange_kernel(n, spread, *refs):
    count = len(spread)
    ins, outs = refs[:count], refs[count:2 * count]
    send_sem, recv_sem, local_sem = refs[2 * count:]
    me = lax.axis_index("pix")
    det = lax.axis_index("det")
    device_of = lambda j: (det, j)
    _greet([lax.rem(me + k, n) for k in range(1, n)], device_of)
    source = lambda a, j: ins[a].at[j] if spread[a] else ins[a]
    sends, locals_ = [], []
    for a in range(count):
        for k in range(1, n):
            peer = lax.rem(me + k, n)
            copy = pltpu.make_async_remote_copy(
                src_ref=source(a, peer), dst_ref=outs[a].at[me], send_sem=send_sem.at[a, k],
                recv_sem=recv_sem.at[a, me], device_id=device_of(peer), device_id_type=MESH)
            copy.start()
            sends.append(copy)
        local = pltpu.make_async_copy(source(a, me), outs[a].at[me], local_sem.at[a])
        local.start()
        locals_.append(local)
    for copy in sends:
        copy.wait_send()
    for a in range(count):
        for k in range(1, n):
            src = lax.rem(me + k, n)
            pltpu.make_async_remote_copy(
                src_ref=source(a, src), dst_ref=outs[a].at[src], send_sem=send_sem.at[a, k],
                recv_sem=recv_sem.at[a, src], device_id=device_of(src), device_id_type=MESH).wait_recv()
        locals_[a].wait()


def pix_exchange(arrays, spread, cid):
    n = lax.axis_size("pix")
    count = len(arrays)
    out_shape = [
        jax.ShapeDtypeStruct(x.shape if s else (n,) + x.shape, x.dtype) for x, s in zip(arrays, spread)
    ]
    return pl.pallas_call(
        functools.partial(_pix_exchange_kernel, n, tuple(spread)),
        out_shape=out_shape,
        in_specs=[pl.BlockSpec(memory_space=pltpu.VMEM)] * count,
        out_specs=[pl.BlockSpec(memory_space=pltpu.VMEM)] * count,
        scratch_shapes=[
            pltpu.SemaphoreType.DMA((count, n)),
            pltpu.SemaphoreType.DMA((count, n)),
            pltpu.SemaphoreType.DMA((count,)),
        ],
        compiler_params=pltpu.CompilerParams(collective_id=cid, has_side_effects=True),
    )(*arrays)


def _all_exchange_kernel(npix, n, spread, *refs):
    count = len(spread)
    ins, outs = refs[:count], refs[count:2 * count]
    send_sem, recv_sem, local_sem = refs[2 * count:]
    me = lax.axis_index("det") * npix + lax.axis_index("pix")
    device_of = lambda c: (lax.div(c, npix), lax.rem(c, npix))
    source = lambda a, c: ins[a].at[c] if spread[a] else ins[a]
    barrier = pltpu.get_barrier_semaphore()

    def greet(k, carry):
        peer = lax.rem(me + k, n)
        pl.semaphore_signal(barrier, inc=1, device_id=device_of(peer), device_id_type=MESH)
        return carry

    lax.fori_loop(1, n, greet, 0)
    pl.semaphore_wait(barrier, n - 1)

    def copy(a, k, c, slot):
        return pltpu.make_async_remote_copy(
            src_ref=source(a, c), dst_ref=outs[a].at[slot], send_sem=send_sem.at[a, k],
            recv_sem=recv_sem.at[a, slot], device_id=device_of(c), device_id_type=MESH)

    def send(k, carry):
        peer = lax.rem(me + k, n)
        for a in range(count):
            copy(a, k, peer, me).start()
        return carry

    lax.fori_loop(1, n, send, 0)
    locals_ = []
    for a in range(count):
        local = pltpu.make_async_copy(source(a, me), outs[a].at[me], local_sem.at[a])
        local.start()
        locals_.append(local)

    def finish(k, carry):
        peer = lax.rem(me + k, n)
        for a in range(count):
            copy(a, k, peer, me).wait_send()
            copy(a, k, peer, peer).wait_recv()
        return carry

    lax.fori_loop(1, n, finish, 0)
    for local in locals_:
        local.wait()


def all_exchange(arrays, spread, cid):
    npix = lax.axis_size("pix")
    n = lax.axis_size("det") * npix
    count = len(arrays)
    out_shape = [
        jax.ShapeDtypeStruct(x.shape if s else (n,) + x.shape, x.dtype) for x, s in zip(arrays, spread)
    ]
    return pl.pallas_call(
        functools.partial(_all_exchange_kernel, npix, n, tuple(spread)),
        out_shape=out_shape,
        in_specs=[pl.BlockSpec(memory_space=pltpu.VMEM)] * count,
        out_specs=[pl.BlockSpec(memory_space=pltpu.VMEM)] * count,
        scratch_shapes=[
            pltpu.SemaphoreType.DMA((count, n)),
            pltpu.SemaphoreType.DMA((count, n)),
            pltpu.SemaphoreType.DMA((count,)),
        ],
        compiler_params=pltpu.CompilerParams(collective_id=cid, has_side_effects=True),
    )(*arrays)


def _round_kernel(npix, n, k, scal, *refs):
    refs = list(refs)
    cells_in = refs.pop(0)
    hit_in = refs.pop(0) if k == 1 else None
    prev_in, local_in = (refs.pop(0), refs.pop(0)) if scal else (None, None)
    first_out, sky_all = refs.pop(0), refs.pop(0)
    scal_all = refs.pop(0) if scal else None
    recv, sky_cell = refs.pop(0), refs.pop(0)
    scal_cell = refs.pop(0) if scal else None
    send_sem, recv_sem, local_sem = refs
    me = lax.axis_index("det") * npix + lax.axis_index("pix")
    device_of = lambda c: (lax.div(c, npix), lax.rem(c, npix))
    barrier = pltpu.get_barrier_semaphore()

    def greet(j, carry):
        peer = lax.rem(me + j, n)
        pl.semaphore_signal(barrier, inc=1, device_id=device_of(peer), device_id_type=MESH)
        return carry

    lax.fori_loop(1, n, greet, 0)
    pl.semaphore_wait(barrier, n - 1)

    def exchange(a, src, dst, spread):
        def copy(j, c, slot):
            return pltpu.make_async_remote_copy(
                src_ref=src.at[c] if spread else src, dst_ref=dst.at[slot],
                send_sem=send_sem.at[a, j], recv_sem=recv_sem.at[a, slot],
                device_id=device_of(c), device_id_type=MESH)

        def send(j, carry):
            copy(j, lax.rem(me + j, n), me).start()
            return carry

        lax.fori_loop(1, n, send, 0)
        local = pltpu.make_async_copy(src.at[me] if spread else src, dst.at[me], local_sem.at[a])
        local.start()
        return copy, local

    def finish(copy, local):
        def wait(j, carry):
            peer = lax.rem(me + j, n)
            copy(j, peer, me).wait_send()
            copy(j, peer, peer).wait_recv()
            return carry

        lax.fori_loop(1, n, wait, 0)
        local.wait()

    finish(*exchange(0, cells_in, recv, True))
    rows = sky_cell.shape[0]
    acc = lax.fori_loop(
        0, n, lambda c, t: t + recv[c].astype(jnp.float32), jnp.zeros((k * rows, 128), jnp.float32))
    if k == 2:
        hit_plus = acc[:rows] + 1.0
        binned = acc[rows:]
        first_out[...] = hit_plus
    else:
        hit_plus = hit_in[...]
        binned = acc
        first_out[...] = binned
    sky = (binned / hit_plus).astype(sky_cell.dtype)
    sky_cell[...] = sky
    if scal:
        sky_wide = sky.astype(jnp.float32)
        lane = lax.broadcasted_iota(jnp.int32, (1, 128), 1)
        products = (jnp.where(lane == 5, jnp.sum(prev_in[...] * sky_wide), 0.0)
                    + jnp.where(lane == 6, jnp.sum(binned * sky_wide), 0.0))
        scal_cell[...] = local_in[...] + products
    pending = [exchange(1, sky_cell, sky_all, False)]
    if scal:
        pending.append(exchange(2, scal_cell, scal_all, False))
    for item in pending:
        finish(*item)


def fused_round(cells, k, hit_plus, prev, local, cid):
    npix = lax.axis_size("pix")
    n = lax.axis_size("det") * npix
    rows = cells.shape[1] // k
    scal = prev is not None
    args = [cells] + ([hit_plus] if k == 1 else []) + ([prev, local] if scal else [])
    out_shape = [jax.ShapeDtypeStruct((rows, 128), jnp.float32),
                 jax.ShapeDtypeStruct((n, rows, 128), jnp.bfloat16)]
    scratch = [pltpu.VMEM(cells.shape, cells.dtype), pltpu.VMEM((rows, 128), jnp.bfloat16)]
    if scal:
        out_shape.append(jax.ShapeDtypeStruct((n, 1, 128), jnp.float32))
        scratch.append(pltpu.VMEM((1, 128), jnp.float32))
    return pl.pallas_call(
        functools.partial(_round_kernel, npix, n, k, scal),
        out_shape=out_shape,
        in_specs=[pl.BlockSpec(memory_space=pltpu.VMEM)] * len(args),
        out_specs=[pl.BlockSpec(memory_space=pltpu.VMEM)] * len(out_shape),
        scratch_shapes=scratch + [
            pltpu.SemaphoreType.DMA((3, n)),
            pltpu.SemaphoreType.DMA((3, n)),
            pltpu.SemaphoreType.DMA((3,)),
        ],
        compiler_params=pltpu.CompilerParams(collective_id=cid, has_side_effects=True),
    )(*args)


def body(timestream, weights, block_owner, block_local, baseline_of):
    series_data = timestream[0]
    weight_rows = weights[0]
    owners = block_owner[0, :, 0]
    local_idx = block_local[0]
    segments_row = baseline_of[0]
    blocks, samples, pixels = weight_rows.shape
    pix_count = lax.axis_size("pix")
    devices = lax.axis_size("det") * pix_count
    sky_blocks_count = pix_count * PB_DEV
    cell = sky_blocks_count // devices
    cell_rows = cell * pixels // 128

    base_hot = (segments_row[:, None] == jnp.arange(NBASE_DEV)[None, :]).astype(jnp.float32)
    per_base = jnp.sum(base_hot, axis=0)
    weight_n = 1.0 + per_base
    block_pix = owners * PB_DEV + local_idx
    sky_hot = (block_pix[None, :] == jnp.arange(sky_blocks_count)[:, None]).astype(jnp.float32)
    sky_hot_t = (block_pix[:, None] == jnp.arange(sky_blocks_count)[None, :]).astype(jnp.bfloat16)

    unit_row_vector = jnp.ones((pixels,), jnp.bfloat16)
    row_sums = jnp.einsum(
        "bsp,p->bs", weight_rows, unit_row_vector, preferred_element_type=jnp.float32
    ).astype(jnp.bfloat16)
    stacked = jnp.stack(
        [row_sums, series_data.astype(jnp.bfloat16), jnp.ones_like(row_sums)]
    )
    first_terms = jnp.einsum(
        "kbs,bsp->kbp", stacked, weight_rows, preferred_element_type=jnp.float32
    )
    col_sums = first_terms[2]
    series_block_sums = jnp.sum(series_data, axis=1)

    def to_cells(terms):
        dense = jnp.einsum("qb,kbp->kqp", sky_hot.astype(jnp.bfloat16), terms.astype(jnp.bfloat16),
                           preferred_element_type=jnp.float32)
        k = terms.shape[0]
        dense = dense.reshape(k, devices, cell_rows, 128).transpose(1, 0, 2, 3)
        return dense.reshape(devices, k * cell_rows, 128).astype(jnp.bfloat16)

    def to_blocks(sky_cells):
        return jnp.dot(sky_hot_t, sky_cells.reshape(sky_blocks_count, pixels),
                       preferred_element_type=jnp.float32)

    def scalar_rows(values):
        row = jnp.zeros((1, 128), jnp.float32)
        return row.at[0, : values.shape[0]].set(values)

    def cell_sum(arrived, k):
        total = jnp.sum(arrived.astype(jnp.float32), axis=0)
        return total.reshape(k, cell, pixels)

    hit_plus, back1 = fused_round(to_cells(first_terms[:2]), 2, None, None, None, 0)
    projected0 = jnp.sum(col_sums * to_blocks(back1), axis=1)
    r0 = jnp.dot(series_block_sums - projected0, base_hot, precision=HIGHEST) / samples

    def normal_action(amps, projected_blocks):
        collapsed = jnp.dot(projected_blocks, base_hot, precision=HIGHEST)
        return amps * weight_n - collapsed / samples

    def cells_of(amps):
        per_block = jnp.dot(base_hot, amps, precision=HIGHEST)
        return to_cells((per_block[:, None] * col_sums)[None])

    binned_r0, sky_r0 = fused_round(cells_of(r0), 1, hit_plus, None, None, 1)
    v1 = normal_action(r0, jnp.sum(col_sums * to_blocks(sky_r0), axis=1))
    left = jnp.stack([r0, r0, v1, r0 * weight_n, v1 * weight_n])
    right = jnp.stack([r0, v1, v1, v1, v1])
    partials = jnp.sum(left * right, axis=1)
    local = jnp.pad(partials, (0, 128 - partials.shape[0])).reshape(1, 128)
    _, sky_v1, carried = fused_round(cells_of(v1), 1, hit_plus, binned_r0, local, 2)
    total_row = jnp.sum(carried, axis=0)
    picks = (jnp.arange(128)[:, None] == (jnp.arange(7 * NBASE_DEV) // NBASE_DEV)[None, :])
    rows = jnp.dot(total_row, picks.astype(jnp.float32), precision=HIGHEST).reshape(7, NBASE_DEV)
    v2 = normal_action(v1, jnp.sum(col_sums * to_blocks(sky_v1), axis=1))

    rr0, r0v1, v1v1 = rows[0], rows[1], rows[2]
    r0v2 = rows[3] - rows[5] / samples
    v1v2 = rows[4] - rows[6] / samples
    alpha0 = rr0 / r0v1
    rr1 = rr0 - 2.0 * alpha0 * r0v1 + alpha0 * alpha0 * v1v1
    beta0 = rr1 / rr0
    grow = 1.0 + beta0
    d1_ad1 = grow * grow * r0v1 - grow * alpha0 * r0v2 - alpha0 * grow * v1v1 + alpha0 * alpha0 * v1v2
    alpha1 = rr1 / d1_ad1
    d1 = grow * r0 - alpha0 * v1
    ad1 = grow * v1 - alpha0 * v2
    offset_levels = alpha0 * r0 + alpha1 * d1
    leftover_error = r0 - alpha0 * v1 - alpha1 * ad1
    return (offset_levels[None], leftover_error[None])


def solution(mesh):
    placed = (
        P(("det", "pix"), None, None),
        P(("det", "pix"), None, None, None),
        P(("det", "pix"), None, None),
        P(("det", "pix"), None),
        P(("det", "pix"), None),
    )
    return jax.shard_map(
        body,
        mesh=mesh,
        in_specs=placed,
        out_specs=(P(("det", "pix"), None), P(("det", "pix"), None)),
        check_vma=False,
    )
```

```python
import functools

import jax
import jax.numpy as jnp
from jax import lax
from jax.experimental import pallas as pl
from jax.experimental.pallas import tpu as pltpu
from jax.sharding import PartitionSpec as P

MESH = pl.DeviceIdType.MESH
PB_DEV = 64
NBASE_DEV = 128
HIGHEST = lax.Precision.HIGHEST


def _greet(peers, device_of):
    barrier = pltpu.get_barrier_semaphore()
    for peer in peers:
        pl.semaphore_signal(barrier, inc=1, device_id=device_of(peer), device_id_type=MESH)
    pl.semaphore_wait(barrier, len(peers))


def _det_sum_kernel(n, x_ref, o_ref, recv, send_sem, recv_sem, local_sem):
    me = lax.axis_index("det")
    pix = lax.axis_index("pix")
    device_of = lambda d: (d, pix)
    _greet([lax.rem(me + k, n) for k in range(1, n)], device_of)
    sends = []
    for k in range(1, n):
        peer = lax.rem(me + k, n)
        copy = pltpu.make_async_remote_copy(
            src_ref=x_ref, dst_ref=recv.at[me], send_sem=send_sem.at[k],
            recv_sem=recv_sem.at[me], device_id=device_of(peer), device_id_type=MESH)
        copy.start()
        sends.append(copy)
    local = pltpu.make_async_copy(x_ref, recv.at[me], local_sem)
    local.start()
    for copy in sends:
        copy.wait_send()
    for k in range(1, n):
        src = lax.rem(me + k, n)
        pltpu.make_async_remote_copy(
            src_ref=x_ref, dst_ref=recv.at[src], send_sem=send_sem.at[k],
            recv_sem=recv_sem.at[src], device_id=device_of(src), device_id_type=MESH).wait_recv()
    local.wait()
    acc = recv[0]
    for s in range(1, n):
        acc = acc + recv[s]
    o_ref[...] = acc


def det_sum(x, cid):
    n = lax.axis_size("det")
    return pl.pallas_call(
        functools.partial(_det_sum_kernel, n),
        out_shape=jax.ShapeDtypeStruct(x.shape, x.dtype),
        in_specs=[pl.BlockSpec(memory_space=pltpu.VMEM)],
        out_specs=pl.BlockSpec(memory_space=pltpu.VMEM),
        scratch_shapes=[
            pltpu.VMEM((n,) + x.shape, x.dtype),
            pltpu.SemaphoreType.DMA((n,)),
            pltpu.SemaphoreType.DMA((n,)),
            pltpu.SemaphoreType.DMA(()),
        ],
        compiler_params=pltpu.CompilerParams(collective_id=cid, has_side_effects=True),
    )(x)


def _pix_exchange_kernel(n, spread, *refs):
    count = len(spread)
    ins, outs = refs[:count], refs[count:2 * count]
    send_sem, recv_sem, local_sem = refs[2 * count:]
    me = lax.axis_index("pix")
    det = lax.axis_index("det")
    device_of = lambda j: (det, j)
    _greet([lax.rem(me + k, n) for k in range(1, n)], device_of)
    source = lambda a, j: ins[a].at[j] if spread[a] else ins[a]
    sends, locals_ = [], []
    for a in range(count):
        for k in range(1, n):
            peer = lax.rem(me + k, n)
            copy = pltpu.make_async_remote_copy(
                src_ref=source(a, peer), dst_ref=outs[a].at[me], send_sem=send_sem.at[a, k],
                recv_sem=recv_sem.at[a, me], device_id=device_of(peer), device_id_type=MESH)
            copy.start()
            sends.append(copy)
        local = pltpu.make_async_copy(source(a, me), outs[a].at[me], local_sem.at[a])
        local.start()
        locals_.append(local)
    for copy in sends:
        copy.wait_send()
    for a in range(count):
        for k in range(1, n):
            src = lax.rem(me + k, n)
            pltpu.make_async_remote_copy(
                src_ref=source(a, src), dst_ref=outs[a].at[src], send_sem=send_sem.at[a, k],
                recv_sem=recv_sem.at[a, src], device_id=device_of(src), device_id_type=MESH).wait_recv()
        locals_[a].wait()


def pix_exchange(arrays, spread, cid):
    n = lax.axis_size("pix")
    count = len(arrays)
    out_shape = [
        jax.ShapeDtypeStruct(x.shape if s else (n,) + x.shape, x.dtype) for x, s in zip(arrays, spread)
    ]
    return pl.pallas_call(
        functools.partial(_pix_exchange_kernel, n, tuple(spread)),
        out_shape=out_shape,
        in_specs=[pl.BlockSpec(memory_space=pltpu.VMEM)] * count,
        out_specs=[pl.BlockSpec(memory_space=pltpu.VMEM)] * count,
        scratch_shapes=[
            pltpu.SemaphoreType.DMA((count, n)),
            pltpu.SemaphoreType.DMA((count, n)),
            pltpu.SemaphoreType.DMA((count,)),
        ],
        compiler_params=pltpu.CompilerParams(collective_id=cid, has_side_effects=True),
    )(*arrays)


def _all_exchange_kernel(npix, n, spread, *refs):
    count = len(spread)
    ins, outs = refs[:count], refs[count:2 * count]
    send_sem, recv_sem, local_sem = refs[2 * count:]
    me = lax.axis_index("det") * npix + lax.axis_index("pix")
    device_of = lambda c: (lax.div(c, npix), lax.rem(c, npix))
    source = lambda a, c: ins[a].at[c] if spread[a] else ins[a]
    barrier = pltpu.get_barrier_semaphore()

    def greet(k, carry):
        peer = lax.rem(me + k, n)
        pl.semaphore_signal(barrier, inc=1, device_id=device_of(peer), device_id_type=MESH)
        return carry

    lax.fori_loop(1, n, greet, 0)
    pl.semaphore_wait(barrier, n - 1)

    def copy(a, k, c, slot):
        return pltpu.make_async_remote_copy(
            src_ref=source(a, c), dst_ref=outs[a].at[slot], send_sem=send_sem.at[a, k],
            recv_sem=recv_sem.at[a, slot], device_id=device_of(c), device_id_type=MESH)

    def send(k, carry):
        peer = lax.rem(me + k, n)
        for a in range(count):
            copy(a, k, peer, me).start()
        return carry

    lax.fori_loop(1, n, send, 0)
    locals_ = []
    for a in range(count):
        local = pltpu.make_async_copy(source(a, me), outs[a].at[me], local_sem.at[a])
        local.start()
        locals_.append(local)

    def finish(k, carry):
        peer = lax.rem(me + k, n)
        for a in range(count):
            copy(a, k, peer, me).wait_send()
            copy(a, k, peer, peer).wait_recv()
        return carry

    lax.fori_loop(1, n, finish, 0)
    for local in locals_:
        local.wait()


def all_exchange(arrays, spread, cid):
    npix = lax.axis_size("pix")
    n = lax.axis_size("det") * npix
    count = len(arrays)
    out_shape = [
        jax.ShapeDtypeStruct(x.shape if s else (n,) + x.shape, x.dtype) for x, s in zip(arrays, spread)
    ]
    return pl.pallas_call(
        functools.partial(_all_exchange_kernel, npix, n, tuple(spread)),
        out_shape=out_shape,
        in_specs=[pl.BlockSpec(memory_space=pltpu.VMEM)] * count,
        out_specs=[pl.BlockSpec(memory_space=pltpu.VMEM)] * count,
        scratch_shapes=[
            pltpu.SemaphoreType.DMA((count, n)),
            pltpu.SemaphoreType.DMA((count, n)),
            pltpu.SemaphoreType.DMA((count,)),
        ],
        compiler_params=pltpu.CompilerParams(collective_id=cid, has_side_effects=True),
    )(*arrays)


def _round_kernel(npix, n, k, scal, *refs):
    refs = list(refs)
    cells_in = refs.pop(0)
    hit_in = refs.pop(0) if k == 1 else None
    prev_in, local_in = (refs.pop(0), refs.pop(0)) if scal else (None, None)
    first_out, sky_all = refs.pop(0), refs.pop(0)
    scal_all = refs.pop(0) if scal else None
    recv, sky_cell = refs.pop(0), refs.pop(0)
    scal_cell = refs.pop(0) if scal else None
    send_sem, recv_sem, local_sem = refs
    me = lax.axis_index("det") * npix + lax.axis_index("pix")
    device_of = lambda c: (lax.div(c, npix), lax.rem(c, npix))
    barrier = pltpu.get_barrier_semaphore()

    def greet(j, carry):
        peer = lax.rem(me + j, n)
        pl.semaphore_signal(barrier, inc=1, device_id=device_of(peer), device_id_type=MESH)
        return carry

    lax.fori_loop(1, n, greet, 0)
    pl.semaphore_wait(barrier, n - 1)

    def exchange(a, src, dst, spread):
        def copy(j, c, slot):
            return pltpu.make_async_remote_copy(
                src_ref=src.at[c] if spread else src, dst_ref=dst.at[slot],
                send_sem=send_sem.at[a, j], recv_sem=recv_sem.at[a, slot],
                device_id=device_of(c), device_id_type=MESH)

        def send(j, carry):
            copy(j, lax.rem(me + j, n), me).start()
            return carry

        lax.fori_loop(1, n, send, 0)
        local = pltpu.make_async_copy(src.at[me] if spread else src, dst.at[me], local_sem.at[a])
        local.start()
        return copy, local

    def finish(copy, local):
        def wait(j, carry):
            peer = lax.rem(me + j, n)
            copy(j, peer, me).wait_send()
            copy(j, peer, peer).wait_recv()
            return carry

        lax.fori_loop(1, n, wait, 0)
        local.wait()

    finish(*exchange(0, cells_in, recv, True))
    rows = sky_cell.shape[0]
    acc = lax.fori_loop(
        0, n, lambda c, t: t + recv[c].astype(jnp.float32), jnp.zeros((k * rows, 128), jnp.float32))
    if k == 2:
        hit_plus = acc[:rows] + 1.0
        binned = acc[rows:]
        first_out[...] = hit_plus
    else:
        hit_plus = hit_in[...]
        binned = acc
        first_out[...] = binned
    sky = (binned / hit_plus).astype(sky_cell.dtype)
    sky_cell[...] = sky
    if scal:
        sky_wide = sky.astype(jnp.float32)
        lane = lax.broadcasted_iota(jnp.int32, (1, 128), 1)
        products = (jnp.where(lane == 5, jnp.sum(prev_in[...] * sky_wide), 0.0)
                    + jnp.where(lane == 6, jnp.sum(binned * sky_wide), 0.0))
        scal_cell[...] = local_in[...] + products
    pending = [exchange(1, sky_cell, sky_all, False)]
    if scal:
        pending.append(exchange(2, scal_cell, scal_all, False))
    for item in pending:
        finish(*item)


def fused_round(cells, k, hit_plus, prev, local, cid):
    npix = lax.axis_size("pix")
    n = lax.axis_size("det") * npix
    rows = cells.shape[1] // k
    scal = prev is not None
    args = [cells] + ([hit_plus] if k == 1 else []) + ([prev, local] if scal else [])
    out_shape = [jax.ShapeDtypeStruct((rows, 128), jnp.float32),
                 jax.ShapeDtypeStruct((n, rows, 128), jnp.bfloat16)]
    scratch = [pltpu.VMEM(cells.shape, cells.dtype), pltpu.VMEM((rows, 128), jnp.bfloat16)]
    if scal:
        out_shape.append(jax.ShapeDtypeStruct((n, 1, 128), jnp.float32))
        scratch.append(pltpu.VMEM((1, 128), jnp.float32))
    return pl.pallas_call(
        functools.partial(_round_kernel, npix, n, k, scal),
        out_shape=out_shape,
        in_specs=[pl.BlockSpec(memory_space=pltpu.VMEM)] * len(args),
        out_specs=[pl.BlockSpec(memory_space=pltpu.VMEM)] * len(out_shape),
        scratch_shapes=scratch + [
            pltpu.SemaphoreType.DMA((3, n)),
            pltpu.SemaphoreType.DMA((3, n)),
            pltpu.SemaphoreType.DMA((3,)),
        ],
        compiler_params=pltpu.CompilerParams(collective_id=cid, has_side_effects=True),
    )(*args)


def body(timestream, weights, block_owner, block_local, baseline_of):
    series_data = timestream[0]
    weight_rows = weights[0]
    owners = block_owner[0, :, 0]
    local_idx = block_local[0]
    segments_row = baseline_of[0]
    blocks, samples, pixels = weight_rows.shape
    pix_count = lax.axis_size("pix")
    devices = lax.axis_size("det") * pix_count
    sky_blocks_count = pix_count * PB_DEV
    cell = sky_blocks_count // devices
    cell_rows = cell * pixels // 128

    base_hot = (segments_row[:, None] == jnp.arange(NBASE_DEV)[None, :]).astype(jnp.float32)
    per_base = jnp.sum(base_hot, axis=0)
    weight_n = 1.0 + per_base
    block_pix = owners * PB_DEV + local_idx
    sky_hot = (block_pix[None, :] == jnp.arange(sky_blocks_count)[:, None]).astype(jnp.float32)
    sky_hot_t = (block_pix[:, None] == jnp.arange(sky_blocks_count)[None, :]).astype(jnp.bfloat16)

    unit_rows = jnp.ones((8, pixels), jnp.bfloat16)
    row_sums = jnp.einsum(
        "kp,bsp->kbs", unit_rows, weight_rows, preferred_element_type=jnp.float32
    )[0].astype(jnp.bfloat16)
    stacked = jnp.stack(
        [row_sums, series_data.astype(jnp.bfloat16), jnp.ones_like(row_sums)]
    )
    first_terms = jnp.einsum(
        "kbs,bsp->kbp", stacked, weight_rows, preferred_element_type=jnp.float32
    )
    col_sums = first_terms[2]
    series_block_sums = jnp.sum(series_data, axis=1)

    def to_cells(terms):
        dense = jnp.einsum("qb,kbp->kqp", sky_hot.astype(jnp.bfloat16), terms.astype(jnp.bfloat16),
                           preferred_element_type=jnp.float32)
        k = terms.shape[0]
        dense = dense.reshape(k, devices, cell_rows, 128).transpose(1, 0, 2, 3)
        return dense.reshape(devices, k * cell_rows, 128).astype(jnp.bfloat16)

    def to_blocks(sky_cells):
        return jnp.dot(sky_hot_t, sky_cells.reshape(sky_blocks_count, pixels),
                       preferred_element_type=jnp.float32)

    def scalar_rows(values):
        row = jnp.zeros((1, 128), jnp.float32)
        return row.at[0, : values.shape[0]].set(values)

    def cell_sum(arrived, k):
        total = jnp.sum(arrived.astype(jnp.float32), axis=0)
        return total.reshape(k, cell, pixels)

    hit_plus, back1 = fused_round(to_cells(first_terms[:2]), 2, None, None, None, 0)
    projected0 = jnp.sum(col_sums * to_blocks(back1), axis=1)
    r0 = jnp.dot(series_block_sums - projected0, base_hot, precision=HIGHEST) / samples

    def normal_action(amps, projected_blocks):
        collapsed = jnp.dot(projected_blocks, base_hot, precision=HIGHEST)
        return amps * weight_n - collapsed / samples

    def cells_of(amps):
        per_block = jnp.dot(base_hot, amps, precision=HIGHEST)
        return to_cells((per_block[:, None] * col_sums)[None])

    binned_r0, sky_r0 = fused_round(cells_of(r0), 1, hit_plus, None, None, 1)
    v1 = normal_action(r0, jnp.sum(col_sums * to_blocks(sky_r0), axis=1))
    left = jnp.stack([r0, r0, v1, r0 * weight_n, v1 * weight_n])
    right = jnp.stack([r0, v1, v1, v1, v1])
    partials = jnp.sum(left * right, axis=1)
    local = jnp.pad(partials, (0, 128 - partials.shape[0])).reshape(1, 128)
    _, sky_v1, carried = fused_round(cells_of(v1), 1, hit_plus, binned_r0, local, 2)
    total_row = jnp.sum(carried, axis=0)
    picks = (jnp.arange(128)[:, None] == (jnp.arange(7 * NBASE_DEV) // NBASE_DEV)[None, :])
    rows = jnp.dot(total_row, picks.astype(jnp.float32), precision=HIGHEST).reshape(7, NBASE_DEV)
    v2 = normal_action(v1, jnp.sum(col_sums * to_blocks(sky_v1), axis=1))

    rr0, r0v1, v1v1 = rows[0], rows[1], rows[2]
    r0v2 = rows[3] - rows[5] / samples
    v1v2 = rows[4] - rows[6] / samples
    alpha0 = rr0 / r0v1
    rr1 = rr0 - 2.0 * alpha0 * r0v1 + alpha0 * alpha0 * v1v1
    beta0 = rr1 / rr0
    grow = 1.0 + beta0
    d1_ad1 = grow * grow * r0v1 - grow * alpha0 * r0v2 - alpha0 * grow * v1v1 + alpha0 * alpha0 * v1v2
    alpha1 = rr1 / d1_ad1
    d1 = grow * r0 - alpha0 * v1
    ad1 = grow * v1 - alpha0 * v2
    offset_levels = alpha0 * r0 + alpha1 * d1
    leftover_error = r0 - alpha0 * v1 - alpha1 * ad1
    return (offset_levels[None], leftover_error[None])


def solution(mesh):
    placed = (
        P(("det", "pix"), None, None),
        P(("det", "pix"), None, None, None),
        P(("det", "pix"), None, None),
        P(("det", "pix"), None),
        P(("det", "pix"), None),
    )
    return jax.shard_map(
        body,
        mesh=mesh,
        in_specs=placed,
        out_specs=(P(("det", "pix"), None), P(("det", "pix"), None)),
        check_vma=False,
    )
```

```python
import functools

import jax
import jax.numpy as jnp
from jax import lax
from jax.experimental import pallas as pl
from jax.experimental.pallas import tpu as pltpu
from jax.sharding import PartitionSpec as P

MESH = pl.DeviceIdType.MESH
PB_DEV = 64
NBASE_DEV = 128
HIGHEST = lax.Precision.HIGHEST


def _greet(peers, device_of):
    barrier = pltpu.get_barrier_semaphore()
    for peer in peers:
        pl.semaphore_signal(barrier, inc=1, device_id=device_of(peer), device_id_type=MESH)
    pl.semaphore_wait(barrier, len(peers))


def _det_sum_kernel(n, x_ref, o_ref, recv, send_sem, recv_sem, local_sem):
    me = lax.axis_index("det")
    pix = lax.axis_index("pix")
    device_of = lambda d: (d, pix)
    _greet([lax.rem(me + k, n) for k in range(1, n)], device_of)
    sends = []
    for k in range(1, n):
        peer = lax.rem(me + k, n)
        copy = pltpu.make_async_remote_copy(
            src_ref=x_ref, dst_ref=recv.at[me], send_sem=send_sem.at[k],
            recv_sem=recv_sem.at[me], device_id=device_of(peer), device_id_type=MESH)
        copy.start()
        sends.append(copy)
    local = pltpu.make_async_copy(x_ref, recv.at[me], local_sem)
    local.start()
    for copy in sends:
        copy.wait_send()
    for k in range(1, n):
        src = lax.rem(me + k, n)
        pltpu.make_async_remote_copy(
            src_ref=x_ref, dst_ref=recv.at[src], send_sem=send_sem.at[k],
            recv_sem=recv_sem.at[src], device_id=device_of(src), device_id_type=MESH).wait_recv()
    local.wait()
    acc = recv[0]
    for s in range(1, n):
        acc = acc + recv[s]
    o_ref[...] = acc


def det_sum(x, cid):
    n = lax.axis_size("det")
    return pl.pallas_call(
        functools.partial(_det_sum_kernel, n),
        out_shape=jax.ShapeDtypeStruct(x.shape, x.dtype),
        in_specs=[pl.BlockSpec(memory_space=pltpu.VMEM)],
        out_specs=pl.BlockSpec(memory_space=pltpu.VMEM),
        scratch_shapes=[
            pltpu.VMEM((n,) + x.shape, x.dtype),
            pltpu.SemaphoreType.DMA((n,)),
            pltpu.SemaphoreType.DMA((n,)),
            pltpu.SemaphoreType.DMA(()),
        ],
        compiler_params=pltpu.CompilerParams(collective_id=cid, has_side_effects=True),
    )(x)


def _pix_exchange_kernel(n, spread, *refs):
    count = len(spread)
    ins, outs = refs[:count], refs[count:2 * count]
    send_sem, recv_sem, local_sem = refs[2 * count:]
    me = lax.axis_index("pix")
    det = lax.axis_index("det")
    device_of = lambda j: (det, j)
    _greet([lax.rem(me + k, n) for k in range(1, n)], device_of)
    source = lambda a, j: ins[a].at[j] if spread[a] else ins[a]
    sends, locals_ = [], []
    for a in range(count):
        for k in range(1, n):
            peer = lax.rem(me + k, n)
            copy = pltpu.make_async_remote_copy(
                src_ref=source(a, peer), dst_ref=outs[a].at[me], send_sem=send_sem.at[a, k],
                recv_sem=recv_sem.at[a, me], device_id=device_of(peer), device_id_type=MESH)
            copy.start()
            sends.append(copy)
        local = pltpu.make_async_copy(source(a, me), outs[a].at[me], local_sem.at[a])
        local.start()
        locals_.append(local)
    for copy in sends:
        copy.wait_send()
    for a in range(count):
        for k in range(1, n):
            src = lax.rem(me + k, n)
            pltpu.make_async_remote_copy(
                src_ref=source(a, src), dst_ref=outs[a].at[src], send_sem=send_sem.at[a, k],
                recv_sem=recv_sem.at[a, src], device_id=device_of(src), device_id_type=MESH).wait_recv()
        locals_[a].wait()


def pix_exchange(arrays, spread, cid):
    n = lax.axis_size("pix")
    count = len(arrays)
    out_shape = [
        jax.ShapeDtypeStruct(x.shape if s else (n,) + x.shape, x.dtype) for x, s in zip(arrays, spread)
    ]
    return pl.pallas_call(
        functools.partial(_pix_exchange_kernel, n, tuple(spread)),
        out_shape=out_shape,
        in_specs=[pl.BlockSpec(memory_space=pltpu.VMEM)] * count,
        out_specs=[pl.BlockSpec(memory_space=pltpu.VMEM)] * count,
        scratch_shapes=[
            pltpu.SemaphoreType.DMA((count, n)),
            pltpu.SemaphoreType.DMA((count, n)),
            pltpu.SemaphoreType.DMA((count,)),
        ],
        compiler_params=pltpu.CompilerParams(collective_id=cid, has_side_effects=True),
    )(*arrays)


def _all_exchange_kernel(npix, n, spread, *refs):
    count = len(spread)
    ins, outs = refs[:count], refs[count:2 * count]
    send_sem, recv_sem, local_sem = refs[2 * count:]
    me = lax.axis_index("det") * npix + lax.axis_index("pix")
    device_of = lambda c: (lax.div(c, npix), lax.rem(c, npix))
    source = lambda a, c: ins[a].at[c] if spread[a] else ins[a]
    barrier = pltpu.get_barrier_semaphore()

    def greet(k, carry):
        peer = lax.rem(me + k, n)
        pl.semaphore_signal(barrier, inc=1, device_id=device_of(peer), device_id_type=MESH)
        return carry

    lax.fori_loop(1, n, greet, 0)
    pl.semaphore_wait(barrier, n - 1)

    def copy(a, k, c, slot):
        return pltpu.make_async_remote_copy(
            src_ref=source(a, c), dst_ref=outs[a].at[slot], send_sem=send_sem.at[a, k],
            recv_sem=recv_sem.at[a, slot], device_id=device_of(c), device_id_type=MESH)

    def send(k, carry):
        peer = lax.rem(me + k, n)
        for a in range(count):
            copy(a, k, peer, me).start()
        return carry

    lax.fori_loop(1, n, send, 0)
    locals_ = []
    for a in range(count):
        local = pltpu.make_async_copy(source(a, me), outs[a].at[me], local_sem.at[a])
        local.start()
        locals_.append(local)

    def finish(k, carry):
        peer = lax.rem(me + k, n)
        for a in range(count):
            copy(a, k, peer, me).wait_send()
            copy(a, k, peer, peer).wait_recv()
        return carry

    lax.fori_loop(1, n, finish, 0)
    for local in locals_:
        local.wait()


def all_exchange(arrays, spread, cid):
    npix = lax.axis_size("pix")
    n = lax.axis_size("det") * npix
    count = len(arrays)
    out_shape = [
        jax.ShapeDtypeStruct(x.shape if s else (n,) + x.shape, x.dtype) for x, s in zip(arrays, spread)
    ]
    return pl.pallas_call(
        functools.partial(_all_exchange_kernel, npix, n, tuple(spread)),
        out_shape=out_shape,
        in_specs=[pl.BlockSpec(memory_space=pltpu.VMEM)] * count,
        out_specs=[pl.BlockSpec(memory_space=pltpu.VMEM)] * count,
        scratch_shapes=[
            pltpu.SemaphoreType.DMA((count, n)),
            pltpu.SemaphoreType.DMA((count, n)),
            pltpu.SemaphoreType.DMA((count,)),
        ],
        compiler_params=pltpu.CompilerParams(collective_id=cid, has_side_effects=True),
    )(*arrays)


def _round_kernel(npix, n, k, scal, *refs):
    refs = list(refs)
    cells_in = refs.pop(0)
    hit_in = refs.pop(0) if k == 1 else None
    prev_in, local_in = (refs.pop(0), refs.pop(0)) if scal else (None, None)
    first_out, sky_all = refs.pop(0), refs.pop(0)
    scal_all = refs.pop(0) if scal else None
    recv, sky_cell = refs.pop(0), refs.pop(0)
    scal_cell = refs.pop(0) if scal else None
    send_sem, recv_sem, local_sem = refs
    me = lax.axis_index("det") * npix + lax.axis_index("pix")
    device_of = lambda c: (lax.div(c, npix), lax.rem(c, npix))
    barrier = pltpu.get_barrier_semaphore()

    def greet(j, carry):
        peer = lax.rem(me + j, n)
        pl.semaphore_signal(barrier, inc=1, device_id=device_of(peer), device_id_type=MESH)
        return carry

    lax.fori_loop(1, n, greet, 0, unroll=4)
    pl.semaphore_wait(barrier, n - 1)

    def exchange(a, src, dst, spread):
        def copy(j, c, slot):
            return pltpu.make_async_remote_copy(
                src_ref=src.at[c] if spread else src, dst_ref=dst.at[slot],
                send_sem=send_sem.at[a, j], recv_sem=recv_sem.at[a, slot],
                device_id=device_of(c), device_id_type=MESH)

        def send(j, carry):
            copy(j, lax.rem(me + j, n), me).start()
            return carry

        lax.fori_loop(1, n, send, 0, unroll=4)
        local = pltpu.make_async_copy(src.at[me] if spread else src, dst.at[me], local_sem.at[a])
        local.start()
        return copy, local

    def finish(copy, local):
        def wait(j, carry):
            peer = lax.rem(me + j, n)
            copy(j, peer, me).wait_send()
            copy(j, peer, peer).wait_recv()
            return carry

        lax.fori_loop(1, n, wait, 0, unroll=4)
        local.wait()

    finish(*exchange(0, cells_in, recv, True))
    rows = sky_cell.shape[0]
    acc = lax.fori_loop(
        0, n, lambda c, t: t + recv[c].astype(jnp.float32), jnp.zeros((k * rows, 128), jnp.float32), unroll=8)
    if k == 2:
        hit_plus = acc[:rows] + 1.0
        binned = acc[rows:]
        first_out[...] = hit_plus
    else:
        hit_plus = hit_in[...]
        binned = acc
        first_out[...] = binned
    sky = (binned / hit_plus).astype(sky_cell.dtype)
    sky_cell[...] = sky
    if scal:
        sky_wide = sky.astype(jnp.float32)
        lane = lax.broadcasted_iota(jnp.int32, (1, 128), 1)
        products = (jnp.where(lane == 5, jnp.sum(prev_in[...] * sky_wide), 0.0)
                    + jnp.where(lane == 6, jnp.sum(binned * sky_wide), 0.0))
        scal_cell[...] = local_in[...] + products
    pending = [exchange(1, sky_cell, sky_all, False)]
    if scal:
        pending.append(exchange(2, scal_cell, scal_all, False))
    for item in pending:
        finish(*item)


def fused_round(cells, k, hit_plus, prev, local, cid):
    npix = lax.axis_size("pix")
    n = lax.axis_size("det") * npix
    rows = cells.shape[1] // k
    scal = prev is not None
    args = [cells] + ([hit_plus] if k == 1 else []) + ([prev, local] if scal else [])
    out_shape = [jax.ShapeDtypeStruct((rows, 128), jnp.float32),
                 jax.ShapeDtypeStruct((n, rows, 128), jnp.bfloat16)]
    scratch = [pltpu.VMEM(cells.shape, cells.dtype), pltpu.VMEM((rows, 128), jnp.bfloat16)]
    if scal:
        out_shape.append(jax.ShapeDtypeStruct((n, 1, 128), jnp.float32))
        scratch.append(pltpu.VMEM((1, 128), jnp.float32))
    return pl.pallas_call(
        functools.partial(_round_kernel, npix, n, k, scal),
        out_shape=out_shape,
        in_specs=[pl.BlockSpec(memory_space=pltpu.VMEM)] * len(args),
        out_specs=[pl.BlockSpec(memory_space=pltpu.VMEM)] * len(out_shape),
        scratch_shapes=scratch + [
            pltpu.SemaphoreType.DMA((3, n)),
            pltpu.SemaphoreType.DMA((3, n)),
            pltpu.SemaphoreType.DMA((3,)),
        ],
        compiler_params=pltpu.CompilerParams(collective_id=cid, has_side_effects=True),
    )(*args)


def body(timestream, weights, block_owner, block_local, baseline_of):
    series_data = timestream[0]
    weight_rows = weights[0]
    owners = block_owner[0, :, 0]
    local_idx = block_local[0]
    segments_row = baseline_of[0]
    blocks, samples, pixels = weight_rows.shape
    pix_count = lax.axis_size("pix")
    devices = lax.axis_size("det") * pix_count
    sky_blocks_count = pix_count * PB_DEV
    cell = sky_blocks_count // devices
    cell_rows = cell * pixels // 128

    base_hot = (segments_row[:, None] == jnp.arange(NBASE_DEV)[None, :]).astype(jnp.float32)
    per_base = jnp.sum(base_hot, axis=0)
    weight_n = 1.0 + per_base
    block_pix = owners * PB_DEV + local_idx
    sky_hot = (block_pix[None, :] == jnp.arange(sky_blocks_count)[:, None]).astype(jnp.float32)
    sky_hot_t = (block_pix[:, None] == jnp.arange(sky_blocks_count)[None, :]).astype(jnp.bfloat16)

    unit_rows = jnp.ones((8, pixels), jnp.bfloat16)
    row_sums = jnp.einsum(
        "kp,bsp->kbs", unit_rows, weight_rows, preferred_element_type=jnp.float32
    )[0].astype(jnp.bfloat16)
    stacked = jnp.stack(
        [row_sums, series_data.astype(jnp.bfloat16), jnp.ones_like(row_sums)]
    )
    first_terms = jnp.einsum(
        "kbs,bsp->kbp", stacked, weight_rows, preferred_element_type=jnp.float32
    )
    col_sums = first_terms[2]
    series_block_sums = jnp.sum(series_data, axis=1)

    def to_cells(terms):
        dense = jnp.einsum("qb,kbp->kqp", sky_hot.astype(jnp.bfloat16), terms.astype(jnp.bfloat16),
                           preferred_element_type=jnp.float32)
        k = terms.shape[0]
        dense = dense.reshape(k, devices, cell_rows, 128).transpose(1, 0, 2, 3)
        return dense.reshape(devices, k * cell_rows, 128).astype(jnp.bfloat16)

    def to_blocks(sky_cells):
        return jnp.dot(sky_hot_t, sky_cells.reshape(sky_blocks_count, pixels),
                       preferred_element_type=jnp.float32)

    def scalar_rows(values):
        row = jnp.zeros((1, 128), jnp.float32)
        return row.at[0, : values.shape[0]].set(values)

    def cell_sum(arrived, k):
        total = jnp.sum(arrived.astype(jnp.float32), axis=0)
        return total.reshape(k, cell, pixels)

    hit_plus, back1 = fused_round(to_cells(first_terms[:2]), 2, None, None, None, 0)
    projected0 = jnp.sum(col_sums * to_blocks(back1), axis=1)
    r0 = jnp.dot(series_block_sums - projected0, base_hot, precision=HIGHEST) / samples

    def normal_action(amps, projected_blocks):
        collapsed = jnp.dot(projected_blocks, base_hot, precision=HIGHEST)
        return amps * weight_n - collapsed / samples

    def cells_of(amps):
        per_block = jnp.dot(base_hot, amps, precision=HIGHEST)
        return to_cells((per_block[:, None] * col_sums)[None])

    binned_r0, sky_r0 = fused_round(cells_of(r0), 1, hit_plus, None, None, 1)
    v1 = normal_action(r0, jnp.sum(col_sums * to_blocks(sky_r0), axis=1))
    left = jnp.stack([r0, r0, v1, r0 * weight_n, v1 * weight_n])
    right = jnp.stack([r0, v1, v1, v1, v1])
    partials = jnp.sum(left * right, axis=1)
    local = jnp.pad(partials, (0, 128 - partials.shape[0])).reshape(1, 128)
    _, sky_v1, carried = fused_round(cells_of(v1), 1, hit_plus, binned_r0, local, 2)
    total_row = jnp.sum(carried, axis=0)
    picks = (jnp.arange(128)[:, None] == (jnp.arange(7 * NBASE_DEV) // NBASE_DEV)[None, :])
    rows = jnp.dot(total_row, picks.astype(jnp.float32), precision=HIGHEST).reshape(7, NBASE_DEV)
    v2 = normal_action(v1, jnp.sum(col_sums * to_blocks(sky_v1), axis=1))

    rr0, r0v1, v1v1 = rows[0], rows[1], rows[2]
    r0v2 = rows[3] - rows[5] / samples
    v1v2 = rows[4] - rows[6] / samples
    alpha0 = rr0 / r0v1
    rr1 = rr0 - 2.0 * alpha0 * r0v1 + alpha0 * alpha0 * v1v1
    beta0 = rr1 / rr0
    grow = 1.0 + beta0
    d1_ad1 = grow * grow * r0v1 - grow * alpha0 * r0v2 - alpha0 * grow * v1v1 + alpha0 * alpha0 * v1v2
    alpha1 = rr1 / d1_ad1
    d1 = grow * r0 - alpha0 * v1
    ad1 = grow * v1 - alpha0 * v2
    offset_levels = alpha0 * r0 + alpha1 * d1
    leftover_error = r0 - alpha0 * v1 - alpha1 * ad1
    return (offset_levels[None], leftover_error[None])


def solution(mesh):
    placed = (
        P(("det", "pix"), None, None),
        P(("det", "pix"), None, None, None),
        P(("det", "pix"), None, None),
        P(("det", "pix"), None),
        P(("det", "pix"), None),
    )
    return jax.shard_map(
        body,
        mesh=mesh,
        in_specs=placed,
        out_specs=(P(("det", "pix"), None), P(("det", "pix"), None)),
        check_vma=False,
    )
```

```python
import functools

import jax
import jax.numpy as jnp
from jax import lax
from jax.experimental import pallas as pl
from jax.experimental.pallas import tpu as pltpu
from jax.sharding import PartitionSpec as P

MESH = pl.DeviceIdType.MESH
PB_DEV = 64
NBASE_DEV = 128
HIGHEST = lax.Precision.HIGHEST


def _greet(peers, device_of):
    barrier = pltpu.get_barrier_semaphore()
    for peer in peers:
        pl.semaphore_signal(barrier, inc=1, device_id=device_of(peer), device_id_type=MESH)
    pl.semaphore_wait(barrier, len(peers))


def _det_sum_kernel(n, x_ref, o_ref, recv, send_sem, recv_sem, local_sem):
    me = lax.axis_index("det")
    pix = lax.axis_index("pix")
    device_of = lambda d: (d, pix)
    _greet([lax.rem(me + k, n) for k in range(1, n)], device_of)
    sends = []
    for k in range(1, n):
        peer = lax.rem(me + k, n)
        copy = pltpu.make_async_remote_copy(
            src_ref=x_ref, dst_ref=recv.at[me], send_sem=send_sem.at[k],
            recv_sem=recv_sem.at[me], device_id=device_of(peer), device_id_type=MESH)
        copy.start()
        sends.append(copy)
    local = pltpu.make_async_copy(x_ref, recv.at[me], local_sem)
    local.start()
    for copy in sends:
        copy.wait_send()
    for k in range(1, n):
        src = lax.rem(me + k, n)
        pltpu.make_async_remote_copy(
            src_ref=x_ref, dst_ref=recv.at[src], send_sem=send_sem.at[k],
            recv_sem=recv_sem.at[src], device_id=device_of(src), device_id_type=MESH).wait_recv()
    local.wait()
    acc = recv[0]
    for s in range(1, n):
        acc = acc + recv[s]
    o_ref[...] = acc


def det_sum(x, cid):
    n = lax.axis_size("det")
    return pl.pallas_call(
        functools.partial(_det_sum_kernel, n),
        out_shape=jax.ShapeDtypeStruct(x.shape, x.dtype),
        in_specs=[pl.BlockSpec(memory_space=pltpu.VMEM)],
        out_specs=pl.BlockSpec(memory_space=pltpu.VMEM),
        scratch_shapes=[
            pltpu.VMEM((n,) + x.shape, x.dtype),
            pltpu.SemaphoreType.DMA((n,)),
            pltpu.SemaphoreType.DMA((n,)),
            pltpu.SemaphoreType.DMA(()),
        ],
        compiler_params=pltpu.CompilerParams(collective_id=cid, has_side_effects=True),
    )(x)


def _pix_exchange_kernel(n, spread, *refs):
    count = len(spread)
    ins, outs = refs[:count], refs[count:2 * count]
    send_sem, recv_sem, local_sem = refs[2 * count:]
    me = lax.axis_index("pix")
    det = lax.axis_index("det")
    device_of = lambda j: (det, j)
    _greet([lax.rem(me + k, n) for k in range(1, n)], device_of)
    source = lambda a, j: ins[a].at[j] if spread[a] else ins[a]
    sends, locals_ = [], []
    for a in range(count):
        for k in range(1, n):
            peer = lax.rem(me + k, n)
            copy = pltpu.make_async_remote_copy(
                src_ref=source(a, peer), dst_ref=outs[a].at[me], send_sem=send_sem.at[a, k],
                recv_sem=recv_sem.at[a, me], device_id=device_of(peer), device_id_type=MESH)
            copy.start()
            sends.append(copy)
        local = pltpu.make_async_copy(source(a, me), outs[a].at[me], local_sem.at[a])
        local.start()
        locals_.append(local)
    for copy in sends:
        copy.wait_send()
    for a in range(count):
        for k in range(1, n):
            src = lax.rem(me + k, n)
            pltpu.make_async_remote_copy(
                src_ref=source(a, src), dst_ref=outs[a].at[src], send_sem=send_sem.at[a, k],
                recv_sem=recv_sem.at[a, src], device_id=device_of(src), device_id_type=MESH).wait_recv()
        locals_[a].wait()


def pix_exchange(arrays, spread, cid):
    n = lax.axis_size("pix")
    count = len(arrays)
    out_shape = [
        jax.ShapeDtypeStruct(x.shape if s else (n,) + x.shape, x.dtype) for x, s in zip(arrays, spread)
    ]
    return pl.pallas_call(
        functools.partial(_pix_exchange_kernel, n, tuple(spread)),
        out_shape=out_shape,
        in_specs=[pl.BlockSpec(memory_space=pltpu.VMEM)] * count,
        out_specs=[pl.BlockSpec(memory_space=pltpu.VMEM)] * count,
        scratch_shapes=[
            pltpu.SemaphoreType.DMA((count, n)),
            pltpu.SemaphoreType.DMA((count, n)),
            pltpu.SemaphoreType.DMA((count,)),
        ],
        compiler_params=pltpu.CompilerParams(collective_id=cid, has_side_effects=True),
    )(*arrays)


def _all_exchange_kernel(npix, n, spread, *refs):
    count = len(spread)
    ins, outs = refs[:count], refs[count:2 * count]
    send_sem, recv_sem, local_sem = refs[2 * count:]
    me = lax.axis_index("det") * npix + lax.axis_index("pix")
    device_of = lambda c: (lax.div(c, npix), lax.rem(c, npix))
    source = lambda a, c: ins[a].at[c] if spread[a] else ins[a]
    barrier = pltpu.get_barrier_semaphore()

    def greet(k, carry):
        peer = lax.rem(me + k, n)
        pl.semaphore_signal(barrier, inc=1, device_id=device_of(peer), device_id_type=MESH)
        return carry

    lax.fori_loop(1, n, greet, 0)
    pl.semaphore_wait(barrier, n - 1)

    def copy(a, k, c, slot):
        return pltpu.make_async_remote_copy(
            src_ref=source(a, c), dst_ref=outs[a].at[slot], send_sem=send_sem.at[a, k],
            recv_sem=recv_sem.at[a, slot], device_id=device_of(c), device_id_type=MESH)

    def send(k, carry):
        peer = lax.rem(me + k, n)
        for a in range(count):
            copy(a, k, peer, me).start()
        return carry

    lax.fori_loop(1, n, send, 0)
    locals_ = []
    for a in range(count):
        local = pltpu.make_async_copy(source(a, me), outs[a].at[me], local_sem.at[a])
        local.start()
        locals_.append(local)

    def finish(k, carry):
        peer = lax.rem(me + k, n)
        for a in range(count):
            copy(a, k, peer, me).wait_send()
            copy(a, k, peer, peer).wait_recv()
        return carry

    lax.fori_loop(1, n, finish, 0)
    for local in locals_:
        local.wait()


def all_exchange(arrays, spread, cid):
    npix = lax.axis_size("pix")
    n = lax.axis_size("det") * npix
    count = len(arrays)
    out_shape = [
        jax.ShapeDtypeStruct(x.shape if s else (n,) + x.shape, x.dtype) for x, s in zip(arrays, spread)
    ]
    return pl.pallas_call(
        functools.partial(_all_exchange_kernel, npix, n, tuple(spread)),
        out_shape=out_shape,
        in_specs=[pl.BlockSpec(memory_space=pltpu.VMEM)] * count,
        out_specs=[pl.BlockSpec(memory_space=pltpu.VMEM)] * count,
        scratch_shapes=[
            pltpu.SemaphoreType.DMA((count, n)),
            pltpu.SemaphoreType.DMA((count, n)),
            pltpu.SemaphoreType.DMA((count,)),
        ],
        compiler_params=pltpu.CompilerParams(collective_id=cid, has_side_effects=True),
    )(*arrays)


def _round_kernel(npix, n, k, scal, *refs):
    refs = list(refs)
    cells_in = refs.pop(0)
    hit_in = refs.pop(0) if k == 1 else None
    prev_in, local_in = (refs.pop(0), refs.pop(0)) if scal else (None, None)
    first_out, sky_all = refs.pop(0), refs.pop(0)
    scal_all = refs.pop(0) if scal else None
    recv, sky_cell = refs.pop(0), refs.pop(0)
    scal_cell = refs.pop(0) if scal else None
    send_sem, recv_sem, local_sem = refs
    me = lax.axis_index("det") * npix + lax.axis_index("pix")
    device_of = lambda c: (lax.div(c, npix), lax.rem(c, npix))
    barrier = pltpu.get_barrier_semaphore()

    def greet(j, carry):
        peer = lax.rem(me + j, n)
        pl.semaphore_signal(barrier, inc=1, device_id=device_of(peer), device_id_type=MESH)
        return carry

    lax.fori_loop(1, n, greet, 0, unroll=8)
    pl.semaphore_wait(barrier, n - 1)

    def exchange(a, src, dst, spread):
        def copy(j, c, slot):
            return pltpu.make_async_remote_copy(
                src_ref=src.at[c] if spread else src, dst_ref=dst.at[slot],
                send_sem=send_sem.at[a, j], recv_sem=recv_sem.at[a, slot],
                device_id=device_of(c), device_id_type=MESH)

        def send(j, carry):
            copy(j, lax.rem(me + j, n), me).start()
            return carry

        lax.fori_loop(1, n, send, 0, unroll=8)
        local = pltpu.make_async_copy(src.at[me] if spread else src, dst.at[me], local_sem.at[a])
        local.start()
        return copy, local

    def finish(copy, local):
        def wait(j, carry):
            peer = lax.rem(me + j, n)
            copy(j, peer, me).wait_send()
            copy(j, peer, peer).wait_recv()
            return carry

        lax.fori_loop(1, n, wait, 0, unroll=8)
        local.wait()

    finish(*exchange(0, cells_in, recv, True))
    rows = sky_cell.shape[0]
    acc = lax.fori_loop(
        0, n, lambda c, t: t + recv[c].astype(jnp.float32), jnp.zeros((k * rows, 128), jnp.float32), unroll=16)
    if k == 2:
        hit_plus = acc[:rows] + 1.0
        binned = acc[rows:]
        first_out[...] = hit_plus
    else:
        hit_plus = hit_in[...]
        binned = acc
        first_out[...] = binned
    sky = (binned / hit_plus).astype(sky_cell.dtype)
    sky_cell[...] = sky
    if scal:
        sky_wide = sky.astype(jnp.float32)
        lane = lax.broadcasted_iota(jnp.int32, (1, 128), 1)
        products = (jnp.where(lane == 5, jnp.sum(prev_in[...] * sky_wide), 0.0)
                    + jnp.where(lane == 6, jnp.sum(binned * sky_wide), 0.0))
        scal_cell[...] = local_in[...] + products
    pending = [exchange(1, sky_cell, sky_all, False)]
    if scal:
        pending.append(exchange(2, scal_cell, scal_all, False))
    for item in pending:
        finish(*item)


def fused_round(cells, k, hit_plus, prev, local, cid):
    npix = lax.axis_size("pix")
    n = lax.axis_size("det") * npix
    rows = cells.shape[1] // k
    scal = prev is not None
    args = [cells] + ([hit_plus] if k == 1 else []) + ([prev, local] if scal else [])
    out_shape = [jax.ShapeDtypeStruct((rows, 128), jnp.float32),
                 jax.ShapeDtypeStruct((n, rows, 128), jnp.bfloat16)]
    scratch = [pltpu.VMEM(cells.shape, cells.dtype), pltpu.VMEM((rows, 128), jnp.bfloat16)]
    if scal:
        out_shape.append(jax.ShapeDtypeStruct((n, 1, 128), jnp.float32))
        scratch.append(pltpu.VMEM((1, 128), jnp.float32))
    return pl.pallas_call(
        functools.partial(_round_kernel, npix, n, k, scal),
        out_shape=out_shape,
        in_specs=[pl.BlockSpec(memory_space=pltpu.VMEM)] * len(args),
        out_specs=[pl.BlockSpec(memory_space=pltpu.VMEM)] * len(out_shape),
        scratch_shapes=scratch + [
            pltpu.SemaphoreType.DMA((3, n)),
            pltpu.SemaphoreType.DMA((3, n)),
            pltpu.SemaphoreType.DMA((3,)),
        ],
        compiler_params=pltpu.CompilerParams(collective_id=cid, has_side_effects=True),
    )(*args)


def body(timestream, weights, block_owner, block_local, baseline_of):
    series_data = timestream[0]
    weight_rows = weights[0]
    owners = block_owner[0, :, 0]
    local_idx = block_local[0]
    segments_row = baseline_of[0]
    blocks, samples, pixels = weight_rows.shape
    pix_count = lax.axis_size("pix")
    devices = lax.axis_size("det") * pix_count
    sky_blocks_count = pix_count * PB_DEV
    cell = sky_blocks_count // devices
    cell_rows = cell * pixels // 128

    base_hot = (segments_row[:, None] == jnp.arange(NBASE_DEV)[None, :]).astype(jnp.float32)
    per_base = jnp.sum(base_hot, axis=0)
    weight_n = 1.0 + per_base
    block_pix = owners * PB_DEV + local_idx
    sky_hot = (block_pix[None, :] == jnp.arange(sky_blocks_count)[:, None]).astype(jnp.float32)
    sky_hot_t = (block_pix[:, None] == jnp.arange(sky_blocks_count)[None, :]).astype(jnp.bfloat16)

    unit_rows = jnp.ones((8, pixels), jnp.bfloat16)
    row_sums = jnp.einsum(
        "kp,bsp->kbs", unit_rows, weight_rows, preferred_element_type=jnp.float32
    )[0].astype(jnp.bfloat16)
    stacked = jnp.stack(
        [row_sums, series_data.astype(jnp.bfloat16), jnp.ones_like(row_sums)]
    )
    first_terms = jnp.einsum(
        "kbs,bsp->kbp", stacked, weight_rows, preferred_element_type=jnp.float32
    )
    col_sums = first_terms[2]
    series_block_sums = jnp.sum(series_data, axis=1)

    def to_cells(terms):
        dense = jnp.einsum("qb,kbp->kqp", sky_hot.astype(jnp.bfloat16), terms.astype(jnp.bfloat16),
                           preferred_element_type=jnp.float32)
        k = terms.shape[0]
        dense = dense.reshape(k, devices, cell_rows, 128).transpose(1, 0, 2, 3)
        return dense.reshape(devices, k * cell_rows, 128).astype(jnp.bfloat16)

    def to_blocks(sky_cells):
        return jnp.dot(sky_hot_t, sky_cells.reshape(sky_blocks_count, pixels),
                       preferred_element_type=jnp.float32)

    def scalar_rows(values):
        row = jnp.zeros((1, 128), jnp.float32)
        return row.at[0, : values.shape[0]].set(values)

    def cell_sum(arrived, k):
        total = jnp.sum(arrived.astype(jnp.float32), axis=0)
        return total.reshape(k, cell, pixels)

    hit_plus, back1 = fused_round(to_cells(first_terms[:2]), 2, None, None, None, 0)
    projected0 = jnp.sum(col_sums * to_blocks(back1), axis=1)
    r0 = jnp.dot(series_block_sums - projected0, base_hot, precision=HIGHEST) / samples

    def normal_action(amps, projected_blocks):
        collapsed = jnp.dot(projected_blocks, base_hot, precision=HIGHEST)
        return amps * weight_n - collapsed / samples

    def cells_of(amps):
        per_block = jnp.dot(base_hot, amps, precision=HIGHEST)
        return to_cells((per_block[:, None] * col_sums)[None])

    binned_r0, sky_r0 = fused_round(cells_of(r0), 1, hit_plus, None, None, 1)
    v1 = normal_action(r0, jnp.sum(col_sums * to_blocks(sky_r0), axis=1))
    left = jnp.stack([r0, r0, v1, r0 * weight_n, v1 * weight_n])
    right = jnp.stack([r0, v1, v1, v1, v1])
    partials = jnp.sum(left * right, axis=1)
    local = jnp.pad(partials, (0, 128 - partials.shape[0])).reshape(1, 128)
    _, sky_v1, carried = fused_round(cells_of(v1), 1, hit_plus, binned_r0, local, 2)
    total_row = jnp.sum(carried, axis=0)
    picks = (jnp.arange(128)[:, None] == (jnp.arange(7 * NBASE_DEV) // NBASE_DEV)[None, :])
    rows = jnp.dot(total_row, picks.astype(jnp.float32), precision=HIGHEST).reshape(7, NBASE_DEV)
    v2 = normal_action(v1, jnp.sum(col_sums * to_blocks(sky_v1), axis=1))

    rr0, r0v1, v1v1 = rows[0], rows[1], rows[2]
    r0v2 = rows[3] - rows[5] / samples
    v1v2 = rows[4] - rows[6] / samples
    alpha0 = rr0 / r0v1
    rr1 = rr0 - 2.0 * alpha0 * r0v1 + alpha0 * alpha0 * v1v1
    beta0 = rr1 / rr0
    grow = 1.0 + beta0
    d1_ad1 = grow * grow * r0v1 - grow * alpha0 * r0v2 - alpha0 * grow * v1v1 + alpha0 * alpha0 * v1v2
    alpha1 = rr1 / d1_ad1
    d1 = grow * r0 - alpha0 * v1
    ad1 = grow * v1 - alpha0 * v2
    offset_levels = alpha0 * r0 + alpha1 * d1
    leftover_error = r0 - alpha0 * v1 - alpha1 * ad1
    return (offset_levels[None], leftover_error[None])


def solution(mesh):
    placed = (
        P(("det", "pix"), None, None),
        P(("det", "pix"), None, None, None),
        P(("det", "pix"), None, None),
        P(("det", "pix"), None),
        P(("det", "pix"), None),
    )
    return jax.shard_map(
        body,
        mesh=mesh,
        in_specs=placed,
        out_specs=(P(("det", "pix"), None), P(("det", "pix"), None)),
        check_vma=False,
    )
```

```python
import functools

import jax
import jax.numpy as jnp
from jax import lax
from jax.experimental import pallas as pl
from jax.experimental.pallas import tpu as pltpu
from jax.sharding import PartitionSpec as P

MESH = pl.DeviceIdType.MESH
PB_DEV = 64
NBASE_DEV = 128
HIGHEST = lax.Precision.HIGHEST


def _greet(peers, device_of):
    barrier = pltpu.get_barrier_semaphore()
    for peer in peers:
        pl.semaphore_signal(barrier, inc=1, device_id=device_of(peer), device_id_type=MESH)
    pl.semaphore_wait(barrier, len(peers))


def _det_sum_kernel(n, x_ref, o_ref, recv, send_sem, recv_sem, local_sem):
    me = lax.axis_index("det")
    pix = lax.axis_index("pix")
    device_of = lambda d: (d, pix)
    _greet([lax.rem(me + k, n) for k in range(1, n)], device_of)
    sends = []
    for k in range(1, n):
        peer = lax.rem(me + k, n)
        copy = pltpu.make_async_remote_copy(
            src_ref=x_ref, dst_ref=recv.at[me], send_sem=send_sem.at[k],
            recv_sem=recv_sem.at[me], device_id=device_of(peer), device_id_type=MESH)
        copy.start()
        sends.append(copy)
    local = pltpu.make_async_copy(x_ref, recv.at[me], local_sem)
    local.start()
    for copy in sends:
        copy.wait_send()
    for k in range(1, n):
        src = lax.rem(me + k, n)
        pltpu.make_async_remote_copy(
            src_ref=x_ref, dst_ref=recv.at[src], send_sem=send_sem.at[k],
            recv_sem=recv_sem.at[src], device_id=device_of(src), device_id_type=MESH).wait_recv()
    local.wait()
    acc = recv[0]
    for s in range(1, n):
        acc = acc + recv[s]
    o_ref[...] = acc


def det_sum(x, cid):
    n = lax.axis_size("det")
    return pl.pallas_call(
        functools.partial(_det_sum_kernel, n),
        out_shape=jax.ShapeDtypeStruct(x.shape, x.dtype),
        in_specs=[pl.BlockSpec(memory_space=pltpu.VMEM)],
        out_specs=pl.BlockSpec(memory_space=pltpu.VMEM),
        scratch_shapes=[
            pltpu.VMEM((n,) + x.shape, x.dtype),
            pltpu.SemaphoreType.DMA((n,)),
            pltpu.SemaphoreType.DMA((n,)),
            pltpu.SemaphoreType.DMA(()),
        ],
        compiler_params=pltpu.CompilerParams(collective_id=cid, has_side_effects=True),
    )(x)


def _pix_exchange_kernel(n, spread, *refs):
    count = len(spread)
    ins, outs = refs[:count], refs[count:2 * count]
    send_sem, recv_sem, local_sem = refs[2 * count:]
    me = lax.axis_index("pix")
    det = lax.axis_index("det")
    device_of = lambda j: (det, j)
    _greet([lax.rem(me + k, n) for k in range(1, n)], device_of)
    source = lambda a, j: ins[a].at[j] if spread[a] else ins[a]
    sends, locals_ = [], []
    for a in range(count):
        for k in range(1, n):
            peer = lax.rem(me + k, n)
            copy = pltpu.make_async_remote_copy(
                src_ref=source(a, peer), dst_ref=outs[a].at[me], send_sem=send_sem.at[a, k],
                recv_sem=recv_sem.at[a, me], device_id=device_of(peer), device_id_type=MESH)
            copy.start()
            sends.append(copy)
        local = pltpu.make_async_copy(source(a, me), outs[a].at[me], local_sem.at[a])
        local.start()
        locals_.append(local)
    for copy in sends:
        copy.wait_send()
    for a in range(count):
        for k in range(1, n):
            src = lax.rem(me + k, n)
            pltpu.make_async_remote_copy(
                src_ref=source(a, src), dst_ref=outs[a].at[src], send_sem=send_sem.at[a, k],
                recv_sem=recv_sem.at[a, src], device_id=device_of(src), device_id_type=MESH).wait_recv()
        locals_[a].wait()


def pix_exchange(arrays, spread, cid):
    n = lax.axis_size("pix")
    count = len(arrays)
    out_shape = [
        jax.ShapeDtypeStruct(x.shape if s else (n,) + x.shape, x.dtype) for x, s in zip(arrays, spread)
    ]
    return pl.pallas_call(
        functools.partial(_pix_exchange_kernel, n, tuple(spread)),
        out_shape=out_shape,
        in_specs=[pl.BlockSpec(memory_space=pltpu.VMEM)] * count,
        out_specs=[pl.BlockSpec(memory_space=pltpu.VMEM)] * count,
        scratch_shapes=[
            pltpu.SemaphoreType.DMA((count, n)),
            pltpu.SemaphoreType.DMA((count, n)),
            pltpu.SemaphoreType.DMA((count,)),
        ],
        compiler_params=pltpu.CompilerParams(collective_id=cid, has_side_effects=True),
    )(*arrays)


def _all_exchange_kernel(npix, n, spread, *refs):
    count = len(spread)
    ins, outs = refs[:count], refs[count:2 * count]
    send_sem, recv_sem, local_sem = refs[2 * count:]
    me = lax.axis_index("det") * npix + lax.axis_index("pix")
    device_of = lambda c: (lax.div(c, npix), lax.rem(c, npix))
    source = lambda a, c: ins[a].at[c] if spread[a] else ins[a]
    barrier = pltpu.get_barrier_semaphore()

    def greet(k, carry):
        peer = lax.rem(me + k, n)
        pl.semaphore_signal(barrier, inc=1, device_id=device_of(peer), device_id_type=MESH)
        return carry

    lax.fori_loop(1, n, greet, 0)
    pl.semaphore_wait(barrier, n - 1)

    def copy(a, k, c, slot):
        return pltpu.make_async_remote_copy(
            src_ref=source(a, c), dst_ref=outs[a].at[slot], send_sem=send_sem.at[a, k],
            recv_sem=recv_sem.at[a, slot], device_id=device_of(c), device_id_type=MESH)

    def send(k, carry):
        peer = lax.rem(me + k, n)
        for a in range(count):
            copy(a, k, peer, me).start()
        return carry

    lax.fori_loop(1, n, send, 0)
    locals_ = []
    for a in range(count):
        local = pltpu.make_async_copy(source(a, me), outs[a].at[me], local_sem.at[a])
        local.start()
        locals_.append(local)

    def finish(k, carry):
        peer = lax.rem(me + k, n)
        for a in range(count):
            copy(a, k, peer, me).wait_send()
            copy(a, k, peer, peer).wait_recv()
        return carry

    lax.fori_loop(1, n, finish, 0)
    for local in locals_:
        local.wait()


def all_exchange(arrays, spread, cid):
    npix = lax.axis_size("pix")
    n = lax.axis_size("det") * npix
    count = len(arrays)
    out_shape = [
        jax.ShapeDtypeStruct(x.shape if s else (n,) + x.shape, x.dtype) for x, s in zip(arrays, spread)
    ]
    return pl.pallas_call(
        functools.partial(_all_exchange_kernel, npix, n, tuple(spread)),
        out_shape=out_shape,
        in_specs=[pl.BlockSpec(memory_space=pltpu.VMEM)] * count,
        out_specs=[pl.BlockSpec(memory_space=pltpu.VMEM)] * count,
        scratch_shapes=[
            pltpu.SemaphoreType.DMA((count, n)),
            pltpu.SemaphoreType.DMA((count, n)),
            pltpu.SemaphoreType.DMA((count,)),
        ],
        compiler_params=pltpu.CompilerParams(collective_id=cid, has_side_effects=True),
    )(*arrays)


def _round_kernel(npix, n, k, scal, *refs):
    refs = list(refs)
    cells_in = refs.pop(0)
    hit_in = refs.pop(0) if k == 1 else None
    prev_in, local_in = (refs.pop(0), refs.pop(0)) if scal else (None, None)
    first_out, sky_all = refs.pop(0), refs.pop(0)
    scal_all = refs.pop(0) if scal else None
    recv, sky_cell = refs.pop(0), refs.pop(0)
    scal_cell = refs.pop(0) if scal else None
    send_sem, recv_sem, local_sem = refs
    me = lax.axis_index("det") * npix + lax.axis_index("pix")
    device_of = lambda c: (lax.div(c, npix), lax.rem(c, npix))
    barrier = pltpu.get_barrier_semaphore()

    def greet(j, carry):
        peer = lax.rem(me + j, n)
        pl.semaphore_signal(barrier, inc=1, device_id=device_of(peer), device_id_type=MESH)
        return carry

    lax.fori_loop(1, n, greet, 0, unroll=8)
    pl.semaphore_wait(barrier, n - 1)

    def exchange(items):
        def copy(item, j, c, slot):
            a, src, dst, spread = item
            return pltpu.make_async_remote_copy(
                src_ref=src.at[c] if spread else src, dst_ref=dst.at[slot],
                send_sem=send_sem.at[a, j], recv_sem=recv_sem.at[a, slot],
                device_id=device_of(c), device_id_type=MESH)

        def send(j, carry):
            for item in items:
                copy(item, j, lax.rem(me + j, n), me).start()
            return carry

        lax.fori_loop(1, n, send, 0, unroll=8)
        locals_ = []
        for a, src, dst, spread in items:
            local = pltpu.make_async_copy(src.at[me] if spread else src, dst.at[me], local_sem.at[a])
            local.start()
            locals_.append(local)

        def wait(j, carry):
            peer = lax.rem(me + j, n)
            for item in items:
                copy(item, j, peer, me).wait_send()
                copy(item, j, peer, peer).wait_recv()
            return carry

        lax.fori_loop(1, n, wait, 0, unroll=8)
        for local in locals_:
            local.wait()

    exchange([(0, cells_in, recv, True)])
    rows = sky_cell.shape[0]
    acc = lax.fori_loop(
        0, n, lambda c, t: t + recv[c].astype(jnp.float32), jnp.zeros((k * rows, 128), jnp.float32), unroll=16)
    if k == 2:
        hit_plus = acc[:rows] + 1.0
        binned = acc[rows:]
        first_out[...] = hit_plus
    else:
        hit_plus = hit_in[...]
        binned = acc
        first_out[...] = binned
    sky = (binned / hit_plus).astype(sky_cell.dtype)
    sky_cell[...] = sky
    if scal:
        sky_wide = sky.astype(jnp.float32)
        lane = lax.broadcasted_iota(jnp.int32, (1, 128), 1)
        products = (jnp.where(lane == 5, jnp.sum(prev_in[...] * sky_wide), 0.0)
                    + jnp.where(lane == 6, jnp.sum(binned * sky_wide), 0.0))
        scal_cell[...] = local_in[...] + products
    items = [(1, sky_cell, sky_all, False)]
    if scal:
        items.append((2, scal_cell, scal_all, False))
    exchange(items)


def fused_round(cells, k, hit_plus, prev, local, cid):
    npix = lax.axis_size("pix")
    n = lax.axis_size("det") * npix
    rows = cells.shape[1] // k
    scal = prev is not None
    args = [cells] + ([hit_plus] if k == 1 else []) + ([prev, local] if scal else [])
    out_shape = [jax.ShapeDtypeStruct((rows, 128), jnp.float32),
                 jax.ShapeDtypeStruct((n, rows, 128), jnp.bfloat16)]
    scratch = [pltpu.VMEM(cells.shape, cells.dtype), pltpu.VMEM((rows, 128), jnp.bfloat16)]
    if scal:
        out_shape.append(jax.ShapeDtypeStruct((n, 1, 128), jnp.float32))
        scratch.append(pltpu.VMEM((1, 128), jnp.float32))
    return pl.pallas_call(
        functools.partial(_round_kernel, npix, n, k, scal),
        out_shape=out_shape,
        in_specs=[pl.BlockSpec(memory_space=pltpu.VMEM)] * len(args),
        out_specs=[pl.BlockSpec(memory_space=pltpu.VMEM)] * len(out_shape),
        scratch_shapes=scratch + [
            pltpu.SemaphoreType.DMA((3, n)),
            pltpu.SemaphoreType.DMA((3, n)),
            pltpu.SemaphoreType.DMA((3,)),
        ],
        compiler_params=pltpu.CompilerParams(collective_id=cid, has_side_effects=True),
    )(*args)


def body(timestream, weights, block_owner, block_local, baseline_of):
    series_data = timestream[0]
    weight_rows = weights[0]
    owners = block_owner[0, :, 0]
    local_idx = block_local[0]
    segments_row = baseline_of[0]
    blocks, samples, pixels = weight_rows.shape
    pix_count = lax.axis_size("pix")
    devices = lax.axis_size("det") * pix_count
    sky_blocks_count = pix_count * PB_DEV
    cell = sky_blocks_count // devices
    cell_rows = cell * pixels // 128

    base_hot = (segments_row[:, None] == jnp.arange(NBASE_DEV)[None, :]).astype(jnp.float32)
    per_base = jnp.sum(base_hot, axis=0)
    weight_n = 1.0 + per_base
    block_pix = owners * PB_DEV + local_idx
    sky_hot = (block_pix[None, :] == jnp.arange(sky_blocks_count)[:, None]).astype(jnp.float32)
    sky_hot_t = (block_pix[:, None] == jnp.arange(sky_blocks_count)[None, :]).astype(jnp.bfloat16)

    unit_rows = jnp.ones((8, pixels), jnp.bfloat16)
    row_sums = jnp.einsum(
        "kp,bsp->kbs", unit_rows, weight_rows, preferred_element_type=jnp.float32
    )[0].astype(jnp.bfloat16)
    stacked = jnp.stack(
        [row_sums, series_data.astype(jnp.bfloat16), jnp.ones_like(row_sums)]
    )
    first_terms = jnp.einsum(
        "kbs,bsp->kbp", stacked, weight_rows, preferred_element_type=jnp.float32
    )
    col_sums = first_terms[2]
    series_block_sums = jnp.sum(series_data, axis=1)

    def to_cells(terms):
        dense = jnp.einsum("qb,kbp->kqp", sky_hot.astype(jnp.bfloat16), terms.astype(jnp.bfloat16),
                           preferred_element_type=jnp.float32)
        k = terms.shape[0]
        dense = dense.reshape(k, devices, cell_rows, 128).transpose(1, 0, 2, 3)
        return dense.reshape(devices, k * cell_rows, 128).astype(jnp.bfloat16)

    def to_blocks(sky_cells):
        return jnp.dot(sky_hot_t, sky_cells.reshape(sky_blocks_count, pixels),
                       preferred_element_type=jnp.float32)

    def scalar_rows(values):
        row = jnp.zeros((1, 128), jnp.float32)
        return row.at[0, : values.shape[0]].set(values)

    def cell_sum(arrived, k):
        total = jnp.sum(arrived.astype(jnp.float32), axis=0)
        return total.reshape(k, cell, pixels)

    hit_plus, back1 = fused_round(to_cells(first_terms[:2]), 2, None, None, None, 0)
    projected0 = jnp.sum(col_sums * to_blocks(back1), axis=1)
    r0 = jnp.dot(series_block_sums - projected0, base_hot, precision=HIGHEST) / samples

    def normal_action(amps, projected_blocks):
        collapsed = jnp.dot(projected_blocks, base_hot, precision=HIGHEST)
        return amps * weight_n - collapsed / samples

    def cells_of(amps):
        per_block = jnp.dot(base_hot, amps, precision=HIGHEST)
        return to_cells((per_block[:, None] * col_sums)[None])

    binned_r0, sky_r0 = fused_round(cells_of(r0), 1, hit_plus, None, None, 1)
    v1 = normal_action(r0, jnp.sum(col_sums * to_blocks(sky_r0), axis=1))
    left = jnp.stack([r0, r0, v1, r0 * weight_n, v1 * weight_n])
    right = jnp.stack([r0, v1, v1, v1, v1])
    partials = jnp.sum(left * right, axis=1)
    local = jnp.pad(partials, (0, 128 - partials.shape[0])).reshape(1, 128)
    _, sky_v1, carried = fused_round(cells_of(v1), 1, hit_plus, binned_r0, local, 2)
    total_row = jnp.sum(carried, axis=0)
    picks = (jnp.arange(128)[:, None] == (jnp.arange(7 * NBASE_DEV) // NBASE_DEV)[None, :])
    rows = jnp.dot(total_row, picks.astype(jnp.float32), precision=HIGHEST).reshape(7, NBASE_DEV)
    v2 = normal_action(v1, jnp.sum(col_sums * to_blocks(sky_v1), axis=1))

    rr0, r0v1, v1v1 = rows[0], rows[1], rows[2]
    r0v2 = rows[3] - rows[5] / samples
    v1v2 = rows[4] - rows[6] / samples
    alpha0 = rr0 / r0v1
    rr1 = rr0 - 2.0 * alpha0 * r0v1 + alpha0 * alpha0 * v1v1
    beta0 = rr1 / rr0
    grow = 1.0 + beta0
    d1_ad1 = grow * grow * r0v1 - grow * alpha0 * r0v2 - alpha0 * grow * v1v1 + alpha0 * alpha0 * v1v2
    alpha1 = rr1 / d1_ad1
    d1 = grow * r0 - alpha0 * v1
    ad1 = grow * v1 - alpha0 * v2
    offset_levels = alpha0 * r0 + alpha1 * d1
    leftover_error = r0 - alpha0 * v1 - alpha1 * ad1
    return (offset_levels[None], leftover_error[None])


def solution(mesh):
    placed = (
        P(("det", "pix"), None, None),
        P(("det", "pix"), None, None, None),
        P(("det", "pix"), None, None),
        P(("det", "pix"), None),
        P(("det", "pix"), None),
    )
    return jax.shard_map(
        body,
        mesh=mesh,
        in_specs=placed,
        out_specs=(P(("det", "pix"), None), P(("det", "pix"), None)),
        check_vma=False,
    )
```

```python
import functools

import jax
import jax.numpy as jnp
from jax import lax
from jax.experimental import pallas as pl
from jax.experimental.pallas import tpu as pltpu
from jax.sharding import PartitionSpec as P

MESH = pl.DeviceIdType.MESH
PB_DEV = 64
NBASE_DEV = 128
HIGHEST = lax.Precision.HIGHEST


def _greet(peers, device_of):
    barrier = pltpu.get_barrier_semaphore()
    for peer in peers:
        pl.semaphore_signal(barrier, inc=1, device_id=device_of(peer), device_id_type=MESH)
    pl.semaphore_wait(barrier, len(peers))


def _det_sum_kernel(n, x_ref, o_ref, recv, send_sem, recv_sem, local_sem):
    me = lax.axis_index("det")
    pix = lax.axis_index("pix")
    device_of = lambda d: (d, pix)
    _greet([lax.rem(me + k, n) for k in range(1, n)], device_of)
    sends = []
    for k in range(1, n):
        peer = lax.rem(me + k, n)
        copy = pltpu.make_async_remote_copy(
            src_ref=x_ref, dst_ref=recv.at[me], send_sem=send_sem.at[k],
            recv_sem=recv_sem.at[me], device_id=device_of(peer), device_id_type=MESH)
        copy.start()
        sends.append(copy)
    local = pltpu.make_async_copy(x_ref, recv.at[me], local_sem)
    local.start()
    for copy in sends:
        copy.wait_send()
    for k in range(1, n):
        src = lax.rem(me + k, n)
        pltpu.make_async_remote_copy(
            src_ref=x_ref, dst_ref=recv.at[src], send_sem=send_sem.at[k],
            recv_sem=recv_sem.at[src], device_id=device_of(src), device_id_type=MESH).wait_recv()
    local.wait()
    acc = recv[0]
    for s in range(1, n):
        acc = acc + recv[s]
    o_ref[...] = acc


def det_sum(x, cid):
    n = lax.axis_size("det")
    return pl.pallas_call(
        functools.partial(_det_sum_kernel, n),
        out_shape=jax.ShapeDtypeStruct(x.shape, x.dtype),
        in_specs=[pl.BlockSpec(memory_space=pltpu.VMEM)],
        out_specs=pl.BlockSpec(memory_space=pltpu.VMEM),
        scratch_shapes=[
            pltpu.VMEM((n,) + x.shape, x.dtype),
            pltpu.SemaphoreType.DMA((n,)),
            pltpu.SemaphoreType.DMA((n,)),
            pltpu.SemaphoreType.DMA(()),
        ],
        compiler_params=pltpu.CompilerParams(collective_id=cid, has_side_effects=True),
    )(x)


def _pix_exchange_kernel(n, spread, *refs):
    count = len(spread)
    ins, outs = refs[:count], refs[count:2 * count]
    send_sem, recv_sem, local_sem = refs[2 * count:]
    me = lax.axis_index("pix")
    det = lax.axis_index("det")
    device_of = lambda j: (det, j)
    _greet([lax.rem(me + k, n) for k in range(1, n)], device_of)
    source = lambda a, j: ins[a].at[j] if spread[a] else ins[a]
    sends, locals_ = [], []
    for a in range(count):
        for k in range(1, n):
            peer = lax.rem(me + k, n)
            copy = pltpu.make_async_remote_copy(
                src_ref=source(a, peer), dst_ref=outs[a].at[me], send_sem=send_sem.at[a, k],
                recv_sem=recv_sem.at[a, me], device_id=device_of(peer), device_id_type=MESH)
            copy.start()
            sends.append(copy)
        local = pltpu.make_async_copy(source(a, me), outs[a].at[me], local_sem.at[a])
        local.start()
        locals_.append(local)
    for copy in sends:
        copy.wait_send()
    for a in range(count):
        for k in range(1, n):
            src = lax.rem(me + k, n)
            pltpu.make_async_remote_copy(
                src_ref=source(a, src), dst_ref=outs[a].at[src], send_sem=send_sem.at[a, k],
                recv_sem=recv_sem.at[a, src], device_id=device_of(src), device_id_type=MESH).wait_recv()
        locals_[a].wait()


def pix_exchange(arrays, spread, cid):
    n = lax.axis_size("pix")
    count = len(arrays)
    out_shape = [
        jax.ShapeDtypeStruct(x.shape if s else (n,) + x.shape, x.dtype) for x, s in zip(arrays, spread)
    ]
    return pl.pallas_call(
        functools.partial(_pix_exchange_kernel, n, tuple(spread)),
        out_shape=out_shape,
        in_specs=[pl.BlockSpec(memory_space=pltpu.VMEM)] * count,
        out_specs=[pl.BlockSpec(memory_space=pltpu.VMEM)] * count,
        scratch_shapes=[
            pltpu.SemaphoreType.DMA((count, n)),
            pltpu.SemaphoreType.DMA((count, n)),
            pltpu.SemaphoreType.DMA((count,)),
        ],
        compiler_params=pltpu.CompilerParams(collective_id=cid, has_side_effects=True),
    )(*arrays)


def _all_exchange_kernel(npix, n, spread, *refs):
    count = len(spread)
    ins, outs = refs[:count], refs[count:2 * count]
    send_sem, recv_sem, local_sem = refs[2 * count:]
    me = lax.axis_index("det") * npix + lax.axis_index("pix")
    device_of = lambda c: (lax.div(c, npix), lax.rem(c, npix))
    source = lambda a, c: ins[a].at[c] if spread[a] else ins[a]
    barrier = pltpu.get_barrier_semaphore()

    def greet(k, carry):
        peer = lax.rem(me + k, n)
        pl.semaphore_signal(barrier, inc=1, device_id=device_of(peer), device_id_type=MESH)
        return carry

    lax.fori_loop(1, n, greet, 0)
    pl.semaphore_wait(barrier, n - 1)

    def copy(a, k, c, slot):
        return pltpu.make_async_remote_copy(
            src_ref=source(a, c), dst_ref=outs[a].at[slot], send_sem=send_sem.at[a, k],
            recv_sem=recv_sem.at[a, slot], device_id=device_of(c), device_id_type=MESH)

    def send(k, carry):
        peer = lax.rem(me + k, n)
        for a in range(count):
            copy(a, k, peer, me).start()
        return carry

    lax.fori_loop(1, n, send, 0)
    locals_ = []
    for a in range(count):
        local = pltpu.make_async_copy(source(a, me), outs[a].at[me], local_sem.at[a])
        local.start()
        locals_.append(local)

    def finish(k, carry):
        peer = lax.rem(me + k, n)
        for a in range(count):
            copy(a, k, peer, me).wait_send()
            copy(a, k, peer, peer).wait_recv()
        return carry

    lax.fori_loop(1, n, finish, 0)
    for local in locals_:
        local.wait()


def all_exchange(arrays, spread, cid):
    npix = lax.axis_size("pix")
    n = lax.axis_size("det") * npix
    count = len(arrays)
    out_shape = [
        jax.ShapeDtypeStruct(x.shape if s else (n,) + x.shape, x.dtype) for x, s in zip(arrays, spread)
    ]
    return pl.pallas_call(
        functools.partial(_all_exchange_kernel, npix, n, tuple(spread)),
        out_shape=out_shape,
        in_specs=[pl.BlockSpec(memory_space=pltpu.VMEM)] * count,
        out_specs=[pl.BlockSpec(memory_space=pltpu.VMEM)] * count,
        scratch_shapes=[
            pltpu.SemaphoreType.DMA((count, n)),
            pltpu.SemaphoreType.DMA((count, n)),
            pltpu.SemaphoreType.DMA((count,)),
        ],
        compiler_params=pltpu.CompilerParams(collective_id=cid, has_side_effects=True),
    )(*arrays)


def _round_kernel(npix, n, k, scal, *refs):
    refs = list(refs)
    cells_in = refs.pop(0)
    hit_in = refs.pop(0) if k == 1 else None
    prev_in, local_in = (refs.pop(0), refs.pop(0)) if scal else (None, None)
    first_out, sky_all = refs.pop(0), refs.pop(0)
    scal_all = refs.pop(0) if scal else None
    recv, sky_cell = refs.pop(0), refs.pop(0)
    scal_cell = refs.pop(0) if scal else None
    send_sem, recv_sem, local_sem = refs
    me = lax.axis_index("det") * npix + lax.axis_index("pix")
    device_of = lambda c: (lax.div(c, npix), lax.rem(c, npix))
    barrier = pltpu.get_barrier_semaphore()

    def greet(j, carry):
        peer = lax.rem(me + j, n)
        pl.semaphore_signal(barrier, inc=1, device_id=device_of(peer), device_id_type=MESH)
        return carry

    lax.fori_loop(1, n, greet, 0, unroll=16)
    pl.semaphore_wait(barrier, n - 1)

    def exchange(items):
        def copy(item, j, c, slot):
            a, src, dst, spread = item
            return pltpu.make_async_remote_copy(
                src_ref=src.at[c] if spread else src, dst_ref=dst.at[slot],
                send_sem=send_sem.at[a, j], recv_sem=recv_sem.at[a, slot],
                device_id=device_of(c), device_id_type=MESH)

        def send(j, carry):
            for item in items:
                copy(item, j, lax.rem(me + j, n), me).start()
            return carry

        lax.fori_loop(1, n, send, 0, unroll=16)
        locals_ = []
        for a, src, dst, spread in items:
            local = pltpu.make_async_copy(src.at[me] if spread else src, dst.at[me], local_sem.at[a])
            local.start()
            locals_.append(local)

        def wait(j, carry):
            peer = lax.rem(me + j, n)
            for item in items:
                copy(item, j, peer, me).wait_send()
                copy(item, j, peer, peer).wait_recv()
            return carry

        lax.fori_loop(1, n, wait, 0, unroll=16)
        for local in locals_:
            local.wait()

    exchange([(0, cells_in, recv, True)])
    rows = sky_cell.shape[0]
    acc = lax.fori_loop(
        0, n, lambda c, t: t + recv[c].astype(jnp.float32), jnp.zeros((k * rows, 128), jnp.float32), unroll=32)
    if k == 2:
        hit_plus = acc[:rows] + 1.0
        binned = acc[rows:]
        first_out[...] = hit_plus
    else:
        hit_plus = hit_in[...]
        binned = acc
        first_out[...] = binned
    sky = (binned / hit_plus).astype(sky_cell.dtype)
    sky_cell[...] = sky
    if scal:
        sky_wide = sky.astype(jnp.float32)
        lane = lax.broadcasted_iota(jnp.int32, (1, 128), 1)
        products = (jnp.where(lane == 5, jnp.sum(prev_in[...] * sky_wide), 0.0)
                    + jnp.where(lane == 6, jnp.sum(binned * sky_wide), 0.0))
        scal_cell[...] = local_in[...] + products
    items = [(1, sky_cell, sky_all, False)]
    if scal:
        items.append((2, scal_cell, scal_all, False))
    exchange(items)


def fused_round(cells, k, hit_plus, prev, local, cid):
    npix = lax.axis_size("pix")
    n = lax.axis_size("det") * npix
    rows = cells.shape[1] // k
    scal = prev is not None
    args = [cells] + ([hit_plus] if k == 1 else []) + ([prev, local] if scal else [])
    out_shape = [jax.ShapeDtypeStruct((rows, 128), jnp.float32),
                 jax.ShapeDtypeStruct((n, rows, 128), jnp.bfloat16)]
    scratch = [pltpu.VMEM(cells.shape, cells.dtype), pltpu.VMEM((rows, 128), jnp.bfloat16)]
    if scal:
        out_shape.append(jax.ShapeDtypeStruct((n, 1, 128), jnp.float32))
        scratch.append(pltpu.VMEM((1, 128), jnp.float32))
    return pl.pallas_call(
        functools.partial(_round_kernel, npix, n, k, scal),
        out_shape=out_shape,
        in_specs=[pl.BlockSpec(memory_space=pltpu.VMEM)] * len(args),
        out_specs=[pl.BlockSpec(memory_space=pltpu.VMEM)] * len(out_shape),
        scratch_shapes=scratch + [
            pltpu.SemaphoreType.DMA((3, n)),
            pltpu.SemaphoreType.DMA((3, n)),
            pltpu.SemaphoreType.DMA((3,)),
        ],
        compiler_params=pltpu.CompilerParams(collective_id=cid, has_side_effects=True),
    )(*args)


def body(timestream, weights, block_owner, block_local, baseline_of):
    series_data = timestream[0]
    weight_rows = weights[0]
    owners = block_owner[0, :, 0]
    local_idx = block_local[0]
    segments_row = baseline_of[0]
    blocks, samples, pixels = weight_rows.shape
    pix_count = lax.axis_size("pix")
    devices = lax.axis_size("det") * pix_count
    sky_blocks_count = pix_count * PB_DEV
    cell = sky_blocks_count // devices
    cell_rows = cell * pixels // 128

    base_hot = (segments_row[:, None] == jnp.arange(NBASE_DEV)[None, :]).astype(jnp.float32)
    per_base = jnp.sum(base_hot, axis=0)
    weight_n = 1.0 + per_base
    block_pix = owners * PB_DEV + local_idx
    sky_hot = (block_pix[None, :] == jnp.arange(sky_blocks_count)[:, None]).astype(jnp.float32)
    sky_hot_t = (block_pix[:, None] == jnp.arange(sky_blocks_count)[None, :]).astype(jnp.bfloat16)

    unit_rows = jnp.ones((8, pixels), jnp.bfloat16)
    row_sums = jnp.einsum(
        "kp,bsp->kbs", unit_rows, weight_rows, preferred_element_type=jnp.float32
    )[0].astype(jnp.bfloat16)
    stacked = jnp.stack(
        [row_sums, series_data.astype(jnp.bfloat16), jnp.ones_like(row_sums)]
    )
    first_terms = jnp.einsum(
        "kbs,bsp->kbp", stacked, weight_rows, preferred_element_type=jnp.float32
    )
    col_sums = first_terms[2]
    series_block_sums = jnp.sum(series_data, axis=1)

    def to_cells(terms):
        dense = jnp.einsum("qb,kbp->kqp", sky_hot.astype(jnp.bfloat16), terms.astype(jnp.bfloat16),
                           preferred_element_type=jnp.float32)
        k = terms.shape[0]
        dense = dense.reshape(k, devices, cell_rows, 128).transpose(1, 0, 2, 3)
        return dense.reshape(devices, k * cell_rows, 128).astype(jnp.bfloat16)

    def to_blocks(sky_cells):
        return jnp.dot(sky_hot_t, sky_cells.reshape(sky_blocks_count, pixels),
                       preferred_element_type=jnp.float32)

    def scalar_rows(values):
        row = jnp.zeros((1, 128), jnp.float32)
        return row.at[0, : values.shape[0]].set(values)

    def cell_sum(arrived, k):
        total = jnp.sum(arrived.astype(jnp.float32), axis=0)
        return total.reshape(k, cell, pixels)

    hit_plus, back1 = fused_round(to_cells(first_terms[:2]), 2, None, None, None, 0)
    projected0 = jnp.sum(col_sums * to_blocks(back1), axis=1)
    r0 = jnp.dot(series_block_sums - projected0, base_hot, precision=HIGHEST) / samples

    def normal_action(amps, projected_blocks):
        collapsed = jnp.dot(projected_blocks, base_hot, precision=HIGHEST)
        return amps * weight_n - collapsed / samples

    def cells_of(amps):
        per_block = jnp.dot(base_hot, amps, precision=HIGHEST)
        return to_cells((per_block[:, None] * col_sums)[None])

    binned_r0, sky_r0 = fused_round(cells_of(r0), 1, hit_plus, None, None, 1)
    v1 = normal_action(r0, jnp.sum(col_sums * to_blocks(sky_r0), axis=1))
    left = jnp.stack([r0, r0, v1, r0 * weight_n, v1 * weight_n])
    right = jnp.stack([r0, v1, v1, v1, v1])
    partials = jnp.sum(left * right, axis=1)
    local = jnp.pad(partials, (0, 128 - partials.shape[0])).reshape(1, 128)
    _, sky_v1, carried = fused_round(cells_of(v1), 1, hit_plus, binned_r0, local, 2)
    total_row = jnp.sum(carried, axis=0)
    picks = (jnp.arange(128)[:, None] == (jnp.arange(7 * NBASE_DEV) // NBASE_DEV)[None, :])
    rows = jnp.dot(total_row, picks.astype(jnp.float32), precision=HIGHEST).reshape(7, NBASE_DEV)
    v2 = normal_action(v1, jnp.sum(col_sums * to_blocks(sky_v1), axis=1))

    rr0, r0v1, v1v1 = rows[0], rows[1], rows[2]
    r0v2 = rows[3] - rows[5] / samples
    v1v2 = rows[4] - rows[6] / samples
    alpha0 = rr0 / r0v1
    rr1 = rr0 - 2.0 * alpha0 * r0v1 + alpha0 * alpha0 * v1v1
    beta0 = rr1 / rr0
    grow = 1.0 + beta0
    d1_ad1 = grow * grow * r0v1 - grow * alpha0 * r0v2 - alpha0 * grow * v1v1 + alpha0 * alpha0 * v1v2
    alpha1 = rr1 / d1_ad1
    d1 = grow * r0 - alpha0 * v1
    ad1 = grow * v1 - alpha0 * v2
    offset_levels = alpha0 * r0 + alpha1 * d1
    leftover_error = r0 - alpha0 * v1 - alpha1 * ad1
    return (offset_levels[None], leftover_error[None])


def solution(mesh):
    placed = (
        P(("det", "pix"), None, None),
        P(("det", "pix"), None, None, None),
        P(("det", "pix"), None, None),
        P(("det", "pix"), None),
        P(("det", "pix"), None),
    )
    return jax.shard_map(
        body,
        mesh=mesh,
        in_specs=placed,
        out_specs=(P(("det", "pix"), None), P(("det", "pix"), None)),
        check_vma=False,
    )
```

```python
import functools

import jax
import jax.numpy as jnp
from jax import lax
from jax.experimental import pallas as pl
from jax.experimental.pallas import tpu as pltpu
from jax.sharding import PartitionSpec as P

MESH = pl.DeviceIdType.MESH
PB_DEV = 64
NBASE_DEV = 128
HIGHEST = lax.Precision.HIGHEST


def _greet(peers, device_of):
    barrier = pltpu.get_barrier_semaphore()
    for peer in peers:
        pl.semaphore_signal(barrier, inc=1, device_id=device_of(peer), device_id_type=MESH)
    pl.semaphore_wait(barrier, len(peers))


def _det_sum_kernel(n, x_ref, o_ref, recv, send_sem, recv_sem, local_sem):
    me = lax.axis_index("det")
    pix = lax.axis_index("pix")
    device_of = lambda d: (d, pix)
    _greet([lax.rem(me + k, n) for k in range(1, n)], device_of)
    sends = []
    for k in range(1, n):
        peer = lax.rem(me + k, n)
        copy = pltpu.make_async_remote_copy(
            src_ref=x_ref, dst_ref=recv.at[me], send_sem=send_sem.at[k],
            recv_sem=recv_sem.at[me], device_id=device_of(peer), device_id_type=MESH)
        copy.start()
        sends.append(copy)
    local = pltpu.make_async_copy(x_ref, recv.at[me], local_sem)
    local.start()
    for copy in sends:
        copy.wait_send()
    for k in range(1, n):
        src = lax.rem(me + k, n)
        pltpu.make_async_remote_copy(
            src_ref=x_ref, dst_ref=recv.at[src], send_sem=send_sem.at[k],
            recv_sem=recv_sem.at[src], device_id=device_of(src), device_id_type=MESH).wait_recv()
    local.wait()
    acc = recv[0]
    for s in range(1, n):
        acc = acc + recv[s]
    o_ref[...] = acc


def det_sum(x, cid):
    n = lax.axis_size("det")
    return pl.pallas_call(
        functools.partial(_det_sum_kernel, n),
        out_shape=jax.ShapeDtypeStruct(x.shape, x.dtype),
        in_specs=[pl.BlockSpec(memory_space=pltpu.VMEM)],
        out_specs=pl.BlockSpec(memory_space=pltpu.VMEM),
        scratch_shapes=[
            pltpu.VMEM((n,) + x.shape, x.dtype),
            pltpu.SemaphoreType.DMA((n,)),
            pltpu.SemaphoreType.DMA((n,)),
            pltpu.SemaphoreType.DMA(()),
        ],
        compiler_params=pltpu.CompilerParams(collective_id=cid, has_side_effects=True),
    )(x)


def _pix_exchange_kernel(n, spread, *refs):
    count = len(spread)
    ins, outs = refs[:count], refs[count:2 * count]
    send_sem, recv_sem, local_sem = refs[2 * count:]
    me = lax.axis_index("pix")
    det = lax.axis_index("det")
    device_of = lambda j: (det, j)
    _greet([lax.rem(me + k, n) for k in range(1, n)], device_of)
    source = lambda a, j: ins[a].at[j] if spread[a] else ins[a]
    sends, locals_ = [], []
    for a in range(count):
        for k in range(1, n):
            peer = lax.rem(me + k, n)
            copy = pltpu.make_async_remote_copy(
                src_ref=source(a, peer), dst_ref=outs[a].at[me], send_sem=send_sem.at[a, k],
                recv_sem=recv_sem.at[a, me], device_id=device_of(peer), device_id_type=MESH)
            copy.start()
            sends.append(copy)
        local = pltpu.make_async_copy(source(a, me), outs[a].at[me], local_sem.at[a])
        local.start()
        locals_.append(local)
    for copy in sends:
        copy.wait_send()
    for a in range(count):
        for k in range(1, n):
            src = lax.rem(me + k, n)
            pltpu.make_async_remote_copy(
                src_ref=source(a, src), dst_ref=outs[a].at[src], send_sem=send_sem.at[a, k],
                recv_sem=recv_sem.at[a, src], device_id=device_of(src), device_id_type=MESH).wait_recv()
        locals_[a].wait()


def pix_exchange(arrays, spread, cid):
    n = lax.axis_size("pix")
    count = len(arrays)
    out_shape = [
        jax.ShapeDtypeStruct(x.shape if s else (n,) + x.shape, x.dtype) for x, s in zip(arrays, spread)
    ]
    return pl.pallas_call(
        functools.partial(_pix_exchange_kernel, n, tuple(spread)),
        out_shape=out_shape,
        in_specs=[pl.BlockSpec(memory_space=pltpu.VMEM)] * count,
        out_specs=[pl.BlockSpec(memory_space=pltpu.VMEM)] * count,
        scratch_shapes=[
            pltpu.SemaphoreType.DMA((count, n)),
            pltpu.SemaphoreType.DMA((count, n)),
            pltpu.SemaphoreType.DMA((count,)),
        ],
        compiler_params=pltpu.CompilerParams(collective_id=cid, has_side_effects=True),
    )(*arrays)


def _all_exchange_kernel(npix, n, spread, *refs):
    count = len(spread)
    ins, outs = refs[:count], refs[count:2 * count]
    send_sem, recv_sem, local_sem = refs[2 * count:]
    me = lax.axis_index("det") * npix + lax.axis_index("pix")
    device_of = lambda c: (lax.div(c, npix), lax.rem(c, npix))
    source = lambda a, c: ins[a].at[c] if spread[a] else ins[a]
    barrier = pltpu.get_barrier_semaphore()

    def greet(k, carry):
        peer = lax.rem(me + k, n)
        pl.semaphore_signal(barrier, inc=1, device_id=device_of(peer), device_id_type=MESH)
        return carry

    lax.fori_loop(1, n, greet, 0)
    pl.semaphore_wait(barrier, n - 1)

    def copy(a, k, c, slot):
        return pltpu.make_async_remote_copy(
            src_ref=source(a, c), dst_ref=outs[a].at[slot], send_sem=send_sem.at[a, k],
            recv_sem=recv_sem.at[a, slot], device_id=device_of(c), device_id_type=MESH)

    def send(k, carry):
        peer = lax.rem(me + k, n)
        for a in range(count):
            copy(a, k, peer, me).start()
        return carry

    lax.fori_loop(1, n, send, 0)
    locals_ = []
    for a in range(count):
        local = pltpu.make_async_copy(source(a, me), outs[a].at[me], local_sem.at[a])
        local.start()
        locals_.append(local)

    def finish(k, carry):
        peer = lax.rem(me + k, n)
        for a in range(count):
            copy(a, k, peer, me).wait_send()
            copy(a, k, peer, peer).wait_recv()
        return carry

    lax.fori_loop(1, n, finish, 0)
    for local in locals_:
        local.wait()


def all_exchange(arrays, spread, cid):
    npix = lax.axis_size("pix")
    n = lax.axis_size("det") * npix
    count = len(arrays)
    out_shape = [
        jax.ShapeDtypeStruct(x.shape if s else (n,) + x.shape, x.dtype) for x, s in zip(arrays, spread)
    ]
    return pl.pallas_call(
        functools.partial(_all_exchange_kernel, npix, n, tuple(spread)),
        out_shape=out_shape,
        in_specs=[pl.BlockSpec(memory_space=pltpu.VMEM)] * count,
        out_specs=[pl.BlockSpec(memory_space=pltpu.VMEM)] * count,
        scratch_shapes=[
            pltpu.SemaphoreType.DMA((count, n)),
            pltpu.SemaphoreType.DMA((count, n)),
            pltpu.SemaphoreType.DMA((count,)),
        ],
        compiler_params=pltpu.CompilerParams(collective_id=cid, has_side_effects=True),
    )(*arrays)


def _round_kernel(npix, n, k, scal, *refs):
    refs = list(refs)
    cells_in = refs.pop(0)
    hit_in = refs.pop(0) if k == 1 else None
    prev_in, local_in = (refs.pop(0), refs.pop(0)) if scal else (None, None)
    first_out, sky_all = refs.pop(0), refs.pop(0)
    scal_all = refs.pop(0) if scal else None
    recv, sky_cell = refs.pop(0), refs.pop(0)
    scal_cell = refs.pop(0) if scal else None
    send_sem, recv_sem, local_sem = refs
    me = lax.axis_index("det") * npix + lax.axis_index("pix")
    device_of = lambda c: (lax.div(c, npix), lax.rem(c, npix))
    barrier = pltpu.get_barrier_semaphore()

    def greet(j, carry):
        peer = lax.rem(me + j, n)
        pl.semaphore_signal(barrier, inc=1, device_id=device_of(peer), device_id_type=MESH)
        return carry

    lax.fori_loop(1, n, greet, 0, unroll=8)
    pl.semaphore_wait(barrier, n - 1)

    def exchange(items, fold=None, init=0):
        def copy(item, j, c, slot):
            a, src, dst, spread = item
            return pltpu.make_async_remote_copy(
                src_ref=src.at[c] if spread else src, dst_ref=dst.at[slot],
                send_sem=send_sem.at[a, j], recv_sem=recv_sem.at[a, slot],
                device_id=device_of(c), device_id_type=MESH)

        def send(j, carry):
            for item in items:
                copy(item, j, lax.rem(me + j, n), me).start()
            return carry

        lax.fori_loop(1, n, send, 0, unroll=8)
        locals_ = []
        for a, src, dst, spread in items:
            local = pltpu.make_async_copy(src.at[me] if spread else src, dst.at[me], local_sem.at[a])
            local.start()
            locals_.append(local)

        def wait(j, carry):
            peer = lax.rem(me + j, n)
            for item in items:
                copy(item, j, peer, me).wait_send()
                copy(item, j, peer, peer).wait_recv()
            return carry if fold is None else fold(peer, carry)

        out = lax.fori_loop(1, n, wait, init, unroll=8)
        for local in locals_:
            local.wait()
        return out

    rows = sky_cell.shape[0]
    acc = exchange([(0, cells_in, recv, True)], lambda c, t: t + recv[c].astype(jnp.float32),
                   jnp.zeros((k * rows, 128), jnp.float32))
    acc = acc + recv[me].astype(jnp.float32)
    if k == 2:
        hit_plus = acc[:rows] + 1.0
        binned = acc[rows:]
        first_out[...] = hit_plus
    else:
        hit_plus = hit_in[...]
        binned = acc
        first_out[...] = binned
    sky = (binned / hit_plus).astype(sky_cell.dtype)
    sky_cell[...] = sky
    if scal:
        sky_wide = sky.astype(jnp.float32)
        lane = lax.broadcasted_iota(jnp.int32, (1, 128), 1)
        products = (jnp.where(lane == 5, jnp.sum(prev_in[...] * sky_wide), 0.0)
                    + jnp.where(lane == 6, jnp.sum(binned * sky_wide), 0.0))
        scal_cell[...] = local_in[...] + products
    items = [(1, sky_cell, sky_all, False)]
    if scal:
        items.append((2, scal_cell, scal_all, False))
    exchange(items)


def fused_round(cells, k, hit_plus, prev, local, cid):
    npix = lax.axis_size("pix")
    n = lax.axis_size("det") * npix
    rows = cells.shape[1] // k
    scal = prev is not None
    args = [cells] + ([hit_plus] if k == 1 else []) + ([prev, local] if scal else [])
    out_shape = [jax.ShapeDtypeStruct((rows, 128), jnp.float32),
                 jax.ShapeDtypeStruct((n, rows, 128), jnp.bfloat16)]
    scratch = [pltpu.VMEM(cells.shape, cells.dtype), pltpu.VMEM((rows, 128), jnp.bfloat16)]
    if scal:
        out_shape.append(jax.ShapeDtypeStruct((n, 1, 128), jnp.float32))
        scratch.append(pltpu.VMEM((1, 128), jnp.float32))
    return pl.pallas_call(
        functools.partial(_round_kernel, npix, n, k, scal),
        out_shape=out_shape,
        in_specs=[pl.BlockSpec(memory_space=pltpu.VMEM)] * len(args),
        out_specs=[pl.BlockSpec(memory_space=pltpu.VMEM)] * len(out_shape),
        scratch_shapes=scratch + [
            pltpu.SemaphoreType.DMA((3, n)),
            pltpu.SemaphoreType.DMA((3, n)),
            pltpu.SemaphoreType.DMA((3,)),
        ],
        compiler_params=pltpu.CompilerParams(collective_id=cid, has_side_effects=True),
    )(*args)


def body(timestream, weights, block_owner, block_local, baseline_of):
    series_data = timestream[0]
    weight_rows = weights[0]
    owners = block_owner[0, :, 0]
    local_idx = block_local[0]
    segments_row = baseline_of[0]
    blocks, samples, pixels = weight_rows.shape
    pix_count = lax.axis_size("pix")
    devices = lax.axis_size("det") * pix_count
    sky_blocks_count = pix_count * PB_DEV
    cell = sky_blocks_count // devices
    cell_rows = cell * pixels // 128

    base_hot = (segments_row[:, None] == jnp.arange(NBASE_DEV)[None, :]).astype(jnp.float32)
    per_base = jnp.sum(base_hot, axis=0)
    weight_n = 1.0 + per_base
    block_pix = owners * PB_DEV + local_idx
    sky_hot = (block_pix[None, :] == jnp.arange(sky_blocks_count)[:, None]).astype(jnp.float32)
    sky_hot_t = (block_pix[:, None] == jnp.arange(sky_blocks_count)[None, :]).astype(jnp.bfloat16)

    unit_rows = jnp.ones((8, pixels), jnp.bfloat16)
    row_sums = jnp.einsum(
        "kp,bsp->kbs", unit_rows, weight_rows, preferred_element_type=jnp.float32
    )[0].astype(jnp.bfloat16)
    stacked = jnp.stack(
        [row_sums, series_data.astype(jnp.bfloat16), jnp.ones_like(row_sums)]
    )
    first_terms = jnp.einsum(
        "kbs,bsp->kbp", stacked, weight_rows, preferred_element_type=jnp.float32
    )
    col_sums = first_terms[2]
    series_block_sums = jnp.sum(series_data, axis=1)

    def to_cells(terms):
        dense = jnp.einsum("qb,kbp->kqp", sky_hot.astype(jnp.bfloat16), terms.astype(jnp.bfloat16),
                           preferred_element_type=jnp.float32)
        k = terms.shape[0]
        dense = dense.reshape(k, devices, cell_rows, 128).transpose(1, 0, 2, 3)
        return dense.reshape(devices, k * cell_rows, 128).astype(jnp.bfloat16)

    def to_blocks(sky_cells):
        return jnp.dot(sky_hot_t, sky_cells.reshape(sky_blocks_count, pixels),
                       preferred_element_type=jnp.float32)

    def scalar_rows(values):
        row = jnp.zeros((1, 128), jnp.float32)
        return row.at[0, : values.shape[0]].set(values)

    def cell_sum(arrived, k):
        total = jnp.sum(arrived.astype(jnp.float32), axis=0)
        return total.reshape(k, cell, pixels)

    hit_plus, back1 = fused_round(to_cells(first_terms[:2]), 2, None, None, None, 0)
    projected0 = jnp.sum(col_sums * to_blocks(back1), axis=1)
    r0 = jnp.dot(series_block_sums - projected0, base_hot, precision=HIGHEST) / samples

    def normal_action(amps, projected_blocks):
        collapsed = jnp.dot(projected_blocks, base_hot, precision=HIGHEST)
        return amps * weight_n - collapsed / samples

    def cells_of(amps):
        per_block = jnp.dot(base_hot, amps, precision=HIGHEST)
        return to_cells((per_block[:, None] * col_sums)[None])

    binned_r0, sky_r0 = fused_round(cells_of(r0), 1, hit_plus, None, None, 1)
    v1 = normal_action(r0, jnp.sum(col_sums * to_blocks(sky_r0), axis=1))
    left = jnp.stack([r0, r0, v1, r0 * weight_n, v1 * weight_n])
    right = jnp.stack([r0, v1, v1, v1, v1])
    partials = jnp.sum(left * right, axis=1)
    local = jnp.pad(partials, (0, 128 - partials.shape[0])).reshape(1, 128)
    _, sky_v1, carried = fused_round(cells_of(v1), 1, hit_plus, binned_r0, local, 2)
    total_row = jnp.sum(carried, axis=0)
    picks = (jnp.arange(128)[:, None] == (jnp.arange(7 * NBASE_DEV) // NBASE_DEV)[None, :])
    rows = jnp.dot(total_row, picks.astype(jnp.float32), precision=HIGHEST).reshape(7, NBASE_DEV)
    v2 = normal_action(v1, jnp.sum(col_sums * to_blocks(sky_v1), axis=1))

    rr0, r0v1, v1v1 = rows[0], rows[1], rows[2]
    r0v2 = rows[3] - rows[5] / samples
    v1v2 = rows[4] - rows[6] / samples
    alpha0 = rr0 / r0v1
    rr1 = rr0 - 2.0 * alpha0 * r0v1 + alpha0 * alpha0 * v1v1
    beta0 = rr1 / rr0
    grow = 1.0 + beta0
    d1_ad1 = grow * grow * r0v1 - grow * alpha0 * r0v2 - alpha0 * grow * v1v1 + alpha0 * alpha0 * v1v2
    alpha1 = rr1 / d1_ad1
    d1 = grow * r0 - alpha0 * v1
    ad1 = grow * v1 - alpha0 * v2
    offset_levels = alpha0 * r0 + alpha1 * d1
    leftover_error = r0 - alpha0 * v1 - alpha1 * ad1
    return (offset_levels[None], leftover_error[None])


def solution(mesh):
    placed = (
        P(("det", "pix"), None, None),
        P(("det", "pix"), None, None, None),
        P(("det", "pix"), None, None),
        P(("det", "pix"), None),
        P(("det", "pix"), None),
    )
    return jax.shard_map(
        body,
        mesh=mesh,
        in_specs=placed,
        out_specs=(P(("det", "pix"), None), P(("det", "pix"), None)),
        check_vma=False,
    )
```
